32 devices in a mesh: expert: 8 (over z, y), tensor: 4 (over x, core).
Axes of the slice: x: 2, y: 2, z: 4, core: 2. Of those that a mesh axis runs over, the one named last changes fastest.
Arguments:
- hidden_in: bfloat16 [4096, 2048], P('expert'), may hold values from -6 to 6
- seq_lengths: int32 [8], P('expert'), may hold values from 256 to 512, as said below
- expert_ids: int32 [4096, 4], P('expert'), may hold values from 0 to 15, all different within a row; in each aligned block of 512 rows (0 to 511, 512 to 1023, ...) at most 192 rows name the same one
- attn_gain: bfloat16 [2048], replicated, may hold values from 0.5 to 1.5
- w_query: bfloat16 [2048, 2048], P(None, 'tensor'), may hold values from -0.125 to 0.125
- w_key: bfloat16 [2048, 2048], P(None, 'tensor'), may hold values from -0.125 to 0.125
- w_value: bfloat16 [2048, 2048], P(None, 'tensor'), may hold values from -0.125 to 0.125
- b_query: bfloat16 [16, 128], P('tensor'), may hold values from -3 to 3
- b_key: bfloat16 [16, 128], P('tensor'), may hold values from -3 to 3
- b_value: bfloat16 [16, 128], P('tensor'), may hold values from -0.1796875 to 0.1796875
- w_output: bfloat16 [2048, 2048], P('tensor'), may hold values from -1 to 1
- ffn_gain: bfloat16 [2048], replicated, may hold values from 0.5 to 1.5
- w_router: bfloat16 [2048, 16], replicated, may hold values from -0.0625 to 0.0625
- w_sigmoid: bfloat16 [2048], replicated, may hold values from -0.125 to 0.125
- shared_gate: bfloat16 [2048, 5632], P(None, 'tensor'), may hold values from -0.125 to 0.125
- shared_up: bfloat16 [2048, 5632], P(None, 'tensor'), may hold values from -0.125 to 0.125
- shared_down: bfloat16 [5632, 2048], P('tensor'), may hold values from -0.078125 to 0.078125
- expert_gate: bfloat16 [16, 2048, 1408], P('expert', None, 'tensor'), may hold values from -0.125 to 0.125
- expert_up: bfloat16 [16, 2048, 1408], P('expert', None, 'tensor'), may hold values from -0.125 to 0.125
- expert_down: bfloat16 [16, 1408, 2048], P('expert', 'tensor'), may hold values from -1.25 to 1.25
- out_grad: bfloat16 [4096, 2048], P('expert'), may hold values from -6 to 6
Outputs:
- layer_out: bfloat16 [4096, 2048], P('expert')
- grad_in: bfloat16 [4096, 2048], P('expert')
- grad_attn_gain: float32 [2048], P('expert')
- grad_w_query: float32 [2048, 2048], P('expert', 'tensor')
- grad_w_key: float32 [2048, 2048], P('expert', 'tensor')
- grad_w_value: float32 [2048, 2048], P('expert', 'tensor')
- grad_b_query: float32 [16, 128], P('tensor', 'expert')
- grad_b_key: float32 [16, 128], P('tensor', 'expert')
- grad_b_value: float32 [16, 128], P('tensor', 'expert')
- grad_w_output: float32 [2048, 2048], P('tensor', 'expert')
- grad_ffn_gain: float32 [2048], P('expert')
- grad_w_router: float32 [2048, 16], P('expert')
- grad_w_sigmoid: float32 [2048], P('expert')
- grad_shared_gate: float32 [2048, 5632], P('expert', 'tensor')
- grad_shared_up: float32 [2048, 5632], P('expert', 'tensor')
- grad_shared_down: float32 [5632, 2048], P('tensor', 'expert')
- grad_expert_gate: float32 [16, 2048, 1408], P('expert', None, 'tensor')
- grad_expert_up: float32 [16, 2048, 1408], P('expert', None, 'tensor')
- grad_expert_down: float32 [16, 1408, 2048], P('expert', 'tensor')
The draws below stay inside these ranges and needn't reach their ends.
Inputs may be any that keep to these rules, and one draw needn't show every extreme that they name: `expert_ids`: in each aligned block of 512 rows (the tokens of one sequence) no expert is named by more than 192 rows, and in some block an expert is named by exactly 192 rows; a row names 4 different experts. `seq_lengths`: some sequence has exactly 512 valid tokens.
All inputs are finite; a program needn't handle non-finite values.
Results may differ from the reference program's by a relative error of at most 0.025.
Values may be sent and summed in bfloat16 or wider, within the bound.
A program may use at most 384 MiB of HBM per device.

```python
import math
import jax
import jax.numpy as jnp
import numpy as np
from jax import lax

D = 2048
HEADS = 16
HEAD_DIM = 128
FS = 5632
FF_E = 1408
TOPK = 4
SEQ = 512
SEQS = 8
TOKENS = 4096
EXPERTS = 16
CAP = 192


def draw_seq_lengths(key, part):
    length_key, pick_key = jax.random.split(key)
    drawn = jax.random.randint(length_key, (SEQS,), SEQ // 2, SEQ + 1)
    longest = jax.random.randint(pick_key, (), 0, SEQS)
    return jnp.where(jnp.arange(SEQS) == longest, SEQ, drawn).astype(jnp.int32)


def block_levels(own_key, extent, cuts, least, top_value):
    def one(dim, blocks):
        steps = jax.random.uniform(jax.random.fold_in(jax.random.fold_in(own_key, 6), dim), (blocks,), jnp.float32, least / len(cuts), top_value / len(cuts))
        return jnp.repeat(jnp.exp(steps), extent[dim] // blocks).reshape((-1,) + (1,) * (len(extent) - dim - 1))

    factor_of = one(*cuts[0])
    for cut in cuts[1:]:
        factor_of = factor_of * one(*cut)
    return factor_of


def routed_block(stream_key, own, number, rows, number_of, top, bound, lean):
    sequence = jax.random.permutation(stream_key, number_of)
    packed, ordinary = shares(number_of, rows * top, bound, lean, True), shares(number_of, rows * top, bound, lean, False)
    places = jnp.arange(number_of)

    def named(lengths, rotation):
        used = int((lengths > 0).sum())
        fixed = max(1, used // 4)
        shifted = fixed + (places - fixed + rotation * (used - fixed)) % max(1, number_of - fixed)
        return jnp.zeros((number_of,), jnp.int32).at[sequence[jnp.where(places < fixed, places, shifted)]].set(jnp.asarray(lengths, jnp.int32))

    lengths = jnp.where(number % 4 == 0, named(packed, number // 4), named(ordinary, number - number // 4 - 1))
    mixed = jax.random.permutation(jax.random.fold_in(own, 3), number_of)
    source_of, sink = mixed[0:number_of // 2 * 2:2], mixed[1:number_of // 2 * 2:2]
    slack = jnp.minimum(lengths[source_of] - 1, bound - lengths[sink]) // 2
    slack = jnp.where((source_of == sequence[0]) | (sink == sequence[0]) | (lengths[sink] == 0), 0, jnp.maximum(slack, 0))
    shifted = jax.random.randint(jax.random.fold_in(own, 4), (number_of // 2,), 0, 1 << 20) % (slack + 1)
    lengths = lengths.at[source_of].add(-shifted).at[sink].add(shifted)
    items = jnp.searchsorted(jnp.cumsum(lengths), jnp.arange(rows * top), side="right").astype(jnp.int32)
    grid = items.reshape(top, rows).T
    grid = grid[jax.random.permutation(jax.random.fold_in(own, 1), rows)]
    rotation = jax.random.randint(jax.random.fold_in(own, 2), (rows, 1), 0, top)
    return jnp.take_along_axis(grid, (jnp.arange(top)[None, :] + rotation) % top, axis=1)


def shares(count, total, limit, lean, full):
    loads = [(1 << 20) // math.isqrt(standing ** lean) + 1 for standing in range(1, count + 1)]
    largest = limit if full else min(limit, max(-(-total // count), total * loads[0] // sum(loads)))
    least = 1 if total - largest >= count - 1 else 0
    counts, surplus = [largest] + [least] * (count - 1), total - largest - least * (count - 1)
    while surplus > 0:
        free = [i for i in range(1, count) if counts[i] < largest] or [i for i in range(1, count) if counts[i] < limit]
        mass, budget = sum([loads[i] for i in free]), surplus
        for i in free:
            extra = min(limit - counts[i], max(1, budget * loads[i] // mass), surplus)
            counts[i] = counts[i] + extra
            surplus = surplus - extra
    return np.array(counts)


def scatter_about(key, dims, width, limit, cuts=(), kind=jnp.bfloat16):
    values = jax.random.normal(key, dims, jnp.float32) * width
    if len(cuts) > 0:
        values = block_levels(key, dims, cuts, -0.22, 0.18) * values
    return jnp.clip(values, min=-limit, max=limit).astype(kind)


def setup_inputs(seed: int = 0) -> dict:
    splits = jax.random.split(jax.random.key(seed), 22)
    hidden_in = scatter_about(splits[0], (TOKENS, D), 1.0, 6.0, ((0, 8),))
    seq_lengths = draw_seq_lengths(jax.random.fold_in(splits[21], 71), 0)
    expert_ids_keys = jax.random.split(jax.random.fold_in(splits[2], 1), TOKENS // SEQ)
    expert_ids_turns = jax.random.permutation(jax.random.fold_in(splits[2], 3), TOKENS // SEQ)
    expert_ids = jax.vmap(lambda own, number: routed_block(jax.random.fold_in(splits[2], 2), own, number, SEQ, EXPERTS, TOPK, CAP, 1))(expert_ids_keys, expert_ids_turns).reshape((TOKENS, TOPK))
    attn_gain = jnp.clip(1.0 + 0.1 * jax.random.normal(splits[3], (D,), jnp.float32), 0.5, 1.5).astype(jnp.bfloat16)
    w_query = scatter_about(splits[4], (D, HEADS * HEAD_DIM), D ** -0.5, 0.125, ((1, 4),))
    w_key = scatter_about(splits[5], (D, HEADS * HEAD_DIM), D ** -0.5, 0.125, ((1, 4),))
    w_value = scatter_about(splits[6], (D, HEADS * HEAD_DIM), D ** -0.5, 0.125, ((1, 4),))
    b_query = scatter_about(splits[7], (HEADS, HEAD_DIM), 0.5, 3.0, ((0, 4),))
    b_key = scatter_about(splits[8], (HEADS, HEAD_DIM), 0.5, 3.0, ((0, 4),))
    b_value = scatter_about(splits[9], (HEADS, HEAD_DIM), 0.03, 0.1796875, ((0, 4),))
    w_output = scatter_about(splits[10], (HEADS * HEAD_DIM, D), (max(1, HEADS * HEAD_DIM // 64)) ** -0.5, 1.0, ((0, 4),))
    ffn_gain = jnp.clip(1.0 + 0.1 * jax.random.normal(splits[11], (D,), jnp.float32), 0.5, 1.5).astype(jnp.bfloat16)
    w_router = scatter_about(splits[12], (D, EXPERTS), (4 * D) ** -0.5, 0.0625)
    w_sigmoid = scatter_about(splits[13], (D,), D ** -0.5, 0.125)
    shared_gate = scatter_about(splits[14], (D, FS), D ** -0.5, 0.125, ((1, 4),))
    shared_up = scatter_about(splits[15], (D, FS), D ** -0.5, 0.125, ((1, 4),))
    shared_down = scatter_about(splits[16], (FS, D), FS ** -0.5, 0.078125, ((0, 4),))
    expert_gate = scatter_about(splits[17], (EXPERTS, D, FF_E), D ** -0.5, 0.125, ((0, 8), (2, 4)))
    expert_up = scatter_about(splits[18], (EXPERTS, D, FF_E), D ** -0.5, 0.125, ((0, 8), (2, 4)))
    expert_down = scatter_about(splits[19], (EXPERTS, FF_E, D), (max(1, FF_E * 4 // (EXPERTS * EXPERTS))) ** -0.5, 1.25, ((0, 8), (1, 4)))
    out_grad = scatter_about(splits[20], (TOKENS, D), 1.0, 6.0, ((0, 8),))
    return dict(hidden_in=hidden_in, seq_lengths=seq_lengths, expert_ids=expert_ids, attn_gain=attn_gain, w_query=w_query, w_key=w_key, w_value=w_value, b_query=b_query, b_key=b_key, b_value=b_value, w_output=w_output, ffn_gain=ffn_gain, w_router=w_router, w_sigmoid=w_sigmoid, shared_gate=shared_gate, shared_up=shared_up, shared_down=shared_down, expert_gate=expert_gate, expert_up=expert_up, expert_down=expert_down, out_grad=out_grad)


@jax.custom_vjp
def low(v):
    return lax.optimization_barrier(v.astype(jnp.bfloat16)).astype(jnp.float32)

@jax.custom_vjp
def low_back(v):
    return v

def low_keep(v):
    return (low(v), None)

def low_pass(kept, grad):
    return (grad,)

def back_keep(v):
    return (v, None)

def back_low(kept, grad):
    return (low(grad),)
low.defvjp(low_keep, low_pass)
low_back.defvjp(back_keep, back_low)
rope_base = 1000000.0
norm_eps = 1e-06

def precise(left, right):
    return jnp.dot(left, right, precision=lax.Precision.HIGHEST, preferred_element_type=jnp.float32)

def rms_norm(values, gain):
    return values * lax.rsqrt(lax.optimization_barrier(jnp.mean(values * values, axis=-1, keepdims=True)) + norm_eps) * gain

def rotary_tables(length, head_width):
    half_width = head_width // 2
    freq = jnp.exp(jnp.arange(half_width, dtype=jnp.float32) * (-2.0 * math.log(rope_base) / head_width))
    angle = jnp.arange(length, dtype=jnp.float32)[:, None] * freq[None, :]
    angle = jnp.concatenate([angle, angle], axis=1)
    return (jnp.cos(angle)[:, None, :], jnp.sin(angle)[:, None, :])

def rotate(values):
    half_width = values.shape[-1] // 2
    return jnp.concatenate([-values[..., half_width:], values[..., :half_width]], axis=-1)

def attend_one(inputs):
    query_rows, key_rows, value_rows, length = inputs
    scores = jnp.einsum('qhd,khd->hqk', query_rows, key_rows, precision=lax.Precision.HIGHEST) * (1.0 / math.sqrt(HEAD_DIM))
    scores = low_back(scores)
    query_pos = jnp.arange(SEQ)[:, None]
    key_pos = jnp.arange(SEQ)[None, :]
    allowed = (key_pos <= query_pos) & (key_pos < length)
    scores = jnp.where(allowed[None], scores, -1e+30)
    probs = low(jax.nn.softmax(scores, axis=-1))
    return jnp.einsum('hqk,khd->qhd', probs, value_rows, precision=lax.Precision.HIGHEST)

def expert_block(inputs):
    rows_in, gate_weight, up_weight, down_weight = inputs
    gate_pre = low_back(precise(rows_in, gate_weight))
    up_pre = low_back(precise(rows_in, up_weight))
    hidden = low(jax.nn.silu(gate_pre) * up_pre)
    return low_back(precise(hidden, down_weight))

def reference(hidden_in, seq_lengths, expert_ids, attn_gain, w_query, w_key, w_value, b_query, b_key, b_value, w_output, ffn_gain, w_router, w_sigmoid, shared_gate, shared_up, shared_down, expert_gate, expert_up, expert_down, out_grad):
    positions = jnp.arange(TOKENS, dtype=jnp.int32) % SEQ
    token_lengths = jnp.repeat(seq_lengths, SEQ)
    valid = (positions < token_lengths).astype(jnp.float32)
    onehot = (expert_ids[:, :, None] == jnp.arange(EXPERTS, dtype=jnp.int32)[None, None, :]).astype(jnp.float32)
    flat_ids = expert_ids.reshape(SEQS, SEQ * TOPK).astype(jnp.int32)
    hot = (flat_ids[:, :, None] == jnp.arange(EXPERTS, dtype=jnp.int32)[None, None, :]).astype(jnp.int32)
    rank = lax.optimization_barrier(jnp.sum((jnp.cumsum(hot, axis=1) - hot) * hot, axis=2)).astype(jnp.int32)
    group_index = jnp.arange(SEQS, dtype=jnp.int32)[:, None]
    slot = ((flat_ids * SEQS + group_index) * CAP + rank).reshape(-1).astype(jnp.int32)
    token_of = (jnp.arange(TOKENS * TOPK, dtype=jnp.int32) // TOPK).astype(jnp.int32)
    source = jnp.zeros((EXPERTS * SEQS * CAP,), jnp.int32).at[slot].set(token_of)
    filled = jnp.zeros((EXPERTS * SEQS * CAP,), jnp.float32).at[slot].set(1.0)

    def layer_forward(resid_in, gain_attn, query_weight, key_weight, value_weight, query_bias, key_bias, value_bias, output_weight, gain_ffn, router_weight, sigmoid_weight, shared_gate_w, shared_up_w, shared_down_w, expert_gate_w, expert_up_w, expert_down_w):
        normed_attn = low(rms_norm(resid_in, gain_attn))
        query_pre = low_back(precise(normed_attn, query_weight) + query_bias.reshape(-1))
        key_pre = low_back(precise(normed_attn, key_weight) + key_bias.reshape(-1))
        value_all = low(low_back(precise(normed_attn, value_weight) + value_bias.reshape(-1)))
        cosine, sine = rotary_tables(SEQ, HEAD_DIM)
        query_pre = query_pre.reshape(SEQS, SEQ, HEADS, HEAD_DIM)
        key_pre = key_pre.reshape(SEQS, SEQ, HEADS, HEAD_DIM)
        query_rot = low(query_pre * cosine + rotate(query_pre) * sine)
        key_rot = low(key_pre * cosine + rotate(key_pre) * sine)
        value_all = value_all.reshape(SEQS, SEQ, HEADS, HEAD_DIM)
        context = lax.map(jax.checkpoint(attend_one), (query_rot, key_rot, value_all, seq_lengths))
        context = low(low_back(context.reshape(TOKENS, HEADS * HEAD_DIM)))
        attn_out = low_back(precise(context, output_weight))
        resid = resid_in + attn_out
        normed_ffn = low(rms_norm(resid, gain_ffn))
        logits = low_back(precise(normed_ffn, router_weight))
        route_probs = jax.nn.softmax(logits, axis=-1)
        gates = lax.optimization_barrier(jnp.sum(route_probs[:, None, :] * onehot, axis=-1))
        sig = jax.nn.sigmoid(low_back(precise(normed_ffn, sigmoid_weight)))
        shared_a = low_back(precise(normed_ffn, shared_gate_w))
        shared_b = low_back(precise(normed_ffn, shared_up_w))
        shared_hidden = low(jax.nn.silu(shared_a) * shared_b)
        shared_out = low_back(precise(shared_hidden, shared_down_w))
        rows_in = (normed_ffn[source] * filled[:, None]).reshape(EXPERTS, SEQS * CAP, D)
        expert_out = lax.map(jax.checkpoint(expert_block), (rows_in, expert_gate_w, expert_up_w, expert_down_w))
        expert_rows = expert_out.reshape(EXPERTS * SEQS * CAP, D)[slot].reshape(TOKENS, TOPK, D)
        routed = lax.optimization_barrier(jnp.sum(gates[:, :, None] * expert_rows, axis=1))
        return resid + sig[:, None] * shared_out + routed
    params = (hidden_in.astype(jnp.float32), attn_gain.astype(jnp.float32), w_query.astype(jnp.float32), w_key.astype(jnp.float32), w_value.astype(jnp.float32), b_query.astype(jnp.float32), b_key.astype(jnp.float32), b_value.astype(jnp.float32), w_output.astype(jnp.float32), ffn_gain.astype(jnp.float32), w_router.astype(jnp.float32), w_sigmoid.astype(jnp.float32), shared_gate.astype(jnp.float32), shared_up.astype(jnp.float32), shared_down.astype(jnp.float32), expert_gate.astype(jnp.float32), expert_up.astype(jnp.float32), expert_down.astype(jnp.float32))
    primal, pullback = jax.vjp(layer_forward, *params)
    cotangent = out_grad.astype(jnp.float32) * valid[:, None]
    grads = pullback(cotangent)
    return (primal.astype(jnp.bfloat16), grads[0].astype(jnp.bfloat16), grads[1], grads[2], grads[3], grads[4], grads[5], grads[6], grads[7], grads[8], grads[9], grads[10], grads[11], grads[12], grads[13], grads[14], grads[15], grads[16], grads[17])
```

```python
import functools
import math

import jax
import jax.numpy as jnp
from jax import lax
from jax.experimental import pallas as pl
from jax.experimental.pallas import tpu as pltpu
from jax.sharding import PartitionSpec as P

rope_base = 1000000.0
norm_eps = 1e-06
f32 = jnp.float32
bf16 = jnp.bfloat16
whole = pl.BlockSpec(memory_space=pltpu.VMEM)
in_place = pl.BlockSpec(memory_space=pl.ANY)


def rms_scale(values):
    return lax.rsqrt(jnp.mean(values * values, axis=-1, keepdims=True) + norm_eps)


def matmul(left, right):
    return jnp.dot(left, right, preferred_element_type=f32)


def contract_rows(left, right):
    return lax.dot_general(left, right, (((0,), (0,)), ((), ())), preferred_element_type=f32)


def times_transposed(left, right):
    return lax.dot_general(left, right, (((1,), (1,)), ((), ())), preferred_element_type=f32)


def rotate(values):
    half_width = values.shape[-1] // 2
    return jnp.concatenate([-values[..., half_width:], values[..., :half_width]], axis=-1)


def flip_bit(value, bit):
    return value + bit * (1 - 2 * lax.rem(lax.div(value, bit), 2))


class Peers:
    def __init__(self, groups, lanes):
        self.groups, self.lanes = groups, lanes
        self.far = groups // 2
        self.chips = lanes // 2
        self.group = lax.axis_index("expert")
        self.lane = lax.axis_index("tensor")
        self.core = lax.rem(self.lane, 2)
        self.chip = lax.div(self.lane, 2)
        if groups == 8:
            z, y = lax.div(self.group, 2), lax.rem(self.group, 2)
            self.place = z + y * (7 - 2 * z)
        else:
            self.place = self.group

    def group_at(self, offset):
        place = lax.rem(self.place + (offset + self.groups), self.groups)
        if self.groups == 8:
            y = lax.div(place, 4)
            return 2 * (place + y * (7 - 2 * place)) + y
        return place

    def at(self, offset):
        return (self.group_at(offset), self.lane)

    def other_core(self):
        return (self.group, self.lane + 1 - 2 * self.core)

    def chip_bits(self):
        return [1 << i for i in range(self.chips.bit_length() - 1)]

    def other_chip(self, bit):
        return (self.group, 2 * flip_bit(self.chip, bit) + self.core)

    def offsets(self):
        return [0] + [s * k for k in range(1, self.far) for s in (1, -1)] + [self.far]

    def meet(self, peers):
        barrier = pltpu.get_barrier_semaphore()
        for peer in peers:
            pl.semaphore_signal(
                barrier, inc=1, device_id=peer, device_id_type=pl.DeviceIdType.MESH
            )
        pl.semaphore_wait(barrier, len(peers))


class Copies:
    def __init__(self, send_sems, recv_sems):
        self.send_sems, self.recv_sems = send_sems, recv_sems
        self.started = []
        self.count = 0

    def start(self, source, target, peer, arriving=None):
        index = self.count
        self.count += 1

        def copy(source, target):
            return pltpu.make_async_remote_copy(
                src_ref=source,
                dst_ref=target,
                send_sem=self.send_sems.at[index],
                recv_sem=self.recv_sems.at[index],
                device_id=peer,
                device_id_type=pl.DeviceIdType.MESH,
            )

        mine = copy(source, target)
        mine.start()
        self.started.append(mine)
        arriving = target if arriving is None else arriving
        return copy(arriving, arriving).wait_recv

    def finish(self):
        for copy in self.started:
            copy.wait_send()


def tiles(rows, size, step):
    def body(i, carry):
        step(pl.ds(pl.multiple_of(i * size, size), size))
        return carry

    lax.fori_loop(0, rows // size, body, 0)


def gather_kernel(
    groups, lanes, part, hidden, gain, grad, ids,
    resid, normed, tokens_all, grads_all, ids_all,
    total, from_core, from_chip, send_sems, recv_sems, local_sems,
):
    peers = Peers(groups, lanes)
    far, bits = peers.far, peers.chip_bits()
    seq, _ = grad.shape
    half = seq // 2
    piece = seq // lanes
    half_rows = pl.ds(pl.multiple_of(peers.core * half, half), half)
    other_rows = pl.ds(pl.multiple_of((1 - peers.core) * half, half), half)
    first = pl.multiple_of((peers.core * peers.chips + peers.chip) * piece, piece)
    me = peers.group
    others = [k for k in peers.offsets() if k != 0]
    peers.meet(
        [peers.at(k) for k in others]
        + [peers.other_core()]
        + [peers.other_chip(b) for b in bits]
    )
    copies = Copies(send_sems, recv_sems)

    own_grad = pltpu.make_async_copy(grad, grads_all.at[me], local_sems.at[0])
    own_grad.start()

    def hop(array, k, start, size, source=None):
        held = peers.group_at(k + 1 if k < 0 else k - 1)
        rows = pl.ds(pl.multiple_of(start, size), size)
        return copies.start(
            array.at[held, rows] if source is None else source,
            array.at[held, rows],
            peers.at(1) if k < 0 else peers.at(-1),
            array.at[peers.group_at(k), rows],
        )

    def chip_swap(array, k, bit):
        slot = peers.group_at(k)
        size = bit * piece
        start = (peers.core * peers.chips + lax.div(peers.chip, bit) * bit) * piece
        theirs = (peers.core * peers.chips + lax.div(flip_bit(peers.chip, bit), bit) * bit) * piece
        rows = pl.ds(pl.multiple_of(start, size), size)
        arriving = pl.ds(pl.multiple_of(theirs, size), size)
        return copies.start(
            array.at[slot, rows], array.at[slot, rows], peers.other_chip(bit),
            array.at[slot, arriving],
        )

    def core_swap(array, k, source=None):
        slot = peers.group_at(k)
        return copies.start(
            array.at[slot, half_rows] if source is None else source,
            array.at[slot, half_rows],
            peers.other_core(),
            array.at[slot, other_rows],
        )

    ids_all[me] = ids[...]
    late = [
        copies.start(ids, ids_all.at[me], peers.at(k), ids_all.at[peers.group_at(-k)])
        for k in others
    ]
    own_piece = grad.at[pl.ds(first, piece)]
    g_ring = {k: hop(grads_all, k, first, piece, own_piece) for k in (-1, 1)}
    got_core = copies.start(part.at[other_rows], from_core, peers.other_core())
    got_core()
    start_of_half = peers.core * half

    def add_core(rows):
        mine = pl.ds(pl.multiple_of(start_of_half + rows.start, rows.size), rows.size)
        both = part[mine, :].astype(f32) + from_core[rows, :].astype(f32)
        total[rows, :] = both.astype(bf16)

    tiles(half, 32, add_core)
    got_chip = copies.start(total, from_chip.at[0], peers.other_chip(bits[0]))
    chip_copy = copies.started.pop()
    for k in range(2, far):
        for s in (-1, 1):
            g_ring[s * (k - 1)]()
            g_ring[s * k] = hop(grads_all, s * k, first, piece)
        if k == 2:
            got_chip()
            for i, bit in enumerate(bits):

                def add_chip(rows, i=i):
                    both = total[rows, :].astype(f32) + from_chip[i, rows, :].astype(f32)
                    if i + 1 < len(bits):
                        total[rows, :] = both.astype(bf16)
                        return
                    both = hidden[rows, :].astype(f32) + both
                    resid[rows, :] = both
                    normed[rows, :] = (both * rms_scale(both) * gain[...]).astype(bf16)

                chip_copy.wait_send()
                tiles(half, 32, add_chip)
                if i + 1 < len(bits):
                    copies.start(total, from_chip.at[i + 1], peers.other_chip(bits[i + 1]))()
                    chip_copy = copies.started.pop()
            x_ring = {k2: hop(tokens_all, k2, start_of_half, half, normed) for k2 in (-1, 1)}
            late.append(core_swap(tokens_all, 0, normed))
            own_rows = pltpu.make_async_copy(
                normed, tokens_all.at[me, half_rows], local_sems.at[1]
            )
            own_rows.start()
    for s in (-1, 1):
        g_ring[s * (far - 1)]()
    ahead_half = hop(grads_all, -far, first, piece // 2)
    back_half = hop(grads_all, far, first + piece // 2, piece // 2)
    order = [s * k for k in range(1, far) for s in (-1, 1)] + [far]
    swaps = {k: chip_swap(grads_all, k, bits[0]) for k in order[:-1]}
    ahead_half()
    back_half()
    swaps[far] = chip_swap(grads_all, far, bits[0])

    def finish_grads(ks):
        for k in ks:
            swaps[k]()
            for bit in bits[1:]:
                chip_swap(grads_all, k, bit)()
            late.append(core_swap(grads_all, k))

    for k in range(2, far):
        finish_grads([-(k - 1), k - 1])
        for s in (-1, 1):
            x_ring[s * (k - 1)]()
            x_ring[s * k] = hop(tokens_all, s * k, start_of_half, half)
            late.append(core_swap(tokens_all, s * (k - 1)))
    for s in (-1, 1):
        x_ring[s * (far - 1)]()
    ahead_half = hop(tokens_all, -far, start_of_half, half // 2)
    back_half = hop(tokens_all, far, start_of_half + half // 2, half // 2)
    for s in (-1, 1):
        late.append(core_swap(tokens_all, s * (far - 1)))
    finish_grads([1 - far, far - 1, far])
    ahead_half()
    back_half()
    late.append(core_swap(tokens_all, far))
    for wait in late:
        wait()
    own_grad.wait()
    own_rows.wait()
    copies.finish()


def gather_tokens(groups, lanes, part, hidden_half, gain, grad, ids):
    seq, width = grad.shape
    half = seq // 2
    bits = (lanes // 2).bit_length() - 1
    copies = 2 * groups + 2 + bits + groups * (bits + 4)
    return pl.pallas_call(
        functools.partial(gather_kernel, groups, lanes),
        out_shape=(
            jax.ShapeDtypeStruct((half, width), f32),
            jax.ShapeDtypeStruct((half, width), bf16),
            jax.ShapeDtypeStruct((groups, seq, width), bf16),
            jax.ShapeDtypeStruct((groups, seq, width), bf16),
            jax.ShapeDtypeStruct((groups,) + ids.shape, jnp.int32),
        ),
        in_specs=[whole, whole, whole, in_place, whole],
        out_specs=(whole, whole, in_place, in_place, whole),
        scratch_shapes=[
            pltpu.VMEM((half, width), bf16),
            pltpu.VMEM((half, width), bf16),
            pltpu.VMEM((max(bits, 1), half, width), bf16),
            pltpu.SemaphoreType.DMA((copies,)),
            pltpu.SemaphoreType.DMA((copies,)),
            pltpu.SemaphoreType.DMA((2,)),
        ],
        compiler_params=pltpu.CompilerParams(
            collective_id=0, has_side_effects=True, vmem_limit_bytes=40 * 1024 * 1024
        ),
        name="gather_tokens",
    )(part, hidden_half, gain, grad, ids)


def reduce_kernel(
    groups, lanes, tokens, parts, small,
    total, small_total,
    kept, from_core, from_ring, from_chip, small_in, small_swap,
    send_sems, recv_sems, local_sems,
):
    peers = Peers(groups, lanes)
    far, bits = peers.far, peers.chip_bits()
    rows_all = kept.shape[1]
    half = rows_all // 2
    me = peers.group
    offsets = [far] + [s * k for k in range(far - 1, 0, -1) for s in (1, -1)] + [0]
    number = {k: i for i, k in enumerate(offsets)}
    others = [k for k in offsets if k != 0]
    peers.meet(
        [peers.at(k) for k in others]
        + [peers.other_core()]
        + [peers.other_chip(b) for b in bits]
    )
    copies = Copies(send_sems, recv_sems)
    if tokens:
        keep_rows = pl.ds(pl.multiple_of(peers.core * rows_all, rows_all), rows_all)
        give_rows = pl.ds(pl.multiple_of((1 - peers.core) * rows_all, rows_all), rows_all)
    loads, given = {}, {}
    for k in offsets:
        slot = peers.group_at(k)
        source = parts.at[slot, keep_rows] if tokens else parts.at[slot]
        loads[k] = pltpu.make_async_copy(source, kept.at[number[k]], local_sems.at[number[k]])
        loads[k].start()
        if tokens:
            given[k] = copies.start(
                parts.at[slot, give_rows], from_core.at[number[k]], peers.other_core()
            )
    small_got = [
        copies.start(small.at[peers.group_at(k)], small_in.at[number[k]], peers.at(k))
        for k in others
    ]

    def ready(k):
        loads[k].wait()
        if tokens:
            given[k]()

    def add(k, start, size, arrived=None):
        i = number[k]

        def step(rows):
            at = pl.ds(pl.multiple_of(start + rows.start, rows.size), rows.size)
            value = kept[i, at, :].astype(f32)
            if tokens:
                value = value + from_core[i, at, :].astype(f32)
            if arrived is not None:
                value = value + from_ring[arrived, at, :].astype(f32)
            kept[i, at, :] = value.astype(bf16)

        tiles(size, 32, step)

    def send(k, start, size, ahead, arriving):
        rows = pl.ds(start, size)
        return copies.start(
            kept.at[number[k], rows],
            from_ring.at[arriving, rows],
            peers.at(1) if ahead else peers.at(-1),
        )

    ready(far)
    add(far, 0, half)
    up = send(far, 0, half, True, 0)
    add(far, half, half)
    down = send(far, half, half, False, 0)
    up_at = down_at = 0
    for k in range(far - 1, 0, -1):
        ready(k)
        ready(-k)
        if k == far - 1:
            add(k, half, half)
            add(-k, 0, half)
            up()
            add(k, 0, half, up_at)
        else:
            up()
            add(k, 0, rows_all, up_at)
        up = send(k, 0, rows_all, True, 2 * (far - k) - 1)
        down()
        if k == far - 1:
            add(-k, half, half, down_at)
        else:
            add(-k, 0, rows_all, down_at)
        down = send(-k, 0, rows_all, False, 2 * (far - k))
        up_at, down_at = 2 * (far - k) - 1, 2 * (far - k)
    ready(0)

    for wait in small_got:
        wait()
    small_sum = small[me]
    for k in others:
        small_sum = small_sum + small_in[number[k]]
    small_total[...] = small_sum
    for i, peer in enumerate([peers.other_core()] + [peers.other_chip(b) for b in bits]):
        small_swap[2 * i] = small_total[...]
        copies.start(small_swap.at[2 * i], small_swap.at[2 * i + 1], peer)()
        small_total[...] = small_swap[2 * i] + small_swap[2 * i + 1]

    up()
    down()
    home = number[0]

    def last(rows):
        value = kept[home, rows, :].astype(f32)
        if tokens:
            value = value + from_core[home, rows, :].astype(f32)
        value = value + from_ring[up_at, rows, :].astype(f32)
        value = value + from_ring[down_at, rows, :].astype(f32)
        if tokens:
            kept[home, rows, :] = value.astype(bf16)
        else:
            total[rows, :] = value

    tiles(rows_all, 32, last)
    if tokens:
        for i, bit in enumerate(bits):
            wait = copies.start(kept.at[home], from_chip.at[i], peers.other_chip(bit))
            wait()
            copies.started.pop().wait_send()

            def join(rows, i=i):
                value = kept[home, rows, :].astype(f32) + from_chip[i, rows, :].astype(f32)
                if i + 1 < len(bits):
                    kept[home, rows, :] = value.astype(bf16)
                else:
                    total[rows, :] = value

            tiles(rows_all, 32, join)
    copies.finish()


def reduce_parts(groups, lanes, parts, small, tokens, collective_id):
    rows = parts.shape[1] // 2 if tokens else parts.shape[1]
    width = parts.shape[2]
    bits = (lanes // 2).bit_length() - 1
    far = groups // 2
    copies = (groups if tokens else 0) + (groups - 1) + 2 * far + (1 + bits) + bits
    shape = (rows, width)
    return pl.pallas_call(
        functools.partial(reduce_kernel, groups, lanes, tokens),
        out_shape=(
            jax.ShapeDtypeStruct(shape, f32),
            jax.ShapeDtypeStruct(small.shape[1:], f32),
        ),
        in_specs=[in_place, whole],
        out_specs=(whole, whole),
        scratch_shapes=[
            pltpu.VMEM((groups,) + shape, bf16),
            pltpu.VMEM(((groups if tokens else 1),) + shape, bf16),
            pltpu.VMEM((2 * far - 1,) + shape, bf16),
            pltpu.VMEM(((max(bits, 1) if tokens else 1),) + shape, bf16),
            pltpu.VMEM(small.shape, f32),
            pltpu.VMEM((2 * (1 + bits),) + small.shape[1:], f32),
            pltpu.SemaphoreType.DMA((copies,)),
            pltpu.SemaphoreType.DMA((copies,)),
            pltpu.SemaphoreType.DMA((groups,)),
        ],
        compiler_params=pltpu.CompilerParams(
            collective_id=collective_id,
            has_side_effects=True,
            vmem_limit_bytes=58 * 1024 * 1024,
        ),
        name="reduce_tokens" if tokens else "reduce_weights",
    )(parts, small)


def attend_forward(query, key, value, allowed, score_scale):
    scores = jnp.einsum("qhd,khd->hqk", query, key, preferred_element_type=f32) * score_scale
    scores = jnp.where(allowed[None], scores, -1e30)
    highest = jnp.max(scores, axis=-1, keepdims=True)
    log_total = highest + jnp.log(jnp.sum(jnp.exp(scores - highest), axis=-1, keepdims=True))
    probs = jnp.exp(scores - log_total)
    contexts = jnp.einsum("hqk,khd->qhd", probs.astype(bf16), value, preferred_element_type=f32)
    return contexts.astype(bf16), log_total


def attend_backward(query, key, value, d_context, log_total, allowed, score_scale):
    scores = jnp.einsum("qhd,khd->hqk", query, key, preferred_element_type=f32) * score_scale
    probs = jnp.exp(jnp.where(allowed[None], scores, -1e30) - log_total)
    d_probs = jnp.einsum("qhd,khd->hqk", d_context, value, preferred_element_type=f32)
    row_dot = jnp.sum(probs * d_probs, axis=-1, keepdims=True)
    d_scores = (probs * (d_probs - row_dot)).astype(bf16)
    d_query = jnp.einsum("hqk,khd->qhd", d_scores, key, preferred_element_type=f32) * score_scale
    d_key = jnp.einsum("hqk,qhd->khd", d_scores, query, preferred_element_type=f32) * score_scale
    d_value = jnp.einsum("hqk,qhd->khd", probs.astype(bf16), d_context, preferred_element_type=f32)
    return d_query, d_key, d_value


def norm_backward(values, scale, gain, d_normed):
    inner = d_normed * gain
    mean = jnp.mean(inner * values, axis=-1, keepdims=True)
    return scale * inner - values * (scale * scale * scale) * mean


def gated_backward(a, b, d_hidden):
    sigma = jax.nn.sigmoid(a)
    d_a = (d_hidden * b * sigma * (1.0 + a * (1.0 - sigma))).astype(bf16)
    d_b = (d_hidden * a * sigma).astype(bf16)
    return d_a, d_b


class Experts:
    def __init__(self, weights, router, w_sigmoid, first_expert, capacity):
        (self.gate, self.up, self.down, self.s_gate, self.s_up, self.s_down) = weights
        self.router = router
        self.w_sigmoid = w_sigmoid
        self.first = first_expert
        self.capacity = capacity

    def run(self, tokens, grads, ids):
        held = self.gate.shape[0]
        m, s, d = tokens.shape
        local = jnp.arange(held, dtype=jnp.int32) + self.first
        named = jnp.any(ids[:, None, :, :] == local[None, :, None, None], axis=2)
        earlier = (jnp.arange(s)[:, None] < jnp.arange(s)[None, :]).astype(bf16)
        rank = jnp.einsum(
            "met,tu->meu", named.astype(bf16), earlier, preferred_element_type=f32
        ).astype(jnp.int32)
        place = jnp.where(named, rank, -1)
        pick = (
            place[:, :, None, :] == jnp.arange(self.capacity, dtype=jnp.int32)[None, None, :, None]
        )
        pick_flat = pick.astype(bf16).reshape(m, held * self.capacity, s)
        shape4 = (m, held, self.capacity, d)
        rows = jnp.einsum("mrt,mtd->mrd", pick_flat, tokens, preferred_element_type=f32)
        rows = rows.astype(bf16).reshape(shape4)
        row_grads = jnp.einsum("mrt,mtd->mrd", pick_flat, grads, preferred_element_type=f32)
        row_grads = row_grads.astype(bf16).reshape(shape4)
        logits = jnp.einsum("mtd,de->mte", tokens, self.router, preferred_element_type=f32)
        probs = jax.nn.softmax(logits, axis=-1)
        mine = lax.dynamic_slice_in_dim(probs, self.first, held, 2)
        gate_rows = jnp.sum(
            jnp.where(pick, jnp.swapaxes(mine, 1, 2)[:, :, None, :], 0.0), axis=-1, keepdims=True
        )
        sig = jax.nn.sigmoid(
            jnp.einsum("mtd,d->mt", tokens, self.w_sigmoid, preferred_element_type=f32)
        )[:, :, None]
        a = jnp.einsum("mecd,edf->mecf", rows, self.gate, preferred_element_type=f32)
        b = jnp.einsum("mecd,edf->mecf", rows, self.up, preferred_element_type=f32)
        u = jnp.einsum("mecd,efd->mecf", row_grads, self.down, preferred_element_type=f32)
        hidden = (jax.nn.silu(a) * b).astype(bf16).astype(f32)
        d_gate_rows = jnp.sum(hidden * u, axis=-1, keepdims=True)
        gated_hidden = (hidden * gate_rows).astype(bf16)
        d_a, d_b = gated_backward(a, b, u * gate_rows)
        out_rows = jnp.einsum(
            "mecf,efd->mecd", gated_hidden, self.down, preferred_element_type=f32
        ).astype(bf16)
        in_rows = (
            jnp.einsum("mecf,edf->mecd", d_a, self.gate, preferred_element_type=f32)
            + jnp.einsum("mecf,edf->mecd", d_b, self.up, preferred_element_type=f32)
        ).astype(bf16)
        s_a = jnp.einsum("mtd,df->mtf", tokens, self.s_gate, preferred_element_type=f32)
        s_b = jnp.einsum("mtd,df->mtf", tokens, self.s_up, preferred_element_type=f32)
        s_u = jnp.einsum("mtd,fd->mtf", grads, self.s_down, preferred_element_type=f32)
        s_hidden = (jax.nn.silu(s_a) * s_b).astype(bf16).astype(f32)
        d_sig = jnp.sum(s_hidden * s_u, axis=-1)
        s_gated = (s_hidden * sig).astype(bf16)
        s_d_a, s_d_b = gated_backward(s_a, s_b, s_u * sig)
        flat = (m, held * self.capacity, d)
        outs = jnp.einsum(
            "mrt,mrd->mtd", pick_flat, out_rows.reshape(flat), preferred_element_type=f32
        ) + jnp.einsum("mtf,fd->mtd", s_gated, self.s_down, preferred_element_type=f32)
        d_in = (
            jnp.einsum("mrt,mrd->mtd", pick_flat, in_rows.reshape(flat), preferred_element_type=f32)
            + jnp.einsum("mtf,df->mtd", s_d_a, self.s_gate, preferred_element_type=f32)
            + jnp.einsum("mtf,df->mtd", s_d_b, self.s_up, preferred_element_type=f32)
        )
        d_gates = jnp.sum(jnp.where(pick, d_gate_rows, 0.0), axis=2)
        saved = (rows, row_grads, gated_hidden, d_a, d_b, tokens, grads, s_gated, s_d_a, s_d_b)
        return outs.astype(bf16), d_in.astype(bf16), d_gates, d_sig, saved

    def weight_grads(self, saved):
        rows, row_grads, gated_hidden, d_a, d_b, tokens, grads, s_gated, s_d_a, s_d_b = saved
        return (
            jnp.einsum("mecd,mecf->edf", rows, d_a, preferred_element_type=f32),
            jnp.einsum("mecd,mecf->edf", rows, d_b, preferred_element_type=f32),
            jnp.einsum("mecf,mecd->efd", gated_hidden, row_grads, preferred_element_type=f32),
            jnp.einsum("mtd,mtf->df", tokens, s_d_a, preferred_element_type=f32),
            jnp.einsum("mtd,mtf->df", tokens, s_d_b, preferred_element_type=f32),
            jnp.einsum("mtf,mtd->fd", s_gated, grads, preferred_element_type=f32),
        )


def on_device(
    hidden_in,
    seq_lengths,
    expert_ids,
    attn_gain,
    w_query,
    w_key,
    w_value,
    b_query,
    b_key,
    b_value,
    w_output,
    ffn_gain,
    w_router,
    w_sigmoid,
    shared_gate,
    shared_up,
    shared_down,
    expert_gate,
    expert_up,
    expert_down,
    out_grad,
):
    seq, width = hidden_in.shape
    heads, head_width = b_query.shape
    head_all = heads * head_width
    top_count = expert_ids.shape[1]
    experts_all = w_router.shape[1]
    held = expert_gate.shape[0]
    groups = lax.axis_size("expert")
    lane_count = lax.axis_size("tensor")
    group = lax.axis_index("expert")
    lane = lax.axis_index("tensor")
    capacity = 3 * seq * top_count // (2 * experts_all)
    score_scale = 1.0 / math.sqrt(head_width)
    length = seq_lengths[0]
    half = seq // 2
    features = width // groups
    half_start = (lane % 2) * half

    def half_of(array):
        return lax.dynamic_slice_in_dim(array, half_start, half, 0)

    def swap(values, bit):
        return lax.ppermute(values, "tensor", [(i, i ^ bit) for i in range(lane_count)])

    def sum_lanes(values):
        other = lax.dynamic_slice_in_dim(values, half - half_start, half, 0)
        total = (half_of(values).astype(f32) + swap(other, 1).astype(f32)).astype(bf16)
        for bit in range(1, (lane_count // 2).bit_length()):
            total32 = total.astype(f32) + swap(total, 1 << bit).astype(f32)
            total = total32.astype(bf16)
        return total32

    def both_halves(mine):
        other = swap(mine, 1)
        lower = jnp.where(half_start == 0, mine, other)
        upper = jnp.where(half_start == 0, other, mine)
        return jnp.concatenate([lower, upper], axis=0)

    hidden = hidden_in.astype(f32)
    position = jnp.arange(seq, dtype=jnp.int32)
    grad_low = jnp.where((position < length)[:, None], out_grad, jnp.zeros_like(out_grad))

    gain_attn = attn_gain.astype(f32)
    attn_scale = rms_scale(hidden)
    normed_attn = (hidden * attn_scale * gain_attn).astype(bf16)
    freq = jnp.exp(
        jnp.arange(head_width // 2, dtype=f32) * (-2.0 * math.log(rope_base) / head_width)
    )
    angle = position.astype(f32)[:, None] * freq[None, :]
    angle = jnp.concatenate([angle, angle], axis=1)
    cosine, sine = jnp.cos(angle)[:, None, :], jnp.sin(angle)[:, None, :]
    by_head = (seq, heads, head_width)
    query_pre = (matmul(normed_attn, w_query) + b_query.reshape(-1).astype(f32)).reshape(by_head)
    key_pre = (matmul(normed_attn, w_key) + b_key.reshape(-1).astype(f32)).reshape(by_head)
    value_pre = matmul(normed_attn, w_value) + b_value.reshape(-1).astype(f32)
    query = (query_pre * cosine + rotate(query_pre) * sine).astype(bf16)
    key = (key_pre * cosine + rotate(key_pre) * sine).astype(bf16)
    value = value_pre.astype(bf16).reshape(by_head)
    allowed = (position[None, :] <= position[:, None]) & (position[None, :] < length)
    context, log_total = attend_forward(query, key, value, allowed, score_scale)
    context_flat = context.reshape(seq, head_all)
    gain_ffn = ffn_gain.astype(f32)
    ids = jnp.pad(expert_ids.T, ((0, -top_count % 8), (0, 0)), constant_values=-1)
    resid, normed, tokens_all, grads_all, ids_all = gather_tokens(
        groups,
        lane_count,
        matmul(context_flat, w_output).astype(bf16),
        half_of(hidden_in),
        gain_ffn[None, :],
        grad_low,
        ids,
    )

    ffn_scale = rms_scale(resid)
    logits = matmul(normed, w_router)
    route_probs = jax.nn.softmax(logits, axis=-1)
    sig = jax.nn.sigmoid(jnp.dot(normed, w_sigmoid, preferred_element_type=f32))

    units = shared_gate.shape[1] // groups
    experts = Experts(
        (
            expert_gate,
            expert_up,
            expert_down,
            lax.dynamic_slice_in_dim(shared_gate, group * units, units, 1),
            lax.dynamic_slice_in_dim(shared_up, group * units, units, 1),
            lax.dynamic_slice_in_dim(shared_down, group * units, units, 0),
        ),
        w_router,
        w_sigmoid,
        group * held,
        capacity,
    )
    outs, d_in, d_gates, d_sig, saved = experts.run(tokens_all, grads_all, ids_all[:, :top_count])
    g_gate, g_up, g_down, g_s_gate, g_s_up, g_s_down = experts.weight_grads(saved)

    spread = (
        (group * held + jnp.arange(held))[:, None] == jnp.arange(experts_all)[None, :]
    ).astype(f32)
    small = jnp.concatenate(
        [
            jnp.sum(d_gates[:, :, None, :] * spread[None, :, :, None], axis=1),
            d_sig[:, None, :],
            jnp.zeros((groups, -(experts_all + 1) % 8, seq), f32),
        ],
        axis=1,
    )
    d_in_sum, small = reduce_parts(groups, lane_count, d_in, small, True, 1)
    small = half_of(small.T)
    d_probs_route, sig_grad = small[:, :experts_all], small[:, experts_all]
    d_logits = (
        route_probs
        * (d_probs_route - jnp.sum(route_probs * d_probs_route, axis=-1, keepdims=True))
    ).astype(bf16)
    d_sig_logit = (sig_grad * sig * (1.0 - sig)).astype(bf16)
    d_from_gates = (
        times_transposed(d_logits, w_router)
        + d_sig_logit.astype(f32)[:, None] * w_sigmoid.astype(f32)[None, :]
    )
    d_normed = d_in_sum + d_from_gates
    d_resid = half_of(grad_low).astype(f32) + norm_backward(resid, ffn_scale, gain_ffn, d_normed)
    d_attn = both_halves(d_resid.astype(bf16))

    d_context = times_transposed(d_attn, w_output).astype(bf16).reshape(by_head)
    d_query_rot, d_key_rot, d_value_all = attend_backward(
        query, key, value, d_context, log_total, allowed, score_scale
    )

    def unrope(values):
        return (values * cosine - rotate(values) * sine).astype(bf16).reshape(seq, head_all)

    d_query, d_key = unrope(d_query_rot), unrope(d_key_rot)
    d_value = d_value_all.astype(bf16).reshape(seq, head_all)
    d_normed_attn = (
        times_transposed(d_query, w_query)
        + times_transposed(d_key, w_key)
        + times_transposed(d_value, w_value)
    )
    grads = [contract_rows(normed_attn, d) for d in (d_query, d_key, d_value)]
    grads.append(contract_rows(d_attn, context_flat))
    grads = jnp.concatenate([g.astype(bf16) for g in grads], axis=1)

    rows = half // (lane_count // 2)
    start = (lane // 2) * rows
    mine = [
        lax.dynamic_slice_in_dim(a, start, rows, 0)
        for a in (d_normed * resid * ffn_scale, normed, d_logits, d_sig_logit[:, None])
    ]
    router_part = contract_rows(jnp.concatenate([mine[2], mine[3]], axis=1), mine[1])
    bias_part = jnp.concatenate(
        [jnp.sum(d.astype(f32), axis=0) for d in (d_query, d_key, d_value)]
    ).reshape(-1, features)
    to_groups = jnp.concatenate(
        [
            router_part,
            jnp.sum(mine[0], axis=0)[None],
            jnp.sum(d_normed_attn * hidden * attn_scale, axis=0)[None],
        ],
        axis=0,
    )
    to_groups = jnp.swapaxes(to_groups.reshape(-1, groups, features), 0, 1)
    lane_slots = (jnp.arange(lane_count) == lane).astype(f32)[:, None, None] * bias_part[None]
    lane_slots = lane_slots.reshape(-1, features)
    small = jnp.concatenate(
        [to_groups, jnp.broadcast_to(lane_slots[None], (groups,) + lane_slots.shape)], axis=1
    )
    small = jnp.pad(small, ((0, 0), (0, -small.shape[1] % 8), (0, 0)))
    grads, small = reduce_parts(
        groups, lane_count, grads.reshape(groups, features, -1), small, False, 2
    )
    biases = lax.dynamic_slice_in_dim(
        small, experts_all + 3 + lane * bias_part.shape[0], bias_part.shape[0], 0
    ).reshape(3, heads, head_width)
    biases = lax.dynamic_slice_in_dim(
        biases, group * (head_width // groups), head_width // groups, 2
    )

    outs = lax.psum_scatter(
        outs.reshape(groups * seq, width), ("expert", "tensor"), scatter_dimension=0, tiled=True
    )
    outs = lax.all_gather(outs, "tensor", axis=0, tiled=True)
    layer_out = both_halves((resid + half_of(outs).astype(f32)).astype(bf16))
    d_normed_in = sum_lanes(d_normed_attn.astype(bf16))
    grad_in = d_resid + norm_backward(half_of(hidden), half_of(attn_scale), gain_attn, d_normed_in)
    grad_in = both_halves(grad_in.astype(bf16))

    wide = jnp.concatenate([g_s_gate, g_s_up], axis=1).astype(bf16)
    wide = lax.all_to_all(wide, "expert", split_axis=0, concat_axis=1, tiled=True).astype(f32)
    wide = wide.reshape(features, groups, 2, units)
    grad_shared_gate = wide[:, :, 0].reshape(features, groups * units)
    grad_shared_up = wide[:, :, 1].reshape(features, groups * units)
    grad_shared_down = lax.all_to_all(
        g_s_down.astype(bf16), "expert", split_axis=1, concat_axis=0, tiled=True
    ).astype(f32)
    return (
        layer_out,
        grad_in,
        small[experts_all + 2],
        grads[:, :head_all],
        grads[:, head_all : 2 * head_all],
        grads[:, 2 * head_all : 3 * head_all],
        biases[0],
        biases[1],
        biases[2],
        grads[:, 3 * head_all :].T,
        small[experts_all + 1],
        small[:experts_all].T,
        small[experts_all],
        grad_shared_gate,
        grad_shared_up,
        grad_shared_down,
        g_gate,
        g_up,
        g_down,
    )


def solution(mesh):
    placed = (
        P("expert", None),
        P("expert"),
        P("expert", None),
        P(),
        P(None, "tensor"),
        P(None, "tensor"),
        P(None, "tensor"),
        P("tensor", None),
        P("tensor", None),
        P("tensor", None),
        P("tensor", None),
        P(),
        P(),
        P(),
        P(None, "tensor"),
        P(None, "tensor"),
        P("tensor", None),
        P("expert", None, "tensor"),
        P("expert", None, "tensor"),
        P("expert", "tensor", None),
        P("expert", None),
    )
    return jax.shard_map(
        on_device,
        mesh=mesh,
        in_specs=placed,
        out_specs=(
            P("expert", None),
            P("expert", None),
            P("expert"),
            P("expert", "tensor"),
            P("expert", "tensor"),
            P("expert", "tensor"),
            P("tensor", "expert"),
            P("tensor", "expert"),
            P("tensor", "expert"),
            P("tensor", "expert"),
            P("expert"),
            P("expert", None),
            P("expert"),
            P("expert", "tensor"),
            P("expert", "tensor"),
            P("tensor", "expert"),
            P("expert", None, "tensor"),
            P("expert", None, "tensor"),
            P("expert", "tensor", None),
        ),
        check_vma=False,
    )
```

```python
import functools
import math

import jax
import jax.numpy as jnp
from jax import lax
from jax.experimental import pallas as pl
from jax.experimental.pallas import tpu as pltpu
from jax.sharding import PartitionSpec as P

rope_base = 1000000.0
norm_eps = 1e-06
f32 = jnp.float32
bf16 = jnp.bfloat16
whole = pl.BlockSpec(memory_space=pltpu.VMEM)
in_place = pl.BlockSpec(memory_space=pl.ANY)


def rms_scale(values):
    return lax.rsqrt(jnp.mean(values * values, axis=-1, keepdims=True) + norm_eps)


def matmul(left, right):
    return jnp.dot(left, right, preferred_element_type=f32)


def contract_rows(left, right):
    return lax.dot_general(left, right, (((0,), (0,)), ((), ())), preferred_element_type=f32)


def times_transposed(left, right):
    return lax.dot_general(left, right, (((1,), (1,)), ((), ())), preferred_element_type=f32)


def rotate(values):
    half_width = values.shape[-1] // 2
    return jnp.concatenate([-values[..., half_width:], values[..., :half_width]], axis=-1)


def flip_bit(value, bit):
    return value + bit * (1 - 2 * lax.rem(lax.div(value, bit), 2))


class Peers:
    def __init__(self, groups, lanes):
        self.groups, self.lanes = groups, lanes
        self.far = groups // 2
        self.chips = lanes // 2
        self.group = lax.axis_index("expert")
        self.lane = lax.axis_index("tensor")
        self.core = lax.rem(self.lane, 2)
        self.chip = lax.div(self.lane, 2)
        if groups == 8:
            z, y = lax.div(self.group, 2), lax.rem(self.group, 2)
            self.place = z + y * (7 - 2 * z)
        else:
            self.place = self.group

    def group_at(self, offset):
        place = lax.rem(self.place + (offset + self.groups), self.groups)
        if self.groups == 8:
            y = lax.div(place, 4)
            return 2 * (place + y * (7 - 2 * place)) + y
        return place

    def at(self, offset):
        return (self.group_at(offset), self.lane)

    def other_core(self):
        return (self.group, self.lane + 1 - 2 * self.core)

    def chip_bits(self):
        return [1 << i for i in range(self.chips.bit_length() - 1)]

    def other_chip(self, bit):
        return (self.group, 2 * flip_bit(self.chip, bit) + self.core)

    def offsets(self):
        return [0] + [s * k for k in range(1, self.far) for s in (1, -1)] + [self.far]

    def meet(self, peers):
        barrier = pltpu.get_barrier_semaphore()
        for peer in peers:
            pl.semaphore_signal(
                barrier, inc=1, device_id=peer, device_id_type=pl.DeviceIdType.MESH
            )
        pl.semaphore_wait(barrier, len(peers))


class Copies:
    def __init__(self, send_sems, recv_sems):
        self.send_sems, self.recv_sems = send_sems, recv_sems
        self.planned = []

    def plan(self, source, target, peer, arriving=None, ends=True):
        index = self.planned_count()
        arriving = target if arriving is None else arriving

        def copy(source, target):
            return pltpu.make_async_remote_copy(
                src_ref=source,
                dst_ref=target,
                send_sem=self.send_sems.at[index],
                recv_sem=self.recv_sems.at[index],
                device_id=peer,
                device_id_type=pl.DeviceIdType.MESH,
            )

        made = Planned(copy(source, target), copy(arriving, arriving))
        self.planned.append((made, ends))
        return made

    def planned_count(self):
        return len(self.planned)

    def start(self, source, target, peer, arriving=None):
        made = self.plan(source, target, peer, arriving)
        made.start()
        return made.wait

    def finish(self):
        for made, ends in self.planned:
            if ends:
                made.sent()


class Planned:
    def __init__(self, mine, theirs):
        self.start, self.sent, self.wait = mine.start, mine.wait_send, theirs.wait_recv


def tiles(rows, size, step):
    def body(i, carry):
        step(pl.ds(pl.multiple_of(i * size, size), size))
        return carry

    lax.fori_loop(0, rows // size, body, 0)


def nt(left, right):
    return lax.dot_general(left, right, (((1,), (1,)), ((), ())), preferred_element_type=f32)


def spans(total, size):
    return [(at, min(size, total - at)) for at in range(0, total, size)]


class Sizes:
    def __init__(self, **sizes):
        self.__dict__.update(sizes)


class Work:
    def __init__(self, sizes, expert, bufs):
        self.sizes, self.expert = sizes, expert
        self.__dict__.update(bufs)

    def place(self, s, ids):
        z = self.sizes
        named = jnp.max(jnp.where(ids == self.expert, 1.0, 0.0), axis=0, keepdims=True)
        named = jnp.concatenate([named, jnp.zeros((7, z.seq), f32)], axis=0).astype(bf16)
        along = nt(named, self.ranker[...]) - 1024.0
        down = nt(self.ranker[...], named) - 1024.0
        slots = lax.broadcasted_iota(jnp.int32, (z.capacity, z.seq), 0).astype(f32)
        self.pick[s] = jnp.where(along[0:1, :] == slots, 1.0, 0.0).astype(bf16)
        slots = lax.broadcasted_iota(jnp.int32, (z.seq, z.capacity), 1).astype(f32)
        self.put[s] = jnp.where(down[:, 0:1] == slots, 1.0, 0.0).astype(bf16)

    def rows_of(self, s):
        return pl.ds(s * self.sizes.capacity, self.sizes.capacity)

    def tokens_of(self, s):
        return pl.ds(s * self.sizes.seq, self.sizes.seq)

    def take(self):
        z = self.sizes

        def step(cols):
            for s in range(2):
                picked = matmul(self.pick[s], self.tokens[self.tokens_of(s), cols])
                self.rows[self.rows_of(s), cols] = picked.astype(bf16)
                picked = matmul(self.pick[s], self.grads[self.tokens_of(s), cols])
                self.row_grads[self.rows_of(s), cols] = picked.astype(bf16)

        tiles(z.width, 256, step)

    def routed(self, small):
        z = self.sizes
        rows = self.rows[...]
        logits = matmul(rows, self.router[...])
        lanes = lax.broadcasted_iota(jnp.int32, logits.shape, 1)
        logits = jnp.where(lanes < z.experts, logits, -1e30)
        weights = jnp.exp(logits - jnp.max(logits, axis=1, keepdims=True))
        mine = jnp.sum(jnp.where(lanes == self.expert, weights, 0.0), axis=1, keepdims=True)
        gate = mine / jnp.sum(weights, axis=1, keepdims=True)
        d_gate = jnp.zeros_like(gate)
        for at, size in spans(z.ff, 256):
            a = nt(self.rows[...], self.w_in[pl.ds(at, size), :])
            b = nt(self.rows[...], self.w_in[pl.ds(z.ff + at, size), :])
            u = nt(self.row_grads[...], self.w_out[pl.ds(at, size), :])
            cols = pl.ds(at, size)
            sigma = 1.0 / (1.0 + jnp.exp(-a))
            silu = a * sigma
            hidden = (silu * b).astype(bf16).astype(f32)
            d_gate = d_gate + jnp.sum(hidden * u, axis=1, keepdims=True)
            self.gated[:, cols] = (hidden * gate).astype(bf16)
            d_hidden = u * gate
            self.d_a[:, cols] = (d_hidden * b * sigma * (1.0 + a * (1.0 - sigma))).astype(bf16)
            self.d_b[:, cols] = (d_hidden * silu).astype(bf16)
        for s in range(2):
            mine = d_gate[s * z.capacity : (s + 1) * z.capacity]
            small[s][pl.ds(0, 1), :] = jnp.sum(
                jnp.where(self.pick[s].astype(f32) > 0.5, mine, 0.0), axis=0, keepdims=True
            )

        def step(cols):
            back = matmul(self.d_a[...], self.w_in[pl.ds(0, z.ff), cols])
            back = back + matmul(self.d_b[...], self.w_in[pl.ds(z.ff, z.ff), cols])
            self.d_rows[:, cols] = back.astype(bf16)

        tiles(z.width, 256, step)

    def shared(self, small):
        z = self.sizes
        for s in range(2):
            at = self.tokens_of(s)
            tokens = self.tokens[at, :]
            logits = matmul(tokens, self.router[...])
            lanes = lax.broadcasted_iota(jnp.int32, logits.shape, 1)
            logit = jnp.sum(jnp.where(lanes == z.experts, logits, 0.0), axis=1, keepdims=True)
            sig = 1.0 / (1.0 + jnp.exp(-logit))
            both = matmul(tokens, self.s_in[...])
            a, b = both[:, : z.units], both[:, z.units :]
            u = nt(self.grads[at, :], self.s_out[...])
            sigma = 1.0 / (1.0 + jnp.exp(-a))
            silu = a * sigma
            hidden = (silu * b).astype(bf16).astype(f32)
            d_sig = lax.dot_general(
                jnp.ones((8, z.units), f32),
                hidden * u,
                (((1,), (1,)), ((), ())),
                precision=lax.Precision.HIGHEST,
                preferred_element_type=f32,
            )
            small[s][pl.ds(1, 1), :] = d_sig[0:1]
            self.s_gated[at, :] = (hidden * sig).astype(bf16)
            d_hidden = u * sig
            d_a = d_hidden * b * sigma * (1.0 + a * (1.0 - sigma))
            self.s_d_both[at, : z.units] = d_a.astype(bf16)
            self.s_d_both[at, z.units :] = (d_hidden * silu).astype(bf16)

    def give(self):
        z = self.sizes

        def step(cols):
            self.out_rows[...] = matmul(self.gated[...], self.w_out[:, cols]).astype(bf16)
            out = matmul(self.s_gated[...], self.s_out[:, cols])
            back = nt(self.s_d_both[...], self.s_in[cols, :])
            for s in range(2):
                at = slice(s * z.seq, (s + 1) * z.seq)
                mine = out[at] + matmul(self.put[s], self.out_rows[self.rows_of(s), :])
                self.out[self.tokens_of(s), cols] = mine.astype(bf16)
                mine = back[at] + matmul(self.put[s], self.d_rows[self.rows_of(s), cols])
                self.d_in[self.tokens_of(s), cols] = mine.astype(bf16)

        tiles(z.width, 256, step)


def experts_kernel(z, names, *refs):
    r = Sizes(**dict(zip(names, refs)))
    groups, lanes = z.groups, z.lanes
    peers = Peers(groups, lanes)
    far, bits = peers.far, peers.chip_bits()
    seq = z.seq
    half, piece = seq // 2, seq // lanes
    core = peers.core
    own = core * half
    half_rows = pl.ds(pl.multiple_of(own, half), half)
    other_rows = pl.ds(pl.multiple_of(half - own, half), half)
    first = pl.multiple_of((core * peers.chips + peers.chip) * piece, piece)
    me = peers.group
    others = [k for k in peers.offsets() if k != 0]
    step_of = {k: 2 * k - 1 if k > 0 else -2 * k for k in peers.offsets()}
    slot = {k: peers.group_at(k) for k in range(-far, far + 1)}
    ahead, behind = peers.at(1), peers.at(-1)
    core_peer = peers.other_core()
    chip_peer = {b: peers.other_chip(b) for b in bits}
    peers.meet([peers.at(k) for k in others] + [core_peer] + [chip_peer[b] for b in bits])
    copies = Copies(r.send_sems, r.recv_sems)

    def local(source, target, number):
        return pltpu.make_async_copy(source, target, r.local_sems.at[number])

    def remote(source, target, send_sem, recv_sem, peer):
        return pltpu.make_async_remote_copy(
            src_ref=source,
            dst_ref=target,
            send_sem=send_sem,
            recv_sem=recv_sem,
            device_id=peer,
            device_id_type=pl.DeviceIdType.MESH,
        )

    ff_own = z.ff // 2
    mine_at = pl.multiple_of(core * ff_own, 16)
    theirs_at = pl.multiple_of((1 - core) * ff_own, 16)
    weights, traded = [], []
    for number, (source, target, base) in enumerate(
        [(r.gate, r.w_in, 0), (r.up, r.w_in, z.ff), (r.down, r.w_out, 0)]
    ):
        rows = pl.ds(base + mine_at, ff_own)
        weights.append(local(source.at[core], target.at[rows], number))
        traded.append(
            copies.plan(
                source.at[1 - core],
                target.at[rows],
                core_peer,
                target.at[pl.ds(base + theirs_at, ff_own)],
            )
        )
    weights += [
        local(r.s_in_hbm, r.s_in, 3),
        local(r.s_out_hbm, r.s_out, 4),
        local(r.router_hbm, r.router, 5),
    ]
    own_part = local(r.part.at[half_rows], r.total, 6)
    own_grad = local(r.grad, r.grads_all.at[me], 7)
    own_tokens = local(r.normed, r.tokens_all.at[me, half_rows], 8)
    own_hidden = local(r.hidden.at[half_rows], r.stage.at[0], 9)
    keep_resid = local(r.wide, r.resid, 10)

    def hop(array, k, start, size, source=None):
        held = slot[k + 1] if k < 0 else slot[k - 1]
        rows = pl.ds(pl.multiple_of(start, size), size)
        return copies.plan(
            array.at[held, rows] if source is None else source,
            array.at[held, rows],
            ahead if k < 0 else behind,
            array.at[slot[k], rows],
        )

    def chip_swap(array, k, bit):
        size = bit * piece
        start = (core * peers.chips + lax.div(peers.chip, bit) * bit) * piece
        theirs = (core * peers.chips + lax.div(flip_bit(peers.chip, bit), bit) * bit) * piece
        rows = pl.ds(pl.multiple_of(start, size), size)
        arriving = pl.ds(pl.multiple_of(theirs, size), size)
        return copies.plan(
            array.at[slot[k], rows],
            array.at[slot[k], rows],
            chip_peer[bit],
            array.at[slot[k], arriving],
        )

    def core_swap(array, k, source=None):
        return copies.plan(
            array.at[slot[k], half_rows] if source is None else source,
            array.at[slot[k], half_rows],
            core_peer,
            array.at[slot[k], other_rows],
        )

    signed = [s * k for k in range(1, far) for s in (-1, 1)]
    ids_got = [
        copies.plan(r.ids, r.ids_all.at[me], peers.at(k), r.ids_all.at[slot[-k]]) for k in others
    ]
    own_piece = r.grad.at[pl.ds(first, piece)]
    g_ring = {
        k: hop(r.grads_all, k, first, piece, own_piece if abs(k) == 1 else None) for k in signed
    }
    g_ring[-far] = hop(r.grads_all, -far, first, piece // 2)
    g_ring[far] = hop(r.grads_all, far, first + piece // 2, piece // 2)
    x_ring = {
        k: hop(r.tokens_all, k, own, half, r.normed if abs(k) == 1 else None) for k in signed
    }
    x_ring[-far] = hop(r.tokens_all, -far, own, half // 2)
    x_ring[far] = hop(r.tokens_all, far, own + half // 2, half // 2)
    g_chip = {k: [chip_swap(r.grads_all, k, b) for b in bits] for k in others}
    g_core = {k: core_swap(r.grads_all, k) for k in others}
    x_core = {
        k: core_swap(r.tokens_all, k, r.normed if k == 0 else None) for k in peers.offsets()
    }
    part_core = copies.plan(r.part.at[other_rows], r.from_core, core_peer)
    part_chip = [
        copies.plan(r.total, r.part_chip.at[i], chip_peer[b], ends=False)
        for i, b in enumerate(bits)
    ]

    ring_up, ring_down = {}, {}
    lower, upper, all_rows = pl.ds(0, half // 2), pl.ds(half // 2, half // 2), pl.ds(0, half)
    for k in range(far, 0, -1):
        rows_up, rows_down = (lower, upper) if k == far else (all_rows, all_rows)
        at_up, at_down = (0, 0) if k == far else (2 * (far - k) - 1, 2 * (far - k))
        odd = k % 2
        ring_up[k] = copies.plan(
            r.stage.at[odd, rows_up], r.from_ring.at[at_up, rows_up], ahead, ends=False
        )
        ring_down[k] = copies.plan(
            r.stage.at[odd if k == far else 2 + odd, rows_down],
            r.from_ring.at[at_down, rows_down],
            behind,
            ends=False,
        )
    home_chip = [
        copies.plan(r.total, r.from_chip.at[i], chip_peer[b], ends=False)
        for i, b in enumerate(bits)
    ]
    small_peers = [core_peer] + [chip_peer[b] for b in bits]
    small_swaps = [
        copies.plan(r.small_swap.at[2 * i], r.small_swap.at[2 * i + 1], peer)
        for i, peer in enumerate(small_peers)
    ]

    part_core.start()
    own_part.start()
    own_hidden.start()
    g_ring[-1].start()
    g_ring[1].start()
    for copy in ids_got:
        copy.start()
    r.ids_all[me] = r.ids[...]
    for copy in weights + traded:
        copy.start()
    own_grad.start()
    token = lax.broadcasted_iota(jnp.int32, (seq, seq), 0)
    other = lax.broadcasted_iota(jnp.int32, (seq, seq), 1)
    ranks = jnp.where(other < token, 1.0, jnp.where(other == token, 1024.0, 0.0))
    r.ranker[...] = ranks.astype(bf16)

    own_part.wait()
    part_core.wait()

    def add_core(rows):
        both = r.total[rows, :].astype(f32) + r.from_core[rows, :].astype(f32)
        r.total[rows, :] = both.astype(bf16)

    tiles(half, 32, add_core)
    part_chip[0].start()
    own_hidden.wait()
    for k in range(2, far):
        for s in (-1, 1):
            g_ring[s * (k - 1)].wait()
            g_ring[s * k].start()
        if k != 2:
            continue
        for i, bit in enumerate(bits):
            part_chip[i].wait()
            part_chip[i].sent()

            def add_chip(rows, i=i):
                both = r.total[rows, :].astype(f32) + r.part_chip[i, rows, :].astype(f32)
                if i + 1 < len(bits):
                    r.total[rows, :] = both.astype(bf16)
                    return
                both = r.stage[0, rows, :].astype(f32) + both
                r.wide[rows, :] = both
                r.normed[rows, :] = (both * rms_scale(both) * r.gain[...]).astype(bf16)

            tiles(half, 32, add_chip)
            if i + 1 < len(bits):
                part_chip[i + 1].start()
        x_ring[-1].start()
        x_ring[1].start()
        x_core[0].start()
        own_tokens.start()
        keep_resid.start()
    for k in signed[:-2]:
        g_chip[k][0].start()
    for copy in ids_got + weights + traded:
        copy.wait()
    own_grad.wait()
    own_tokens.wait()
    keep_resid.wait()

    def finish_grads(ks):
        for k in ks:
            for i in range(len(bits)):
                g_chip[k][i].wait()
                if i + 1 < len(bits):
                    g_chip[k][i + 1].start()
            g_core[k].start()

    def events(p):
        for q in range(far):

            @pl.when(p == q)
            def _(k=q + 1):
                if k < far:
                    for s in (-1, 1):
                        x_ring[s * k].wait()
                        if k + 1 < far:
                            x_ring[s * (k + 1)].start()
                    if k + 1 == far:
                        x_ring[-far].start()
                        x_ring[far].start()
                    for s in (-1, 1):
                        x_core[s * k].start()
                else:
                    x_ring[-far].wait()
                    x_ring[far].wait()
                    x_core[far].start()
                if k == 1:
                    for s in (-1, 1):
                        g_ring[s * (far - 1)].wait()
                        g_ring[s * far].start()
                        g_chip[s * (far - 1)][0].start()
                if k == 2:
                    g_ring[-far].wait()
                    g_ring[far].wait()
                    g_chip[far][0].start()
                finish_grads([-k, k] if k < far else [far])
                x_core[1 - k].wait()
                x_core[k].wait()
                g_core[k].wait()
                if k > 1:
                    g_core[1 - k].wait()

    def small_copy(i, peer):
        return remote(
            r.small_out.at[i], r.small_in.at[i], r.small_send.at[i], r.small_recv.at[i], peer
        )

    def given_copy(i, source):
        return remote(source, r.given.at[i], r.give_send.at[i], r.give_recv.at[i], core_peer)

    def main(tokens, grads, rows, row_grads, d_rows, out_rows, gated, d_a, d_b, s_gated,
             s_d_both, out, d_in, pick, put):
        work = Work(
            z,
            me * 2 + core,
            dict(
                tokens=tokens, grads=grads, rows=rows, row_grads=row_grads, d_rows=d_rows,
                out_rows=out_rows, gated=gated, d_a=d_a, d_b=d_b, s_gated=s_gated,
                s_d_both=s_d_both, out=out, d_in=d_in, pick=pick, put=put, w_in=r.w_in,
                w_out=r.w_out, s_in=r.s_in, s_out=r.s_out, router=r.router, ranker=r.ranker,
            ),
        )

        def leave(p, slots):
            found = []
            for s in range(2):
                i = 2 * p + s
                keep = pl.ds(pl.multiple_of(s * seq + own, half), half)
                give = pl.ds(pl.multiple_of(s * seq + half - own, half), half)
                sent = given_copy(i, d_in.at[give])
                kept = local(d_in.at[keep], r.kept.at[i], 12 + s)
                found += [(kept.start, kept.wait), (sent.start, sent.wait_send)]
                for lane in range(lanes):
                    from_row = s * seq + (lane % 2 * peers.chips + lane // 2) * piece
                    stored = local(
                        out.at[pl.ds(from_row, piece)],
                        r.outs_all.at[slots[s], pl.ds(lane * piece, piece)],
                        25 + s * lanes + lane,
                    )
                    found.append((stored.start, stored.wait))
            return found

        def loop(p, carry):
            slots = [peers.group_at(-p), peers.group_at(p + 1)]
            events(p)
            loads = []
            for s in range(2):
                at = pl.ds(s * seq, seq)
                loads.append(local(r.tokens_all.at[slots[s]], tokens.at[at], s))
                loads.append(local(r.grads_all.at[slots[s]], grads.at[at], 2 + s))
            for copy in loads:
                copy.start()
            for s in range(2):
                work.place(s, r.ids_all[slots[s]])
            for copy in loads:
                copy.wait()
            at = pl.ds(pl.multiple_of(p * 2 * z.capacity, 2 * z.capacity), 2 * z.capacity)
            saves = [
                local(source, target.at[at], 16 + n)
                for n, (source, target) in enumerate(
                    [
                        (rows, r.rows_all),
                        (row_grads, r.row_grads_all),
                        (gated, r.gated_all),
                        (d_a, r.d_a_all),
                        (d_b, r.d_b_all),
                    ]
                )
            ]
            for s in range(2):
                mine = pl.ds(s * seq, seq)
                saves.append(local(s_gated.at[mine], r.s_gated_all.at[slots[s]], 21 + 2 * s))
                saves.append(local(s_d_both.at[mine], r.s_d_both_all.at[slots[s]], 22 + 2 * s))
            small = [r.small_out.at[2 * p], r.small_out.at[2 * p + 1]]
            work.take()
            for copy in saves[:2]:
                copy.start()
            work.routed(small)
            for copy in saves[2:5]:
                copy.start()
            work.shared(small)
            for copy in saves[5:]:
                copy.start()
            small_copy(2 * p + 1, (slots[1], peers.lane)).start()

            @pl.when(p > 0)
            def _():
                small_copy(2 * p, (slots[0], peers.lane)).start()
                for _, wait in leave(p - 1, slots):
                    wait()

            work.give()
            for start, _ in leave(p, slots):
                start()
            for copy in saves:
                copy.wait()
            return carry

        lax.fori_loop(0, far, loop, 0)
        for _, wait in leave(far - 1, [me, me]):
            wait()

    pl.run_scoped(
        main,
        tokens=pltpu.VMEM((2 * seq, z.width), bf16),
        grads=pltpu.VMEM((2 * seq, z.width), bf16),
        rows=pltpu.VMEM((2 * z.capacity, z.width), bf16),
        row_grads=pltpu.VMEM((2 * z.capacity, z.width), bf16),
        d_rows=pltpu.VMEM((2 * z.capacity, z.width), bf16),
        out_rows=pltpu.VMEM((2 * z.capacity, 256), bf16),
        gated=pltpu.VMEM((2 * z.capacity, z.ff), bf16),
        d_a=pltpu.VMEM((2 * z.capacity, z.ff), bf16),
        d_b=pltpu.VMEM((2 * z.capacity, z.ff), bf16),
        s_gated=pltpu.VMEM((2 * seq, z.units), bf16),
        s_d_both=pltpu.VMEM((2 * seq, 2 * z.units), bf16),
        out=pltpu.VMEM((2 * seq, z.width), bf16),
        d_in=pltpu.VMEM((2 * seq, z.width), bf16),
        pick=pltpu.VMEM((2, z.capacity, seq), bf16),
        put=pltpu.VMEM((2, seq, z.capacity), bf16),
    )

    def fetch(k, place, core_place):
        i = step_of[k]
        given_copy(i, r.given.at[i]).wait_recv()
        loads = [
            local(r.kept.at[i], r.stage.at[place], 0),
            local(r.given.at[i], r.stage_core.at[core_place], 1),
        ]
        for copy in loads:
            copy.start()
        for copy in loads:
            copy.wait()

    def arrived(ring, index, rows, place):
        ring.wait()
        copy = local(r.from_ring.at[index, rows], r.stage_ring.at[place, rows], 2 + place)
        copy.start()
        copy.wait()

    def add(place, core_place, start, size, ring_place=None):
        def step(rows):
            at = pl.ds(pl.multiple_of(start + rows.start, rows.size), rows.size)
            value = r.stage[place, at, :].astype(f32) + r.stage_core[core_place, at, :].astype(f32)
            if ring_place is not None:
                value = value + r.stage_ring[ring_place, at, :].astype(f32)
            r.stage[place, at, :] = value.astype(bf16)

        tiles(size, 32, step)

    def ring_stage(k):
        odd = k % 2
        if k + 2 <= far:
            ring_up[k + 2].sent()
            ring_down[k + 2].sent()
        fetch(k, odd, 0)
        fetch(-k, 2 + odd, 1)
        at = 0 if k == far - 1 else 2 * (far - k) - 3
        if k == far - 1:
            add(odd, 0, half // 2, half // 2)
            add(2 + odd, 1, 0, half // 2)
            arrived(ring_up[far], 0, lower, 0)
            add(odd, 0, 0, half // 2, 0)
        else:
            arrived(ring_up[k + 1], at, all_rows, 0)
            add(odd, 0, 0, half, 0)
        ring_up[k].start()
        if k == far - 1:
            arrived(ring_down[far], 0, upper, 1)
            add(2 + odd, 1, half // 2, half // 2, 1)
        else:
            arrived(ring_down[k + 1], at + 1, all_rows, 1)
            add(2 + odd, 1, 0, half, 1)
        ring_down[k].start()

    fetch(far, far % 2, 0)
    add(far % 2, 0, 0, half)
    ring_up[far].start()
    ring_down[far].start()

    features = z.width // groups

    def columns_of(t):
        return pl.ds(pl.multiple_of(t * features, features), features)

    def routed_grads(gated, d_a, d_b, rows, row_grads, wide_in, wide_out):
        whole_loads = [
            local(r.gated_all, gated, 4),
            local(r.d_a_all, d_a, 5),
            local(r.d_b_all, d_b, 6),
        ]

        def loads(t):
            odd = lax.rem(t, 2)
            cols = columns_of(t)
            return [
                local(r.rows_all.at[:, cols], rows.at[odd], 7 + odd),
                local(r.row_grads_all.at[:, cols], row_grads.at[odd], 9 + odd),
            ]

        def stores(t):
            odd = lax.rem(t, 2)
            cols = columns_of(t)
            found = []
            for n, (source, base, target) in enumerate(
                [
                    (wide_in, 0, r.g_gate),
                    (wide_in, z.ff, r.g_up),
                    (wide_out, 0, r.g_down),
                ]
            ):
                here = source.at[odd, pl.ds(base + mine_at, ff_own)]
                there = source.at[odd, pl.ds(base + theirs_at, ff_own)]
                kept = local(here, target.at[core, :, cols], 11 + 2 * n + odd)
                sent = remote(
                    there,
                    target.at[core, :, cols],
                    r.grad_send.at[2 * n + odd],
                    r.grad_recv.at[n * groups + t],
                    core_peer,
                )
                found.append((kept, sent))
            return found

        def settle(t):
            for kept, sent in stores(t):
                kept.wait()
                sent.wait_send()

        def unit(t, carry):
            odd = lax.rem(t, 2)

            @pl.when(t + 1 < groups)
            def _():
                for copy in loads(t + 1):
                    copy.start()

            for copy in loads(t):
                copy.wait()

            @pl.when(t >= 2)
            def _():
                settle(t - 2)

            wide_in[odd, pl.ds(0, z.ff), :] = contract_rows(d_a[...], rows[odd])
            wide_in[odd, pl.ds(z.ff, z.ff), :] = contract_rows(d_b[...], rows[odd])
            wide_out[odd] = contract_rows(gated[...], row_grads[odd])
            for kept, sent in stores(t):
                kept.start()
                sent.start()
            return carry

        for copy in whole_loads + loads(0):
            copy.start()
        for copy in whole_loads:
            copy.wait()
        lax.fori_loop(0, groups // 2, unit, 0)
        ring_stage(far - 1)
        lax.fori_loop(groups // 2, groups, unit, 0)
        settle(groups - 2)
        settle(groups - 1)

    tile_rows = groups * z.capacity
    pl.run_scoped(
        routed_grads,
        gated=pltpu.VMEM((tile_rows, z.ff), bf16),
        d_a=pltpu.VMEM((tile_rows, z.ff), bf16),
        d_b=pltpu.VMEM((tile_rows, z.ff), bf16),
        rows=pltpu.VMEM((2, tile_rows, features), bf16),
        row_grads=pltpu.VMEM((2, tile_rows, features), bf16),
        wide_in=pltpu.VMEM((2, 2 * z.ff, features), f32),
        wide_out=pltpu.VMEM((2, z.ff, features), f32),
    )

    def shared_grads(s_gated, s_d_both, tokens, grads, wide):
        whole_loads = [local(r.s_gated_all, s_gated, 4), local(r.s_d_both_all, s_d_both, 5)]

        def loads(t):
            odd = lax.rem(t, 2)
            cols = columns_of(t)
            return [
                local(r.tokens_all.at[:, :, cols], tokens.at[odd], 7 + odd),
                local(r.grads_all.at[:, :, cols], grads.at[odd], 9 + odd),
            ]

        def store(t):
            odd = lax.rem(t, 2)
            return local(wide.at[odd], r.s_grads.at[t], 11 + odd)

        def flat(array):
            return array.reshape(groups * seq, array.shape[-1])

        def unit(t, carry):
            odd = lax.rem(t, 2)

            @pl.when(t + 1 < groups)
            def _():
                for copy in loads(t + 1):
                    copy.start()

            for copy in loads(t):
                copy.wait()

            @pl.when(t >= 2)
            def _():
                store(t - 2).wait()

            both = contract_rows(flat(s_d_both[...]), flat(tokens[odd]))
            wide[odd, pl.ds(0, 2 * z.units), :] = both.astype(bf16)
            out = contract_rows(flat(s_gated[...]), flat(grads[odd]))
            wide[odd, pl.ds(2 * z.units, z.units), :] = out.astype(bf16)
            store(t).start()
            return carry

        for copy in whole_loads + loads(0):
            copy.start()
        for copy in whole_loads:
            copy.wait()
        stages = list(range(far - 2, 0, -1))
        done = 0
        for n, k in enumerate(stages):
            upto = groups * (n + 1) // len(stages) if n + 1 < len(stages) else groups
            lax.fori_loop(done, upto, unit, 0)
            done = upto
            ring_stage(k)
        store(groups - 2).wait()
        store(groups - 1).wait()

    pl.run_scoped(
        shared_grads,
        s_gated=pltpu.VMEM((groups, seq, z.units), bf16),
        s_d_both=pltpu.VMEM((groups, seq, 2 * z.units), bf16),
        tokens=pltpu.VMEM((2, groups, seq, features), bf16),
        grads=pltpu.VMEM((2, groups, seq, features), bf16),
        wide=pltpu.VMEM((2, 3 * z.units, features), bf16),
    )
    ring_up[2].sent()
    ring_down[2].sent()
    fetch(0, 0, 0)

    r.small_total[...] = jnp.zeros_like(r.small_total)
    d_sig = r.small_out[0, pl.ds(1, 1), :]
    r.small_total[pl.ds(me * 2 + core, 1), :] = r.small_out[0, pl.ds(0, 1), :]
    for k in others:
        i = step_of[k]
        copy = small_copy(i, peers.at(k))
        copy.wait_recv()
        copy.wait_send()
        d_sig = d_sig + r.small_in[i, pl.ds(1, 1), :]
        r.small_total[pl.ds(slot[-k] * 2 + core, 1), :] = r.small_in[i, pl.ds(0, 1), :]
    r.small_total[pl.ds(z.experts, 1), :] = d_sig
    for i, copy in enumerate(small_swaps):
        r.small_swap[2 * i] = r.small_total[...]
        copy.start()
        copy.wait()
        r.small_total[...] = r.small_swap[2 * i] + r.small_swap[2 * i + 1]

    for n, target in enumerate((r.g_gate, r.g_up, r.g_down)):
        for t in range(groups):
            arriving = target.at[1 - core, :, columns_of(t)]
            remote(
                arriving, arriving, r.grad_send.at[0], r.grad_recv.at[n * groups + t], core_peer
            ).wait_recv()

    last_at = 2 * (far - 1) - 1
    arrived(ring_up[1], last_at, all_rows, 0)
    arrived(ring_down[1], last_at + 1, all_rows, 1)

    def last(rows):
        value = r.stage[0, rows, :].astype(f32) + r.stage_core[0, rows, :].astype(f32)
        value = value + r.stage_ring[0, rows, :].astype(f32)
        value = value + r.stage_ring[1, rows, :].astype(f32)
        r.total[rows, :] = value.astype(bf16)

    tiles(half, 32, last)
    for i, copy in enumerate(home_chip):
        copy.start()
        copy.wait()
        copy.sent()

        def join(rows, i=i):
            value = r.total[rows, :].astype(f32) + r.from_chip[i, rows, :].astype(f32)
            if i + 1 < len(bits):
                r.total[rows, :] = value.astype(bf16)
            else:
                r.wide[rows, :] = value

        tiles(half, 32, join)
    keep_total = local(r.wide, r.d_total, 0)
    keep_total.start()
    ring_up[1].sent()
    ring_down[1].sent()
    copies.finish()
    keep_total.wait()


def pad_last(array, size):
    return jnp.pad(array, [(0, 0)] * (array.ndim - 1) + [(0, size - array.shape[-1])])


def round_up(value, unit):
    return -(-value // unit) * unit


def run_experts(groups, lanes, part, hidden, gain, grad, ids, weights, router, capacity):
    gate, up, down, s_gate, s_up, s_down = weights
    seq, width = grad.shape
    ff_own = gate.shape[1]
    units_true = s_gate.shape[1]
    experts = router.shape[1] - 1
    ff, units = 2 * ff_own, round_up(units_true, 128)
    half = seq // 2
    bits = (lanes // 2).bit_length() - 1
    far = groups // 2
    small_rows = round_up(experts + 1, 8)
    z = Sizes(
        groups=groups, lanes=lanes, seq=seq, width=width, ff=ff, units=units,
        capacity=capacity, experts=experts,
    )
    s_in = jnp.concatenate([pad_last(s_gate, units), pad_last(s_up, units)], axis=1)
    s_out = jnp.pad(s_down, ((0, units - units_true), (0, 0)))
    router = pad_last(router, 128)
    ins = {
        "part": (part, in_place), "hidden": (hidden, in_place), "gain": (gain, whole),
        "grad": (grad, in_place), "ids": (ids, whole), "gate": (gate, in_place),
        "up": (up, in_place), "down": (down, in_place), "s_in_hbm": (s_in, in_place),
        "s_out_hbm": (s_out, in_place), "router_hbm": (router, in_place),
    }
    rows_all = groups * capacity
    outs = {
        "normed": ((half, width), bf16, whole),
        "small_total": ((small_rows, seq), f32, whole),
        "resid": ((half, width), f32, in_place),
        "d_total": ((half, width), f32, in_place),
        "outs_all": ((groups, seq, width), bf16, in_place),
        "g_gate": (gate.shape, f32, in_place),
        "g_up": (up.shape, f32, in_place),
        "g_down": (down.shape, f32, in_place),
        "s_grads": ((groups, 3 * units, width // groups), bf16, in_place),
        "tokens_all": ((groups, seq, width), bf16, in_place),
        "grads_all": ((groups, seq, width), bf16, in_place),
        "rows_all": ((rows_all, width), bf16, in_place),
        "row_grads_all": ((rows_all, width), bf16, in_place),
        "gated_all": ((rows_all, ff), bf16, in_place),
        "d_a_all": ((rows_all, ff), bf16, in_place),
        "d_b_all": ((rows_all, ff), bf16, in_place),
        "s_gated_all": ((groups, seq, units), bf16, in_place),
        "s_d_both_all": ((groups, seq, 2 * units), bf16, in_place),
        "kept": ((groups, half, width), bf16, in_place),
        "given": ((groups, half, width), bf16, in_place),
        "from_ring": ((2 * far - 1, half, width), bf16, in_place),
    }
    copies = 3 + 2 * groups + (groups - 1) * (2 + bits) + groups + 1 + bits + 2 * far
    copies += 2 * bits + 1
    scratch = {
        "ids_all": pltpu.VMEM((groups,) + ids.shape, jnp.int32),
        "total": pltpu.VMEM((half, width), bf16),
        "from_core": pltpu.VMEM((half, width), bf16),
        "part_chip": pltpu.VMEM((max(bits, 1), half, width), bf16),
        "from_chip": pltpu.VMEM((max(bits, 1), half, width), bf16),
        "wide": pltpu.VMEM((half, width), f32),
        "stage": pltpu.VMEM((4, half, width), bf16),
        "stage_core": pltpu.VMEM((2, half, width), bf16),
        "stage_ring": pltpu.VMEM((2, half, width), bf16),
        "small_out": pltpu.VMEM((groups, 8, seq), f32),
        "small_in": pltpu.VMEM((groups, 8, seq), f32),
        "small_swap": pltpu.VMEM((2 * (1 + bits), small_rows, seq), f32),
        "ranker": pltpu.VMEM((seq, seq), bf16),
        "w_in": pltpu.VMEM((2 * ff, width), bf16),
        "w_out": pltpu.VMEM((ff, width), bf16),
        "s_in": pltpu.VMEM(s_in.shape, bf16),
        "s_out": pltpu.VMEM(s_out.shape, bf16),
        "router": pltpu.VMEM(router.shape, bf16),
        "send_sems": pltpu.SemaphoreType.DMA((copies,)),
        "recv_sems": pltpu.SemaphoreType.DMA((copies,)),
        "local_sems": pltpu.SemaphoreType.DMA((25 + 2 * lanes,)),
        "give_send": pltpu.SemaphoreType.DMA((groups,)),
        "give_recv": pltpu.SemaphoreType.DMA((groups,)),
        "small_send": pltpu.SemaphoreType.DMA((groups,)),
        "small_recv": pltpu.SemaphoreType.DMA((groups,)),
        "grad_send": pltpu.SemaphoreType.DMA((6,)),
        "grad_recv": pltpu.SemaphoreType.DMA((3 * groups,)),
    }
    names = list(ins) + list(outs) + list(scratch)
    results = pl.pallas_call(
        functools.partial(experts_kernel, z, names),
        out_shape=tuple(jax.ShapeDtypeStruct(s, d) for s, d, _ in outs.values()),
        in_specs=[spec for _, spec in ins.values()],
        out_specs=tuple(spec for _, _, spec in outs.values()),
        scratch_shapes=list(scratch.values()),
        compiler_params=pltpu.CompilerParams(
            collective_id=0, has_side_effects=True, vmem_limit_bytes=63 * 1024 * 1024
        ),
        name="run_experts",
    )(*[array for array, _ in ins.values()])
    return Sizes(**dict(zip(outs, results)), units=units)


def reduce_kernel(
    groups, lanes, tokens, parts, small,
    total, small_total,
    kept, from_core, from_ring, from_chip, small_in, small_swap,
    send_sems, recv_sems, local_sems,
):
    peers = Peers(groups, lanes)
    far, bits = peers.far, peers.chip_bits()
    rows_all = kept.shape[1]
    half = rows_all // 2
    me = peers.group
    offsets = [far] + [s * k for k in range(far - 1, 0, -1) for s in (1, -1)] + [0]
    number = {k: i for i, k in enumerate(offsets)}
    others = [k for k in offsets if k != 0]
    peers.meet(
        [peers.at(k) for k in others]
        + [peers.other_core()]
        + [peers.other_chip(b) for b in bits]
    )
    copies = Copies(send_sems, recv_sems)
    if tokens:
        keep_rows = pl.ds(pl.multiple_of(peers.core * rows_all, rows_all), rows_all)
        give_rows = pl.ds(pl.multiple_of((1 - peers.core) * rows_all, rows_all), rows_all)
    loads, given = {}, {}
    for k in offsets:
        slot = peers.group_at(k)
        source = parts.at[slot, keep_rows] if tokens else parts.at[slot]
        loads[k] = pltpu.make_async_copy(source, kept.at[number[k]], local_sems.at[number[k]])
        loads[k].start()
        if tokens:
            given[k] = copies.start(
                parts.at[slot, give_rows], from_core.at[number[k]], peers.other_core()
            )
    small_got = [
        copies.start(small.at[peers.group_at(k)], small_in.at[number[k]], peers.at(k))
        for k in others
    ]

    def ready(k):
        loads[k].wait()
        if tokens:
            given[k]()

    def add(k, start, size, arrived=None):
        i = number[k]

        def step(rows):
            at = pl.ds(pl.multiple_of(start + rows.start, rows.size), rows.size)
            value = kept[i, at, :].astype(f32)
            if tokens:
                value = value + from_core[i, at, :].astype(f32)
            if arrived is not None:
                value = value + from_ring[arrived, at, :].astype(f32)
            kept[i, at, :] = value.astype(bf16)

        tiles(size, 32, step)

    def send(k, start, size, ahead, arriving):
        rows = pl.ds(start, size)
        return copies.start(
            kept.at[number[k], rows],
            from_ring.at[arriving, rows],
            peers.at(1) if ahead else peers.at(-1),
        )

    ready(far)
    add(far, 0, half)
    up = send(far, 0, half, True, 0)
    add(far, half, half)
    down = send(far, half, half, False, 0)
    up_at = down_at = 0
    for k in range(far - 1, 0, -1):
        ready(k)
        ready(-k)
        if k == far - 1:
            add(k, half, half)
            add(-k, 0, half)
            up()
            add(k, 0, half, up_at)
        else:
            up()
            add(k, 0, rows_all, up_at)
        up = send(k, 0, rows_all, True, 2 * (far - k) - 1)
        down()
        if k == far - 1:
            add(-k, half, half, down_at)
        else:
            add(-k, 0, rows_all, down_at)
        down = send(-k, 0, rows_all, False, 2 * (far - k))
        up_at, down_at = 2 * (far - k) - 1, 2 * (far - k)
    ready(0)

    for wait in small_got:
        wait()
    small_sum = small[me]
    for k in others:
        small_sum = small_sum + small_in[number[k]]
    small_total[...] = small_sum
    for i, peer in enumerate([peers.other_core()] + [peers.other_chip(b) for b in bits]):
        small_swap[2 * i] = small_total[...]
        copies.start(small_swap.at[2 * i], small_swap.at[2 * i + 1], peer)()
        small_total[...] = small_swap[2 * i] + small_swap[2 * i + 1]

    up()
    down()
    home = number[0]

    def last(rows):
        value = kept[home, rows, :].astype(f32)
        if tokens:
            value = value + from_core[home, rows, :].astype(f32)
        value = value + from_ring[up_at, rows, :].astype(f32)
        value = value + from_ring[down_at, rows, :].astype(f32)
        if tokens:
            kept[home, rows, :] = value.astype(bf16)
        else:
            total[rows, :] = value

    tiles(rows_all, 32, last)
    if tokens:
        for i, bit in enumerate(bits):
            wait = copies.start(kept.at[home], from_chip.at[i], peers.other_chip(bit))
            wait()
            copies.planned[-1][0].sent()
            copies.planned[-1] = (copies.planned[-1][0], False)

            def join(rows, i=i):
                value = kept[home, rows, :].astype(f32) + from_chip[i, rows, :].astype(f32)
                if i + 1 < len(bits):
                    kept[home, rows, :] = value.astype(bf16)
                else:
                    total[rows, :] = value

            tiles(rows_all, 32, join)
    copies.finish()


def reduce_parts(groups, lanes, parts, small, tokens, collective_id):
    rows = parts.shape[1] // 2 if tokens else parts.shape[1]
    width = parts.shape[2]
    bits = (lanes // 2).bit_length() - 1
    far = groups // 2
    copies = (groups if tokens else 0) + (groups - 1) + 2 * far + (1 + bits) + bits
    shape = (rows, width)
    return pl.pallas_call(
        functools.partial(reduce_kernel, groups, lanes, tokens),
        out_shape=(
            jax.ShapeDtypeStruct(shape, f32),
            jax.ShapeDtypeStruct(small.shape[1:], f32),
        ),
        in_specs=[in_place, whole],
        out_specs=(whole, whole),
        scratch_shapes=[
            pltpu.VMEM((groups,) + shape, bf16),
            pltpu.VMEM(((groups if tokens else 1),) + shape, bf16),
            pltpu.VMEM((2 * far - 1,) + shape, bf16),
            pltpu.VMEM(((max(bits, 1) if tokens else 1),) + shape, bf16),
            pltpu.VMEM(small.shape, f32),
            pltpu.VMEM((2 * (1 + bits),) + small.shape[1:], f32),
            pltpu.SemaphoreType.DMA((copies,)),
            pltpu.SemaphoreType.DMA((copies,)),
            pltpu.SemaphoreType.DMA((groups,)),
        ],
        compiler_params=pltpu.CompilerParams(
            collective_id=collective_id,
            has_side_effects=True,
            vmem_limit_bytes=58 * 1024 * 1024,
        ),
        name="reduce_tokens" if tokens else "reduce_weights",
    )(parts, small)


def attend_forward(query, key, value, allowed, score_scale):
    scores = jnp.einsum("qhd,khd->hqk", query, key, preferred_element_type=f32) * score_scale
    scores = jnp.where(allowed[None], scores, -1e30)
    highest = jnp.max(scores, axis=-1, keepdims=True)
    log_total = highest + jnp.log(jnp.sum(jnp.exp(scores - highest), axis=-1, keepdims=True))
    probs = jnp.exp(scores - log_total)
    contexts = jnp.einsum("hqk,khd->qhd", probs.astype(bf16), value, preferred_element_type=f32)
    return contexts.astype(bf16), log_total


def attend_backward(query, key, value, d_context, log_total, allowed, score_scale):
    scores = jnp.einsum("qhd,khd->hqk", query, key, preferred_element_type=f32) * score_scale
    probs = jnp.exp(jnp.where(allowed[None], scores, -1e30) - log_total)
    d_probs = jnp.einsum("qhd,khd->hqk", d_context, value, preferred_element_type=f32)
    row_dot = jnp.sum(probs * d_probs, axis=-1, keepdims=True)
    d_scores = (probs * (d_probs - row_dot)).astype(bf16)
    d_query = jnp.einsum("hqk,khd->qhd", d_scores, key, preferred_element_type=f32) * score_scale
    d_key = jnp.einsum("hqk,qhd->khd", d_scores, query, preferred_element_type=f32) * score_scale
    d_value = jnp.einsum("hqk,qhd->khd", probs.astype(bf16), d_context, preferred_element_type=f32)
    return d_query, d_key, d_value


def norm_backward(values, scale, gain, d_normed):
    inner = d_normed * gain
    mean = jnp.mean(inner * values, axis=-1, keepdims=True)
    return scale * inner - values * (scale * scale * scale) * mean


def on_device(
    hidden_in,
    seq_lengths,
    expert_ids,
    attn_gain,
    w_query,
    w_key,
    w_value,
    b_query,
    b_key,
    b_value,
    w_output,
    ffn_gain,
    w_router,
    w_sigmoid,
    shared_gate,
    shared_up,
    shared_down,
    expert_gate,
    expert_up,
    expert_down,
    out_grad,
):
    seq, width = hidden_in.shape
    heads, head_width = b_query.shape
    head_all = heads * head_width
    top_count = expert_ids.shape[1]
    experts_all = w_router.shape[1]
    held = expert_gate.shape[0]
    groups = lax.axis_size("expert")
    lane_count = lax.axis_size("tensor")
    group = lax.axis_index("expert")
    lane = lax.axis_index("tensor")
    capacity = 3 * seq * top_count // (2 * experts_all)
    score_scale = 1.0 / math.sqrt(head_width)
    length = seq_lengths[0]
    half = seq // 2
    features = width // groups
    half_start = (lane % 2) * half

    def half_of(array):
        return lax.dynamic_slice_in_dim(array, half_start, half, 0)

    def swap(values, bit):
        return lax.ppermute(values, "tensor", [(i, i ^ bit) for i in range(lane_count)])

    def sum_lanes(values):
        other = lax.dynamic_slice_in_dim(values, half - half_start, half, 0)
        total = (half_of(values).astype(f32) + swap(other, 1).astype(f32)).astype(bf16)
        for bit in range(1, (lane_count // 2).bit_length()):
            total32 = total.astype(f32) + swap(total, 1 << bit).astype(f32)
            total = total32.astype(bf16)
        return total32

    def both_halves(mine):
        other = swap(mine, 1)
        lower = jnp.where(half_start == 0, mine, other)
        upper = jnp.where(half_start == 0, other, mine)
        return jnp.concatenate([lower, upper], axis=0)

    hidden = hidden_in.astype(f32)
    position = jnp.arange(seq, dtype=jnp.int32)
    grad_low = jnp.where((position < length)[:, None], out_grad, jnp.zeros_like(out_grad))

    gain_attn = attn_gain.astype(f32)
    attn_scale = rms_scale(hidden)
    normed_attn = (hidden * attn_scale * gain_attn).astype(bf16)
    freq = jnp.exp(
        jnp.arange(head_width // 2, dtype=f32) * (-2.0 * math.log(rope_base) / head_width)
    )
    angle = position.astype(f32)[:, None] * freq[None, :]
    angle = jnp.concatenate([angle, angle], axis=1)
    cosine, sine = jnp.cos(angle)[:, None, :], jnp.sin(angle)[:, None, :]
    by_head = (seq, heads, head_width)
    query_pre = (matmul(normed_attn, w_query) + b_query.reshape(-1).astype(f32)).reshape(by_head)
    key_pre = (matmul(normed_attn, w_key) + b_key.reshape(-1).astype(f32)).reshape(by_head)
    value_pre = matmul(normed_attn, w_value) + b_value.reshape(-1).astype(f32)
    query = (query_pre * cosine + rotate(query_pre) * sine).astype(bf16)
    key = (key_pre * cosine + rotate(key_pre) * sine).astype(bf16)
    value = value_pre.astype(bf16).reshape(by_head)
    allowed = (position[None, :] <= position[:, None]) & (position[None, :] < length)
    context, log_total = attend_forward(query, key, value, allowed, score_scale)
    context_flat = context.reshape(seq, head_all)
    gain_ffn = ffn_gain.astype(f32)
    ids = jnp.pad(expert_ids.T, ((0, -top_count % 8), (0, 0)), constant_values=-1)
    units = shared_gate.shape[1] // groups
    ex = run_experts(
        groups,
        lane_count,
        matmul(context_flat, w_output).astype(bf16),
        hidden_in,
        gain_ffn[None, :],
        grad_low,
        ids,
        (
            jnp.swapaxes(expert_gate, 1, 2),
            jnp.swapaxes(expert_up, 1, 2),
            expert_down,
            lax.dynamic_slice_in_dim(shared_gate, group * units, units, 1),
            lax.dynamic_slice_in_dim(shared_up, group * units, units, 1),
            lax.dynamic_slice_in_dim(shared_down, group * units, units, 0),
        ),
        jnp.concatenate([w_router, w_sigmoid[:, None]], axis=1),
        capacity,
    )
    resid, normed, outs, d_in_sum, small = (
        ex.resid, ex.normed, ex.outs_all, ex.d_total, ex.small_total
    )
    g_gate, g_up, g_down = jnp.swapaxes(ex.g_gate, 1, 2), jnp.swapaxes(ex.g_up, 1, 2), ex.g_down

    ffn_scale = rms_scale(resid)
    logits = matmul(normed, w_router)
    route_probs = jax.nn.softmax(logits, axis=-1)
    sig = jax.nn.sigmoid(jnp.dot(normed, w_sigmoid, preferred_element_type=f32))

    small = half_of(small.T)
    d_probs_route, sig_grad = small[:, :experts_all], small[:, experts_all]
    d_logits = (
        route_probs
        * (d_probs_route - jnp.sum(route_probs * d_probs_route, axis=-1, keepdims=True))
    ).astype(bf16)
    d_sig_logit = (sig_grad * sig * (1.0 - sig)).astype(bf16)
    d_from_gates = (
        times_transposed(d_logits, w_router)
        + d_sig_logit.astype(f32)[:, None] * w_sigmoid.astype(f32)[None, :]
    )
    d_normed = d_in_sum + d_from_gates
    d_resid = half_of(grad_low).astype(f32) + norm_backward(resid, ffn_scale, gain_ffn, d_normed)
    d_attn = both_halves(d_resid.astype(bf16))

    d_context = times_transposed(d_attn, w_output).astype(bf16).reshape(by_head)
    d_query_rot, d_key_rot, d_value_all = attend_backward(
        query, key, value, d_context, log_total, allowed, score_scale
    )

    def unrope(values):
        return (values * cosine - rotate(values) * sine).astype(bf16).reshape(seq, head_all)

    d_query, d_key = unrope(d_query_rot), unrope(d_key_rot)
    d_value = d_value_all.astype(bf16).reshape(seq, head_all)
    d_normed_attn = (
        times_transposed(d_query, w_query)
        + times_transposed(d_key, w_key)
        + times_transposed(d_value, w_value)
    )
    grads = [contract_rows(normed_attn, d) for d in (d_query, d_key, d_value)]
    grads.append(contract_rows(d_attn, context_flat))
    grads = jnp.concatenate([g.astype(bf16) for g in grads], axis=1)

    rows = half // (lane_count // 2)
    start = (lane // 2) * rows
    mine = [
        lax.dynamic_slice_in_dim(a, start, rows, 0)
        for a in (d_normed * resid * ffn_scale, normed, d_logits, d_sig_logit[:, None])
    ]
    router_part = contract_rows(jnp.concatenate([mine[2], mine[3]], axis=1), mine[1])
    bias_part = jnp.concatenate(
        [jnp.sum(d.astype(f32), axis=0) for d in (d_query, d_key, d_value)]
    ).reshape(-1, features)
    to_groups = jnp.concatenate(
        [
            router_part,
            jnp.sum(mine[0], axis=0)[None],
            jnp.sum(d_normed_attn * hidden * attn_scale, axis=0)[None],
        ],
        axis=0,
    )
    to_groups = jnp.swapaxes(to_groups.reshape(-1, groups, features), 0, 1)
    lane_slots = (jnp.arange(lane_count) == lane).astype(f32)[:, None, None] * bias_part[None]
    lane_slots = lane_slots.reshape(-1, features)
    small = jnp.concatenate(
        [to_groups, jnp.broadcast_to(lane_slots[None], (groups,) + lane_slots.shape)], axis=1
    )
    small = jnp.pad(small, ((0, 0), (0, -small.shape[1] % 8), (0, 0)))
    grads, small = reduce_parts(
        groups, lane_count, grads.reshape(groups, features, -1), small, False, 2
    )
    biases = lax.dynamic_slice_in_dim(
        small, experts_all + 3 + lane * bias_part.shape[0], bias_part.shape[0], 0
    ).reshape(3, heads, head_width)
    biases = lax.dynamic_slice_in_dim(
        biases, group * (head_width // groups), head_width // groups, 2
    )

    outs = lax.psum_scatter(
        outs.reshape(groups * seq, width), ("expert", "tensor"), scatter_dimension=0, tiled=True
    )
    outs, grads = lax.optimization_barrier((outs, grads))
    chip = lane // 2
    piece = seq // lane_count
    layer = lax.dynamic_slice_in_dim(resid, chip * piece, piece, 0) + outs.astype(f32)
    layer = layer.astype(bf16)
    for bit in range((lane_count // 2).bit_length() - 1):
        other = swap(layer, 2 << bit)
        low = (chip >> bit) % 2 == 0
        layer = jnp.concatenate(
            [jnp.where(low, layer, other), jnp.where(low, other, layer)], axis=0
        )
    layer_out = both_halves(layer)
    d_normed_in = sum_lanes(d_normed_attn.astype(bf16))
    grad_in = d_resid + norm_backward(half_of(hidden), half_of(attn_scale), gain_attn, d_normed_in)
    grad_in = both_halves(grad_in.astype(bf16))

    shared = lax.all_to_all(ex.s_grads, "expert", split_axis=0, concat_axis=0, tiled=True)
    shared = shared.reshape(groups, 3, ex.units, features)[:, :, :units].astype(f32)
    shared = jnp.swapaxes(shared, 0, 1).reshape(3, groups * units, features)
    grad_shared_gate, grad_shared_up, grad_shared_down = shared[0].T, shared[1].T, shared[2]
    return (
        layer_out,
        grad_in,
        small[experts_all + 2],
        grads[:, :head_all],
        grads[:, head_all : 2 * head_all],
        grads[:, 2 * head_all : 3 * head_all],
        biases[0],
        biases[1],
        biases[2],
        grads[:, 3 * head_all :].T,
        small[experts_all + 1],
        small[:experts_all].T,
        small[experts_all],
        grad_shared_gate,
        grad_shared_up,
        grad_shared_down,
        g_gate,
        g_up,
        g_down,
    )


def solution(mesh):
    placed = (
        P("expert", None),
        P("expert"),
        P("expert", None),
        P(),
        P(None, "tensor"),
        P(None, "tensor"),
        P(None, "tensor"),
        P("tensor", None),
        P("tensor", None),
        P("tensor", None),
        P("tensor", None),
        P(),
        P(),
        P(),
        P(None, "tensor"),
        P(None, "tensor"),
        P("tensor", None),
        P("expert", None, "tensor"),
        P("expert", None, "tensor"),
        P("expert", "tensor", None),
        P("expert", None),
    )
    return jax.shard_map(
        on_device,
        mesh=mesh,
        in_specs=placed,
        out_specs=(
            P("expert", None),
            P("expert", None),
            P("expert"),
            P("expert", "tensor"),
            P("expert", "tensor"),
            P("expert", "tensor"),
            P("tensor", "expert"),
            P("tensor", "expert"),
            P("tensor", "expert"),
            P("tensor", "expert"),
            P("expert"),
            P("expert", None),
            P("expert"),
            P("expert", "tensor"),
            P("expert", "tensor"),
            P("tensor", "expert"),
            P("expert", None, "tensor"),
            P("expert", None, "tensor"),
            P("expert", "tensor", None),
        ),
        check_vma=False,
    )
```

```python
import functools
import math

import jax
import jax.numpy as jnp
from jax import lax
from jax.experimental import pallas as pl
from jax.experimental.pallas import tpu as pltpu
from jax.sharding import PartitionSpec as P

rope_base = 1000000.0
norm_eps = 1e-06
f32 = jnp.float32
bf16 = jnp.bfloat16
whole = pl.BlockSpec(memory_space=pltpu.VMEM)
in_place = pl.BlockSpec(memory_space=pl.ANY)


def rms_scale(values):
    return lax.rsqrt(jnp.mean(values * values, axis=-1, keepdims=True) + norm_eps)


def matmul(left, right):
    return jnp.dot(left, right, preferred_element_type=f32)


def contract_rows(left, right):
    return lax.dot_general(left, right, (((0,), (0,)), ((), ())), preferred_element_type=f32)


def times_transposed(left, right):
    return lax.dot_general(left, right, (((1,), (1,)), ((), ())), preferred_element_type=f32)


def rotate(values):
    half_width = values.shape[-1] // 2
    return jnp.concatenate([-values[..., half_width:], values[..., :half_width]], axis=-1)


def flip_bit(value, bit):
    return value + bit * (1 - 2 * lax.rem(lax.div(value, bit), 2))


class Peers:
    def __init__(self, groups, lanes):
        self.groups, self.lanes = groups, lanes
        self.far = groups // 2
        self.chips = lanes // 2
        self.group = lax.axis_index("expert")
        self.lane = lax.axis_index("tensor")
        self.core = lax.rem(self.lane, 2)
        self.chip = lax.div(self.lane, 2)
        if groups == 8:
            z, y = lax.div(self.group, 2), lax.rem(self.group, 2)
            self.place = z + y * (7 - 2 * z)
        else:
            self.place = self.group

    def group_at(self, offset):
        place = lax.rem(self.place + (offset + self.groups), self.groups)
        if self.groups == 8:
            y = lax.div(place, 4)
            return 2 * (place + y * (7 - 2 * place)) + y
        return place

    def at(self, offset):
        return (self.group_at(offset), self.lane)

    def other_core(self):
        return (self.group, self.lane + 1 - 2 * self.core)

    def chip_bits(self):
        return [1 << i for i in range(self.chips.bit_length() - 1)]

    def other_chip(self, bit):
        return (self.group, 2 * flip_bit(self.chip, bit) + self.core)

    def offsets(self):
        return [0] + [s * k for k in range(1, self.far) for s in (1, -1)] + [self.far]

    def meet(self, peers):
        barrier = pltpu.get_barrier_semaphore()
        for peer in peers:
            pl.semaphore_signal(
                barrier, inc=1, device_id=peer, device_id_type=pl.DeviceIdType.MESH
            )
        pl.semaphore_wait(barrier, len(peers))


class Copies:
    def __init__(self, send_sems, recv_sems):
        self.send_sems, self.recv_sems = send_sems, recv_sems
        self.planned = []

    def plan(self, source, target, peer, arriving=None, ends=True):
        index = self.planned_count()
        arriving = target if arriving is None else arriving

        def copy(source, target):
            return pltpu.make_async_remote_copy(
                src_ref=source,
                dst_ref=target,
                send_sem=self.send_sems.at[index],
                recv_sem=self.recv_sems.at[index],
                device_id=peer,
                device_id_type=pl.DeviceIdType.MESH,
            )

        made = Planned(copy(source, target), copy(arriving, arriving))
        self.planned.append((made, ends))
        return made

    def planned_count(self):
        return len(self.planned)

    def start(self, source, target, peer, arriving=None):
        made = self.plan(source, target, peer, arriving)
        made.start()
        return made.wait

    def finish(self):
        for made, ends in self.planned:
            if ends:
                made.sent()


class Planned:
    def __init__(self, mine, theirs):
        self.start, self.sent, self.wait = mine.start, mine.wait_send, theirs.wait_recv


class RingSum:
    def __init__(self, copies, peers, stage, received, rows, places, first=1, last=None, eager=False):
        far = peers.far
        self.far, self.size, self.first, self.eager = far, rows // 2, first, eager
        self.places = places
        self.copies = {}
        for j in range(first, 2 * far if last is None else last + 1):
            for way, peer in ((0, peers.at(1)), (1, peers.at(-1))):
                at = pl.ds(self.start(j, way), self.size)
                self.copies[j, way] = copies.plan(
                    stage.at[self.place(j, way), at],
                    received.at[way, j - 1],
                    peer,
                    ends=False,
                )

    def offset(self, j, way):
        k = self.far - j // 2
        return k if way == 0 or k == self.far else -k

    def start(self, j, way):
        return self.size * ((j + 1 + way) % 2)

    def place(self, j, way):
        return self.places(self.offset(j, way), way)

    def step(self, j, prepare, merge):
        if j % 2 == 0 or j == self.first:
            for way in (0, 1):
                for old in (j - 4, j - 3):
                    if (old, way) in self.copies and j % 2 == 0:
                        self.copies[old, way].sent()
            for way in (0, 1) if j > 1 else (0,):
                prepare(self.offset(j, way), way)
        for way in (0, 1):
            before = (way, j - 3) if j > 2 else None
            if self.eager and j - 2 >= self.first:
                self.copies[j - 2, way].wait()
            merge(self.place(j, way), way if j > 1 else 0, self.start(j, way), self.size, before)
            if self.eager:
                self.copies[j, way].start()
        if self.eager:
            return
        for way in (0, 1):
            if j > self.first:
                self.copies[j - 1, way].wait()
            self.copies[j, way].start()

    def arrived(self):
        for j in (2 * self.far - 2, 2 * self.far - 1)[0 if self.eager else 1 :]:
            for way in (0, 1):
                self.copies[j, way].wait()
        return [
            (way, j - 1, self.start(j, way))
            for j in (2 * self.far - 2, 2 * self.far - 1)
            for way in (0, 1)
        ]

    def finish(self, unsent):
        for j in unsent:
            for way in (0, 1):
                self.copies[j, way].sent()


def tiles(rows, size, step):
    def body(i, carry):
        step(pl.ds(pl.multiple_of(i * size, size), size))
        return carry

    lax.fori_loop(0, rows // size, body, 0)


def nt(left, right):
    return lax.dot_general(left, right, (((1,), (1,)), ((), ())), preferred_element_type=f32)


def spans(total, size):
    return [(at, min(size, total - at)) for at in range(0, total, size)]


class Sizes:
    def __init__(self, **sizes):
        self.__dict__.update(sizes)


class Work:
    def __init__(self, sizes, expert, bufs):
        self.sizes, self.expert = sizes, expert
        self.__dict__.update(bufs)

    def place(self, s, ids):
        z = self.sizes
        named = jnp.max(jnp.where(ids == self.expert, 1.0, 0.0), axis=0, keepdims=True)
        named = jnp.concatenate([named, jnp.zeros((7, z.seq), f32)], axis=0).astype(bf16)
        along = nt(named, self.ranker[...]) - 1024.0
        down = nt(self.ranker[...], named) - 1024.0
        slots = lax.broadcasted_iota(jnp.int32, (z.capacity, z.seq), 0).astype(f32)
        self.pick[s] = jnp.where(along[0:1, :] == slots, 1.0, 0.0).astype(bf16)
        slots = lax.broadcasted_iota(jnp.int32, (z.seq, z.capacity), 1).astype(f32)
        self.put[s] = jnp.where(down[:, 0:1] == slots, 1.0, 0.0).astype(bf16)

    def rows_of(self, s):
        return pl.ds(s * self.sizes.capacity, self.sizes.capacity)

    def tokens_of(self, s):
        return pl.ds(s * self.sizes.seq, self.sizes.seq)

    def take(self):
        z = self.sizes

        def step(cols):
            for s in range(2):
                picked = matmul(self.pick[s], self.tokens[self.tokens_of(s), cols])
                self.rows[self.rows_of(s), cols] = picked.astype(bf16)
                picked = matmul(self.pick[s], self.grads[self.tokens_of(s), cols])
                self.row_grads[self.rows_of(s), cols] = picked.astype(bf16)

        tiles(z.width, 256, step)

    def routed(self, small):
        z = self.sizes
        rows = self.rows[...]
        logits = matmul(rows, self.router[...])
        lanes = lax.broadcasted_iota(jnp.int32, logits.shape, 1)
        logits = jnp.where(lanes < z.experts, logits, -1e30)
        weights = jnp.exp(logits - jnp.max(logits, axis=1, keepdims=True))
        mine = jnp.sum(jnp.where(lanes == self.expert, weights, 0.0), axis=1, keepdims=True)
        gate = mine / jnp.sum(weights, axis=1, keepdims=True)
        d_gate = jnp.zeros_like(gate)
        for at, size in spans(z.ff, 256):
            a = nt(self.rows[...], self.w_in[pl.ds(at, size), :])
            b = nt(self.rows[...], self.w_in[pl.ds(z.ff + at, size), :])
            u = nt(self.row_grads[...], self.w_out[pl.ds(at, size), :])
            cols = pl.ds(at, size)
            sigma = 1.0 / (1.0 + jnp.exp(-a))
            silu = a * sigma
            hidden = (silu * b).astype(bf16).astype(f32)
            d_gate = d_gate + jnp.sum(hidden * u, axis=1, keepdims=True)
            self.gated[:, cols] = (hidden * gate).astype(bf16)
            d_hidden = u * gate
            self.d_a[:, cols] = (d_hidden * b * sigma * (1.0 + a * (1.0 - sigma))).astype(bf16)
            self.d_b[:, cols] = (d_hidden * silu).astype(bf16)
        for s in range(2):
            mine = d_gate[s * z.capacity : (s + 1) * z.capacity]
            small[s][pl.ds(0, 1), :] = jnp.sum(
                jnp.where(self.pick[s].astype(f32) > 0.5, mine, 0.0), axis=0, keepdims=True
            )

        def step(cols):
            back = matmul(self.d_a[...], self.w_in[pl.ds(0, z.ff), cols])
            back = back + matmul(self.d_b[...], self.w_in[pl.ds(z.ff, z.ff), cols])
            self.d_rows[:, cols] = back.astype(bf16)

        tiles(z.width, 256, step)

    def shared(self, small):
        z = self.sizes
        for s in range(2):
            at = self.tokens_of(s)
            tokens = self.tokens[at, :]
            logits = matmul(tokens, self.router[...])
            lanes = lax.broadcasted_iota(jnp.int32, logits.shape, 1)
            logit = jnp.sum(jnp.where(lanes == z.experts, logits, 0.0), axis=1, keepdims=True)
            sig = 1.0 / (1.0 + jnp.exp(-logit))
            both = matmul(tokens, self.s_in[...])
            a, b = both[:, : z.units], both[:, z.units :]
            u = nt(self.grads[at, :], self.s_out[...])
            sigma = 1.0 / (1.0 + jnp.exp(-a))
            silu = a * sigma
            hidden = (silu * b).astype(bf16).astype(f32)
            d_sig = lax.dot_general(
                jnp.ones((8, z.units), f32),
                hidden * u,
                (((1,), (1,)), ((), ())),
                precision=lax.Precision.HIGHEST,
                preferred_element_type=f32,
            )
            small[s][pl.ds(1, 1), :] = d_sig[0:1]
            self.s_gated[at, :] = (hidden * sig).astype(bf16)
            d_hidden = u * sig
            d_a = d_hidden * b * sigma * (1.0 + a * (1.0 - sigma))
            self.s_d_both[at, : z.units] = d_a.astype(bf16)
            self.s_d_both[at, z.units :] = (d_hidden * silu).astype(bf16)

    def give(self):
        z = self.sizes

        def step(cols):
            self.out_rows[...] = matmul(self.gated[...], self.w_out[:, cols]).astype(bf16)
            out = matmul(self.s_gated[...], self.s_out[:, cols])
            back = nt(self.s_d_both[...], self.s_in[cols, :])
            for s in range(2):
                at = slice(s * z.seq, (s + 1) * z.seq)
                mine = out[at] + matmul(self.put[s], self.out_rows[self.rows_of(s), :])
                self.out[self.tokens_of(s), cols] = mine.astype(bf16)
                mine = back[at] + matmul(self.put[s], self.d_rows[self.rows_of(s), cols])
                self.d_in[self.tokens_of(s), cols] = mine.astype(bf16)

        tiles(z.width, 256, step)


def experts_kernel(z, names, *refs):
    r = Sizes(**dict(zip(names, refs)))
    groups, lanes = z.groups, z.lanes
    peers = Peers(groups, lanes)
    far, bits = peers.far, peers.chip_bits()
    seq = z.seq
    half, piece = seq // 2, seq // lanes
    core = peers.core
    own = core * half
    half_rows = pl.ds(pl.multiple_of(own, half), half)
    other_rows = pl.ds(pl.multiple_of(half - own, half), half)
    first = pl.multiple_of((core * peers.chips + peers.chip) * piece, piece)
    me = peers.group
    others = [k for k in peers.offsets() if k != 0]
    step_of = {k: 2 * k - 1 if k > 0 else -2 * k for k in peers.offsets()}
    slot = {k: peers.group_at(k) for k in range(-far, far + 1)}
    ahead, behind = peers.at(1), peers.at(-1)
    core_peer = peers.other_core()
    chip_peer = {b: peers.other_chip(b) for b in bits}
    peers.meet([peers.at(k) for k in others] + [core_peer] + [chip_peer[b] for b in bits])
    copies = Copies(r.send_sems, r.recv_sems)

    def local(source, target, number):
        return pltpu.make_async_copy(source, target, r.local_sems.at[number])

    def remote(source, target, send_sem, recv_sem, peer):
        return pltpu.make_async_remote_copy(
            src_ref=source,
            dst_ref=target,
            send_sem=send_sem,
            recv_sem=recv_sem,
            device_id=peer,
            device_id_type=pl.DeviceIdType.MESH,
        )

    ff_own = z.ff // 2
    mine_at = pl.multiple_of(core * ff_own, 16)
    theirs_at = pl.multiple_of((1 - core) * ff_own, 16)
    weights, traded = [], []
    for number, (source, target, base) in enumerate(
        [(r.gate, r.w_in, 0), (r.up, r.w_in, z.ff), (r.down, r.w_out, 0)]
    ):
        rows = pl.ds(base + mine_at, ff_own)
        weights.append(local(source.at[core], target.at[rows], number))
        traded.append(
            copies.plan(
                source.at[1 - core],
                target.at[rows],
                core_peer,
                target.at[pl.ds(base + theirs_at, ff_own)],
            )
        )
    weights += [
        local(r.s_in_hbm, r.s_in, 3),
        local(r.s_out_hbm, r.s_out, 4),
        local(r.router_hbm, r.router, 5),
    ]
    own_part = local(r.part.at[half_rows], r.total, 6)
    own_grad = local(r.grad, r.grads_all.at[me], 7)
    own_tokens = local(r.normed, r.tokens_all.at[me, half_rows], 8)
    own_hidden = local(r.hidden.at[half_rows], r.stage.at[0], 9)
    keep_resid = local(r.wide, r.resid, 10)

    def hop(array, k, start, size, source=None):
        held = slot[k + 1] if k < 0 else slot[k - 1]
        rows = pl.ds(pl.multiple_of(start, size), size)
        return copies.plan(
            array.at[held, rows] if source is None else source,
            array.at[held, rows],
            ahead if k < 0 else behind,
            array.at[slot[k], rows],
        )

    def chip_swap(array, k, bit):
        size = bit * piece
        start = (core * peers.chips + lax.div(peers.chip, bit) * bit) * piece
        theirs = (core * peers.chips + lax.div(flip_bit(peers.chip, bit), bit) * bit) * piece
        rows = pl.ds(pl.multiple_of(start, size), size)
        arriving = pl.ds(pl.multiple_of(theirs, size), size)
        return copies.plan(
            array.at[slot[k], rows],
            array.at[slot[k], rows],
            chip_peer[bit],
            array.at[slot[k], arriving],
        )

    def core_swap(array, k, source=None):
        return copies.plan(
            array.at[slot[k], half_rows] if source is None else source,
            array.at[slot[k], half_rows],
            core_peer,
            array.at[slot[k], other_rows],
        )

    signed = [s * k for k in range(1, far) for s in (-1, 1)]
    ids_got = [
        copies.plan(r.ids, r.ids_all.at[me], peers.at(k), r.ids_all.at[slot[-k]]) for k in others
    ]
    own_piece = r.grad.at[pl.ds(first, piece)]
    g_ring = {
        k: hop(r.grads_all, k, first, piece, own_piece if abs(k) == 1 else None) for k in signed
    }
    g_ring[-far] = hop(r.grads_all, -far, first, piece // 2)
    g_ring[far] = hop(r.grads_all, far, first + piece // 2, piece // 2)
    x_ring = {
        k: hop(r.tokens_all, k, own, half, r.normed if abs(k) == 1 else None) for k in signed
    }
    x_ring[-far] = hop(r.tokens_all, -far, own, half // 2)
    x_ring[far] = hop(r.tokens_all, far, own + half // 2, half // 2)
    g_chip = {k: [chip_swap(r.grads_all, k, b) for b in bits] for k in others}
    g_core = {k: core_swap(r.grads_all, k) for k in others}
    x_core = {
        k: core_swap(r.tokens_all, k, r.normed if k == 0 else None) for k in peers.offsets()
    }
    part_core = copies.plan(r.part.at[other_rows], r.from_core, core_peer)
    part_chip = [
        copies.plan(r.total, r.part_chip.at[i], chip_peer[b], ends=False)
        for i, b in enumerate(bits)
    ]

    d_ring = RingSum(
        copies, peers, r.stage, r.from_ring, half,
        lambda k, way: k % 2 + (2 * way if abs(k) < far else 0), eager=True,
    )
    y_ring = RingSum(
        copies, peers, r.stage, r.y_early, half,
        lambda k, way: k % 2 + (2 * way if abs(k) < far else 0), last=2,
    )
    home_chip = [
        copies.plan(r.total, r.from_chip.at[i], chip_peer[b], ends=False)
        for i, b in enumerate(bits)
    ]
    small_peers = [core_peer] + [chip_peer[b] for b in bits]
    small_swaps = [
        copies.plan(r.small_swap.at[2 * i], r.small_swap.at[2 * i + 1], peer)
        for i, peer in enumerate(small_peers)
    ]

    part_core.start()
    own_part.start()
    own_hidden.start()
    g_ring[-1].start()
    g_ring[1].start()
    for copy in ids_got:
        copy.start()
    r.ids_all[me] = r.ids[...]
    for copy in weights + traded:
        copy.start()
    own_grad.start()
    token = lax.broadcasted_iota(jnp.int32, (seq, seq), 0)
    other = lax.broadcasted_iota(jnp.int32, (seq, seq), 1)
    ranks = jnp.where(other < token, 1.0, jnp.where(other == token, 1024.0, 0.0))
    r.ranker[...] = ranks.astype(bf16)

    own_part.wait()
    part_core.wait()

    def add_core(rows):
        both = r.total[rows, :].astype(f32) + r.from_core[rows, :].astype(f32)
        r.total[rows, :] = both.astype(bf16)

    tiles(half, 32, add_core)
    part_chip[0].start()
    own_hidden.wait()
    for k in range(2, far):
        for s in (-1, 1):
            g_ring[s * (k - 1)].wait()
            g_ring[s * k].start()
        if k != 2:
            continue
        for i, bit in enumerate(bits):
            part_chip[i].wait()
            part_chip[i].sent()

            def add_chip(rows, i=i):
                both = r.total[rows, :].astype(f32) + r.part_chip[i, rows, :].astype(f32)
                if i + 1 < len(bits):
                    r.total[rows, :] = both.astype(bf16)
                    return
                both = r.stage[0, rows, :].astype(f32) + both
                r.wide[rows, :] = both
                r.normed[rows, :] = (both * rms_scale(both) * r.gain[...]).astype(bf16)

            tiles(half, 32, add_chip)
            if i + 1 < len(bits):
                part_chip[i + 1].start()
        x_ring[-1].start()
        x_ring[1].start()
        x_core[0].start()
        own_tokens.start()
        keep_resid.start()
    for k in signed[:-2]:
        g_chip[k][0].start()
    for copy in ids_got + weights + traded:
        copy.wait()
    own_grad.wait()
    own_tokens.wait()
    keep_resid.wait()

    def finish_grads(ks):
        for k in ks:
            for i in range(len(bits)):
                g_chip[k][i].wait()
                if i + 1 < len(bits):
                    g_chip[k][i + 1].start()
            g_core[k].start()

    def forward(p):
        for q in range(far):

            @pl.when(p == q)
            def _(k=q + 1):
                if k < far:
                    for s in (-1, 1):
                        x_ring[s * k].wait()
                        if k + 1 < far:
                            x_ring[s * (k + 1)].start()
                    if k + 1 == far:
                        x_ring[-far].start()
                        x_ring[far].start()
                    for s in (1, -1):
                        x_core[s * k].start()
                else:
                    x_ring[-far].wait()
                    x_ring[far].wait()
                    x_core[far].start()
                if k == 1:
                    for s in (-1, 1):
                        g_ring[s * (far - 1)].wait()
                        g_ring[s * far].start()
                        g_chip[s * (far - 1)][0].start()
                if k == 2:
                    g_ring[-far].wait()
                    g_ring[far].wait()
                    g_chip[far][0].start()
                finish_grads([k, -k] if k < far else [far])
                x_core[1 - k].wait()
                if k > 1:
                    g_core[1 - k].wait()

    def complete(p):
        for q in range(far):

            @pl.when(p == q)
            def _(k=q + 1):
                x_core[k].wait()
                g_core[k].wait()

    def small_copy(i, peer):
        return remote(
            r.small_out.at[i], r.small_in.at[i], r.small_send.at[i], r.small_recv.at[i], peer
        )

    def given_copy(i, source):
        return remote(source, r.given.at[i], r.give_send.at[i], r.give_recv.at[i], core_peer)

    def y_given_copy(i, source):
        return remote(source, r.y_given.at[i], r.y_send.at[i], r.y_recv.at[i], core_peer)

    def main(tokens, grads, rows, row_grads, d_rows, out_rows, gated, d_a, d_b, s_gated,
             s_d_both, out, d_in, pick, put):
        work = Work(
            z,
            me * 2 + core,
            dict(
                tokens=tokens, grads=grads, rows=rows, row_grads=row_grads, d_rows=d_rows,
                out_rows=out_rows, gated=gated, d_a=d_a, d_b=d_b, s_gated=s_gated,
                s_d_both=s_d_both, out=out, d_in=d_in, pick=pick, put=put, w_in=r.w_in,
                w_out=r.w_out, s_in=r.s_in, s_out=r.s_out, router=r.router, ranker=r.ranker,
            ),
        )

        def leave(p, slots):
            found = []
            for s in range(2):
                i = 2 * p + s
                keep = pl.ds(pl.multiple_of(s * seq + own, half), half)
                give = pl.ds(pl.multiple_of(s * seq + half - own, half), half)
                sent = given_copy(i, d_in.at[give])
                kept = local(d_in.at[keep], r.kept.at[i], 12 + s)
                found += [(kept.start, kept.wait), (sent.start, sent.wait_send)]
                sent = y_given_copy(i, out.at[give])
                found.append((sent.start, sent.wait_send))
                stored = local(out.at[pl.ds(s * seq, seq)], r.outs_all.at[slots[s]], 14 + s)
                found.append((stored.start, stored.wait))
            return found

        def arrivals(p, s):
            slot_now = peers.group_at(p + 1 if s else -p)
            at = pl.ds(s * seq, seq)
            return [
                local(r.tokens_all.at[slot_now], tokens.at[at], s),
                local(r.grads_all.at[slot_now], grads.at[at], 2 + s),
            ]

        def load(p, s):
            @pl.when(p < far)
            def _():
                for copy in arrivals(p, s):
                    copy.start()

        forward(0)
        load(0, 0)
        complete(0)
        load(0, 1)

        def loop(p, carry):
            slots = [peers.group_at(-p), peers.group_at(p + 1)]
            for s in range(2):
                work.place(s, r.ids_all[slots[s]])
            for copy in arrivals(p, 0) + arrivals(p, 1):
                copy.wait()
            at = pl.ds(pl.multiple_of(p * 2 * z.capacity, 2 * z.capacity), 2 * z.capacity)
            saves = [
                local(source, target.at[at], 16 + n)
                for n, (source, target) in enumerate(
                    [
                        (rows, r.rows_all),
                        (row_grads, r.row_grads_all),
                        (gated, r.gated_all),
                        (d_a, r.d_a_all),
                        (d_b, r.d_b_all),
                    ]
                )
            ]
            for s in range(2):
                mine = pl.ds(s * seq, seq)
                saves.append(local(s_gated.at[mine], r.s_gated_all.at[slots[s]], 21 + 2 * s))
                saves.append(local(s_d_both.at[mine], r.s_d_both_all.at[slots[s]], 22 + 2 * s))
            small = [r.small_out.at[2 * p], r.small_out.at[2 * p + 1]]
            work.take()
            for copy in saves[:2]:
                copy.start()
            work.routed(small)
            for copy in saves[2:5]:
                copy.start()
            work.shared(small)
            for copy in saves[5:]:
                copy.start()
            forward(p + 1)
            load(p + 1, 0)
            small_copy(2 * p + 1, (slots[1], peers.lane)).start()

            @pl.when(p > 0)
            def _():
                small_copy(2 * p, (slots[0], peers.lane)).start()
                for _, wait in leave(p - 1, slots):
                    wait()

            work.give()
            for start, _ in leave(p, slots):
                start()
            complete(p + 1)
            load(p + 1, 1)
            for copy in saves:
                copy.wait()
            return carry

        lax.fori_loop(0, far, loop, 0)
        for _, wait in leave(far - 1, [me, me]):
            wait()

    pl.run_scoped(
        main,
        tokens=pltpu.VMEM((2 * seq, z.width), bf16),
        grads=pltpu.VMEM((2 * seq, z.width), bf16),
        rows=pltpu.VMEM((2 * z.capacity, z.width), bf16),
        row_grads=pltpu.VMEM((2 * z.capacity, z.width), bf16),
        d_rows=pltpu.VMEM((2 * z.capacity, z.width), bf16),
        out_rows=pltpu.VMEM((2 * z.capacity, 256), bf16),
        gated=pltpu.VMEM((2 * z.capacity, z.ff), bf16),
        d_a=pltpu.VMEM((2 * z.capacity, z.ff), bf16),
        d_b=pltpu.VMEM((2 * z.capacity, z.ff), bf16),
        s_gated=pltpu.VMEM((2 * seq, z.units), bf16),
        s_d_both=pltpu.VMEM((2 * seq, 2 * z.units), bf16),
        out=pltpu.VMEM((2 * seq, z.width), bf16),
        d_in=pltpu.VMEM((2 * seq, z.width), bf16),
        pick=pltpu.VMEM((2, z.capacity, seq), bf16),
        put=pltpu.VMEM((2, seq, z.capacity), bf16),
    )

    def fetch(k, place, core_place):
        i = step_of[k]
        given_copy(i, r.given.at[i]).wait_recv()
        loads = [
            local(r.kept.at[i], r.stage.at[place], 0),
            local(r.given.at[i], r.stage_core.at[core_place], 1),
        ]
        for copy in loads:
            copy.start()
        for copy in loads:
            copy.wait()

    def prepare(k, way):
        fetch(k, d_ring.places(k, way), way)

    def merge(place, core_place, start, size, before):
        if before is not None:
            copy = local(r.from_ring.at[before], r.stage_ring.at[core_place], 2)
            copy.start()
            copy.wait()

        def step(rows):
            at = pl.ds(start + rows.start, rows.size)
            value = r.stage[place, at, :].astype(f32) + r.stage_core[core_place, at, :].astype(f32)
            if before is not None:
                value = value + r.stage_ring[core_place, rows, :].astype(f32)
            r.stage[place, at, :] = value.astype(bf16)

        tiles(size, 32, step)

    def ring_step(j):
        d_ring.step(j, prepare, merge)

    ring_step(1)
    ring_step(2)

    features = z.width // groups

    def columns_of(t):
        return pl.ds(pl.multiple_of(t * features, features), features)

    def routed_grads(gated, d_a, d_b, rows, row_grads, wide_in, wide_out):
        whole_loads = [
            local(r.gated_all, gated, 4),
            local(r.d_a_all, d_a, 5),
            local(r.d_b_all, d_b, 6),
        ]

        def loads(t):
            odd = lax.rem(t, 2)
            cols = columns_of(t)
            return [
                local(r.rows_all.at[:, cols], rows.at[odd], 7 + odd),
                local(r.row_grads_all.at[:, cols], row_grads.at[odd], 9 + odd),
            ]

        def stores(t):
            odd = lax.rem(t, 2)
            cols = columns_of(t)
            found = []
            for n, (source, base, target) in enumerate(
                [
                    (wide_in, 0, r.g_gate),
                    (wide_in, z.ff, r.g_up),
                    (wide_out, 0, r.g_down),
                ]
            ):
                here = source.at[odd, pl.ds(base + mine_at, ff_own)]
                there = source.at[odd, pl.ds(base + theirs_at, ff_own)]
                kept = local(here, target.at[core, :, cols], 11 + 2 * n + odd)
                sent = remote(
                    there,
                    target.at[core, :, cols],
                    r.grad_send.at[2 * n + odd],
                    r.grad_recv.at[n * groups + t],
                    core_peer,
                )
                found.append((kept, sent))
            return found

        def settle(t):
            for kept, sent in stores(t):
                kept.wait()
                sent.wait_send()

        def unit(t, carry):
            odd = lax.rem(t, 2)

            @pl.when(t + 1 < groups)
            def _():
                for copy in loads(t + 1):
                    copy.start()

            for copy in loads(t):
                copy.wait()

            @pl.when(t >= 2)
            def _():
                settle(t - 2)

            wide_in[odd, pl.ds(0, z.ff), :] = contract_rows(d_a[...], rows[odd]).astype(bf16)
            wide_in[odd, pl.ds(z.ff, z.ff), :] = contract_rows(d_b[...], rows[odd]).astype(bf16)
            wide_out[odd] = contract_rows(gated[...], row_grads[odd]).astype(bf16)
            for kept, sent in stores(t):
                kept.start()
                sent.start()
            return carry

        for copy in whole_loads + loads(0):
            copy.start()
        for copy in whole_loads:
            copy.wait()
        for n in range(3):
            lax.fori_loop(groups * n // 3, groups * (n + 1) // 3, unit, 0)
            if n < 2:
                ring_step(3 + n)
        settle(groups - 2)
        settle(groups - 1)

    tile_rows = groups * z.capacity
    pl.run_scoped(
        routed_grads,
        gated=pltpu.VMEM((tile_rows, z.ff), bf16),
        d_a=pltpu.VMEM((tile_rows, z.ff), bf16),
        d_b=pltpu.VMEM((tile_rows, z.ff), bf16),
        rows=pltpu.VMEM((2, tile_rows, features), bf16),
        row_grads=pltpu.VMEM((2, tile_rows, features), bf16),
        wide_in=pltpu.VMEM((2, 2 * z.ff, features), bf16),
        wide_out=pltpu.VMEM((2, z.ff, features), bf16),
    )

    def shared_grads(s_gated, s_d_both, tokens, grads, wide):
        whole_loads = [local(r.s_gated_all, s_gated, 4), local(r.s_d_both_all, s_d_both, 5)]

        def loads(t):
            odd = lax.rem(t, 2)
            cols = columns_of(t)
            return [
                local(r.tokens_all.at[:, :, cols], tokens.at[odd], 7 + odd),
                local(r.grads_all.at[:, :, cols], grads.at[odd], 9 + odd),
            ]

        def store(t):
            odd = lax.rem(t, 2)
            return local(wide.at[odd], r.s_grads.at[t], 11 + odd)

        def flat(array):
            return array.reshape(groups * seq, array.shape[-1])

        def unit(t, carry):
            odd = lax.rem(t, 2)

            @pl.when(t + 1 < groups)
            def _():
                for copy in loads(t + 1):
                    copy.start()

            for copy in loads(t):
                copy.wait()

            @pl.when(t >= 2)
            def _():
                store(t - 2).wait()

            both = contract_rows(flat(s_d_both[...]), flat(tokens[odd]))
            out = contract_rows(flat(s_gated[...]), flat(grads[odd]))
            used = z.units_used
            for n, part in enumerate((both[:used], both[z.units : z.units + used], out[:used])):
                wide[odd, pl.ds(n * used, used), :] = part.astype(bf16)
            store(t).start()
            return carry

        for copy in whole_loads + loads(0):
            copy.start()
        for copy in whole_loads:
            copy.wait()
        todo = list(range(5, 2 * far))
        for n, j in enumerate(todo):
            ring_step(j)
            lax.fori_loop(groups * n // len(todo), groups * (n + 1) // len(todo), unit, 0)
        store(groups - 2).wait()
        store(groups - 1).wait()

    pl.run_scoped(
        shared_grads,
        s_gated=pltpu.VMEM((groups, seq, z.units), bf16),
        s_d_both=pltpu.VMEM((groups, seq, 2 * z.units), bf16),
        tokens=pltpu.VMEM((2, groups, seq, features), bf16),
        grads=pltpu.VMEM((2, groups, seq, features), bf16),
        wide=pltpu.VMEM((2, 3 * z.units_used, features), bf16),
    )
    d_ring.finish(range(2 * far - 4, 2 * far - 2))
    fetch(0, 0, 0)

    r.small_total[...] = jnp.zeros_like(r.small_total)
    d_sig = r.small_out[0, pl.ds(1, 1), :]
    r.small_total[pl.ds(me * 2 + core, 1), :] = r.small_out[0, pl.ds(0, 1), :]
    for k in others:
        i = step_of[k]
        copy = small_copy(i, peers.at(k))
        copy.wait_recv()
        copy.wait_send()
        d_sig = d_sig + r.small_in[i, pl.ds(1, 1), :]
        r.small_total[pl.ds(slot[-k] * 2 + core, 1), :] = r.small_in[i, pl.ds(0, 1), :]
    r.small_total[pl.ds(z.experts, 1), :] = d_sig
    for i, copy in enumerate(small_swaps):
        r.small_swap[2 * i] = r.small_total[...]
        copy.start()
        copy.wait()
        r.small_total[...] = r.small_swap[2 * i] + r.small_swap[2 * i + 1]

    for n, target in enumerate((r.g_gate, r.g_up, r.g_down)):
        for t in range(groups):
            arriving = target.at[1 - core, :, columns_of(t)]
            remote(
                arriving, arriving, r.grad_send.at[0], r.grad_recv.at[n * groups + t], core_peer
            ).wait_recv()

    def last(way, index, start):
        copy = local(r.from_ring.at[way, index], r.stage_ring.at[0], 2)
        copy.start()
        copy.wait()

        def step(rows):
            at = pl.ds(start + rows.start, rows.size)
            value = r.wide[at, :] + r.stage_ring[0, rows, :].astype(f32)
            r.wide[at, :] = value
            r.total[at, :] = value.astype(bf16)

        tiles(half // 2, 32, step)

    def first_of_home(rows):
        both = r.stage[0, rows, :].astype(f32) + r.stage_core[0, rows, :].astype(f32)
        r.wide[rows, :] = both

    tiles(half, 32, first_of_home)
    for chunk in d_ring.arrived():
        last(*chunk)
    d_ring.finish(range(2 * far - 2, 2 * far))

    def y_prepare(k, way):
        loads = [
            local(r.outs_all.at[slot[k], half_rows], r.stage.at[y_ring.places(k, way)], 0),
            local(r.y_given.at[step_of[k]], r.stage_core.at[way], 1),
        ]
        for copy in loads:
            copy.start()
        for copy in loads:
            copy.wait()

    home_chip[0].start()
    for k in peers.offsets():
        i = step_of[k]
        y_given_copy(i, r.y_given.at[i]).wait_recv()
    y_ring.step(1, y_prepare, merge)
    y_ring.step(2, y_prepare, merge)
    for i, copy in enumerate(home_chip):
        if i > 0:
            copy.start()
        copy.wait()
        copy.sent()

        def join(rows, i=i):
            value = r.total[rows, :].astype(f32) + r.from_chip[i, rows, :].astype(f32)
            if i + 1 < len(bits):
                r.total[rows, :] = value.astype(bf16)
            else:
                r.wide[rows, :] = value

        tiles(half, 32, join)
    keep_total = local(r.wide, r.d_total, 0)
    keep_total.start()
    for way in (0, 1):
        y_ring.copies[2, way].wait()
    y_ring.finish((1, 2))
    copies.finish()
    keep_total.wait()


def pad_last(array, size):
    return jnp.pad(array, [(0, 0)] * (array.ndim - 1) + [(0, size - array.shape[-1])])


def round_up(value, unit):
    return -(-value // unit) * unit


def run_experts(groups, lanes, part, hidden, gain, grad, ids, weights, router, capacity):
    gate, up, down, s_gate, s_up, s_down = weights
    seq, width = grad.shape
    ff_own = gate.shape[1]
    units_true = s_gate.shape[1]
    experts = router.shape[1] - 1
    ff, units = 2 * ff_own, round_up(units_true, 128)
    half = seq // 2
    bits = (lanes // 2).bit_length() - 1
    far = groups // 2
    small_rows = round_up(experts + 1, 8)
    z = Sizes(
        groups=groups, lanes=lanes, seq=seq, width=width, ff=ff, units=units,
        capacity=capacity, experts=experts, units_used=round_up(units_true, 16),
    )
    s_in = jnp.concatenate([pad_last(s_gate, units), pad_last(s_up, units)], axis=1)
    s_out = jnp.pad(s_down, ((0, units - units_true), (0, 0)))
    router = pad_last(router, 128)
    ins = dict(
        part=(part, in_place), hidden=(hidden, in_place), gain=(gain, whole),
        grad=(grad, in_place), ids=(ids, whole), gate=(gate, in_place),
        up=(up, in_place), down=(down, in_place), s_in_hbm=(s_in, in_place),
        s_out_hbm=(s_out, in_place), router_hbm=(router, in_place),
    )
    rows_all = groups * capacity
    outs = dict(
        normed=((half, width), bf16, whole),
        small_total=((small_rows, seq), f32, whole),
        resid=((half, width), f32, in_place),
        d_total=((half, width), f32, in_place),
        outs_all=((groups, seq, width), bf16, in_place),
        g_gate=(gate.shape, bf16, in_place),
        g_up=(up.shape, bf16, in_place),
        g_down=(down.shape, bf16, in_place),
        s_grads=((groups, 3 * z.units_used, width // groups), bf16, in_place),
        tokens_all=((groups, seq, width), bf16, in_place),
        grads_all=((groups, seq, width), bf16, in_place),
        rows_all=((rows_all, width), bf16, in_place),
        row_grads_all=((rows_all, width), bf16, in_place),
        gated_all=((rows_all, ff), bf16, in_place),
        d_a_all=((rows_all, ff), bf16, in_place),
        d_b_all=((rows_all, ff), bf16, in_place),
        s_gated_all=((groups, seq, units), bf16, in_place),
        s_d_both_all=((groups, seq, 2 * units), bf16, in_place),
        kept=((groups, half, width), bf16, in_place),
        given=((groups, half, width), bf16, in_place),
        y_given=((groups, half, width), bf16, in_place),
        y_early=((2, 2, half // 2, width), bf16, in_place),
        from_ring=((2, 2 * far - 1, half // 2, width), bf16, in_place),
    )
    copies = 4 + 3 + 2 * groups + (groups - 1) * (2 + bits) + groups + 1 + bits + 4 * far
    copies += 2 * bits + 1
    scratch = dict(
        ids_all=pltpu.VMEM((groups,) + ids.shape, jnp.int32),
        total=pltpu.VMEM((half, width), bf16),
        from_core=pltpu.VMEM((half, width), bf16),
        part_chip=pltpu.VMEM((max(bits, 1), half, width), bf16),
        from_chip=pltpu.VMEM((max(bits, 1), half, width), bf16),
        wide=pltpu.VMEM((half, width), f32),
        stage=pltpu.VMEM((4, half, width), bf16),
        stage_core=pltpu.VMEM((2, half, width), bf16),
        stage_ring=pltpu.VMEM((2, half // 2, width), bf16),
        small_out=pltpu.VMEM((groups, 8, seq), f32),
        small_in=pltpu.VMEM((groups, 8, seq), f32),
        small_swap=pltpu.VMEM((2 * (1 + bits), small_rows, seq), f32),
        ranker=pltpu.VMEM((seq, seq), bf16),
        w_in=pltpu.VMEM((2 * ff, width), bf16),
        w_out=pltpu.VMEM((ff, width), bf16),
        s_in=pltpu.VMEM(s_in.shape, bf16),
        s_out=pltpu.VMEM(s_out.shape, bf16),
        router=pltpu.VMEM(router.shape, bf16),
        send_sems=pltpu.SemaphoreType.DMA((copies,)),
        recv_sems=pltpu.SemaphoreType.DMA((copies,)),
        local_sems=pltpu.SemaphoreType.DMA((25,)),
        give_send=pltpu.SemaphoreType.DMA((groups,)),
        give_recv=pltpu.SemaphoreType.DMA((groups,)),
        y_send=pltpu.SemaphoreType.DMA((groups,)),
        y_recv=pltpu.SemaphoreType.DMA((groups,)),
        small_send=pltpu.SemaphoreType.DMA((groups,)),
        small_recv=pltpu.SemaphoreType.DMA((groups,)),
        grad_send=pltpu.SemaphoreType.DMA((6,)),
        grad_recv=pltpu.SemaphoreType.DMA((3 * groups,)),
    )
    names = list(ins) + list(outs) + list(scratch)
    results = pl.pallas_call(
        functools.partial(experts_kernel, z, names),
        out_shape=tuple(jax.ShapeDtypeStruct(s, d) for s, d, _ in outs.values()),
        in_specs=[spec for _, spec in ins.values()],
        out_specs=tuple(spec for _, _, spec in outs.values()),
        scratch_shapes=list(scratch.values()),
        compiler_params=pltpu.CompilerParams(
            collective_id=0, has_side_effects=True, vmem_limit_bytes=63 * 1024 * 1024
        ),
        name="run_experts",
    )(*[array for array, _ in ins.values()])
    return Sizes(**dict(zip(outs, results)), units=z.units_used)


def finish_kernel(z, names, *refs):
    r = Sizes(**dict(zip(names, refs)))
    groups, lanes = z.groups, z.lanes
    peers = Peers(groups, lanes)
    far, bits = peers.far, peers.chip_bits()
    seq, heads, head, features = z.seq, z.heads, z.head, z.features
    head_all = heads * head
    half = seq // 2
    own = peers.core * half
    half_rows = pl.ds(pl.multiple_of(own, half), half)
    other_rows = pl.ds(pl.multiple_of(half - own, half), half)
    me = peers.group
    others = [k for k in peers.offsets() if k != 0]
    step_of = {k: 2 * k - 1 if k > 0 else -2 * k for k in peers.offsets()}
    slot = {k: peers.group_at(k) for k in range(-far, far + 1)}
    ahead, behind = peers.at(1), peers.at(-1)
    core_peer = peers.other_core()
    chip_peer = {b: peers.other_chip(b) for b in bits}
    peers.meet([peers.at(k) for k in others] + [core_peer] + [chip_peer[b] for b in bits])
    copies = Copies(r.send_sems, r.recv_sems)

    def local(source, target, number):
        return pltpu.make_async_copy(source, target, r.local_sems.at[number])

    attn_core = copies.plan(
        r.d_attn_half, r.d_attn.at[half_rows], core_peer, r.d_attn.at[other_rows]
    )
    own_attn = local(r.d_attn_half, r.d_attn.at[half_rows], 0)

    y_ring = RingSum(
        copies, peers, r.stage, r.from_ring, half,
        lambda k, way: k % 2 + (2 * way if abs(k) < far else 0), first=3, eager=True,
    )
    w_ring = RingSum(
        copies, peers, r.w_parts, r.w_received, features, lambda k, way: step_of[k], eager=True
    )
    y_chip = [
        copies.plan(r.total, r.from_chip.at[i], chip_peer[b], ends=False)
        for i, b in enumerate(bits)
    ]
    layer_core = copies.plan(
        r.layer_half, r.layer_out.at[half_rows], core_peer, r.layer_out.at[other_rows]
    )
    norm_core = copies.plan(r.d_norm.at[other_rows], r.norm_core, core_peer)
    norm_chip = [
        copies.plan(r.norm_total, r.norm_chip.at[i], chip_peer[b], ends=False)
        for i, b in enumerate(bits)
    ]
    in_core = copies.plan(
        r.in_half, r.grad_in.at[half_rows], core_peer, r.grad_in.at[other_rows]
    )
    small_got = {
        k: copies.plan(r.small_out.at[slot[k]], r.small_in.at[step_of[k]], peers.at(k))
        for k in others
    }
    small_peers = [core_peer] + [chip_peer[b] for b in bits]
    small_swaps = [
        copies.plan(r.small_swap.at[2 * i], r.small_swap.at[2 * i + 1], peer)
        for i, peer in enumerate(small_peers)
    ]

    own_attn.start()
    attn_core.start()

    def fetch(k, place, core_place):
        loads = [
            local(r.outs_all.at[slot[k], half_rows], r.stage.at[place], 1),
            local(r.y_given.at[step_of[k]], r.stage_core.at[core_place], 2),
        ]
        for copy in loads:
            copy.start()
        for copy in loads:
            copy.wait()

    def y_merge(place, core_place, start, size, before):
        if before is not None:
            received = r.y_early if before[1] < 2 else r.from_ring
            copy = local(received.at[before], r.stage_ring.at[core_place], 3)
            copy.start()
            copy.wait()

        def step(rows):
            at = pl.ds(start + rows.start, rows.size)
            value = r.stage[place, at, :].astype(f32) + r.stage_core[core_place, at, :].astype(f32)
            if before is not None:
                value = value + r.stage_ring[core_place, rows, :].astype(f32)
            r.stage[place, at, :] = value.astype(bf16)

        tiles(size, 32, step)

    def y_step(j):
        y_ring.step(j, lambda k, way: fetch(k, y_ring.places(k, way), way), y_merge)

    def w_merge(place, core_place, start, size, before):
        if before is None:
            return

        def step(rows):
            at = pl.ds(start + rows.start, rows.size)
            value = r.w_parts[place, at, :].astype(f32)
            value = value + r.w_received[before[0], before[1], rows, :].astype(f32)
            r.w_parts[place, at, :] = value.astype(bf16)

        tiles(size, 32, step)

    def w_step(j):
        w_ring.step(j, lambda k, way: None, w_merge)

    y_step(3)
    y_step(4)

    def scales(rows):
        scale = rms_scale(r.hidden[rows, :].astype(f32))
        r.scale[rows, :] = jnp.broadcast_to(scale, (scale.shape[0], 128))

    tiles(seq, 64, scales)
    own_attn.wait()
    attn_core.wait()
    query_at = lax.broadcasted_iota(jnp.int32, (seq, seq), 0)
    key_at = lax.broadcasted_iota(jnp.int32, (seq, seq), 1)
    allowed = (key_at <= query_at) & (key_at < r.length[0:1, 0:1])
    r.mask[...] = jnp.where(allowed, 0.0, -1e30)

    def one_head(h, carry):
        query, key, value = r.query[h], r.key[h], r.value[h]
        at = pl.ds(pl.multiple_of(h * head, head), head)
        d_context = nt(r.d_attn[...], r.w_output[at, :]).astype(bf16)
        scores = nt(query, key) * z.score_scale + r.mask[...]
        scores = jnp.exp(scores - jnp.max(scores, axis=1, keepdims=True))
        probs = scores / jnp.sum(scores, axis=1, keepdims=True)
        d_probs = nt(d_context, value)
        row_dot = jnp.sum(probs * d_probs, axis=1, keepdims=True)
        d_scores = (probs * (d_probs - row_dot)).astype(bf16)
        d_query = matmul(d_scores, key) * z.score_scale
        d_key = contract_rows(d_scores, query) * z.score_scale
        d_value = contract_rows(probs.astype(bf16), d_context)

        def unrope(values):
            return values * r.cosine[...] - pltpu.roll(values, head // 2, 1) * r.sine[...]

        for n, values in enumerate((unrope(d_query), unrope(d_key), d_value)):
            cols = pl.ds(pl.multiple_of(n * head_all + h * head, head), head)
            r.d_qkv[:, cols] = values.astype(bf16)
        return carry

    lax.fori_loop(0, heads, one_head, 0)

    def parts(i, carry):
        k = lax.div(i + 1, 2) * (1 - 2 * lax.rem(i + 1, 2))
        cols = pl.ds(pl.multiple_of(peers.group_at(k) * features, features), features)
        part = contract_rows(r.normed[:, cols], r.d_qkv[...])
        r.w_parts[i, :, pl.ds(0, 3 * head_all)] = part.astype(bf16)
        part = contract_rows(r.d_attn[:, cols], r.context[...])
        r.w_parts[i, :, pl.ds(3 * head_all, head_all)] = part.astype(bf16)
        return carry

    lax.fori_loop(0, groups, parts, 0)
    w_step(1)
    w_step(2)

    r.small_out[...] = r.small_start[...]
    bias = jnp.sum(r.d_qkv[...].astype(f32), axis=0, keepdims=True)
    bias_rows = 3 * head_all // features
    gain_row = z.experts + 2

    def back(g, carry):
        cols = pl.ds(pl.multiple_of(g * features, features), features)
        total = nt(r.d_qkv[:, pl.ds(0, head_all)], r.w_query[cols, :])
        total = total + nt(r.d_qkv[:, pl.ds(head_all, head_all)], r.w_key[cols, :])
        total = total + nt(r.d_qkv[:, pl.ds(2 * head_all, head_all)], r.w_value[cols, :])
        r.d_norm[:, cols] = total.astype(bf16)
        scaled = total * (r.hidden[:, cols].astype(f32) * r.scale[:, 0:1])
        r.small_out[g, pl.ds(gain_row, 1), :] = jnp.sum(scaled, axis=0, keepdims=True)
        for i in range(bias_rows):
            row = gain_row + 1 + peers.lane * bias_rows + i
            r.small_out[g, pl.ds(row, 1), :] = bias[:, i * features : (i + 1) * features]
        return carry

    lax.fori_loop(0, groups, back, 0)
    norm_core.start()
    for k in others:
        small_got[k].start()

    norm_core.wait()

    def add_core(rows):
        mine = pl.ds(pl.multiple_of(own + rows.start, rows.size), rows.size)
        both = r.d_norm[mine, :].astype(f32) + r.norm_core[rows, :].astype(f32)
        r.norm_total[rows, :] = both.astype(bf16)

    tiles(half, 32, add_core)
    norm_chip[0].start()
    load_resid = local(r.d_resid, r.wide, 5)
    load_resid.start()

    def norm_finish():
        for i, copy in enumerate(norm_chip):
            copy.wait()
            copy.sent()
            if i + 1 == len(bits):
                load_resid.wait()

            def join(rows, i=i):
                total = r.norm_total[rows, :].astype(f32) + r.norm_chip[i, rows, :].astype(f32)
                if i + 1 < len(bits):
                    r.norm_total[rows, :] = total.astype(bf16)
                    return
                mine = pl.ds(pl.multiple_of(own + rows.start, rows.size), rows.size)
                hidden = r.hidden[mine, :].astype(f32)
                scale = r.scale[mine, 0:1]
                inner = total * r.gain[...]
                mean = jnp.mean(inner * hidden, axis=-1, keepdims=True)
                total = r.wide[rows, :] + scale * inner - hidden * (scale * scale * scale) * mean
                r.in_half[rows, :] = total.astype(bf16)

            tiles(half, 32, join)
            if i + 1 < len(bits):
                norm_chip[i + 1].start()
        in_core.start()
        own_in.start()

    own_in = local(r.in_half, r.grad_in.at[half_rows], 6)
    own_layer = local(r.layer_half, r.layer_out.at[half_rows], 7)
    for j in range(3, 2 * far):
        w_step(j)
        if j + 2 < 2 * far:
            y_step(j + 2)
        if j == 3:
            norm_finish()

    y_ring.finish(range(2 * far - 4, 2 * far - 2))
    fetch(0, 0, 0)

    def first_of_home(rows):
        both = r.stage[0, rows, :].astype(f32) + r.stage_core[0, rows, :].astype(f32)
        r.wide[rows, :] = both

    tiles(half, 32, first_of_home)

    def last(way, index, start):
        copy = local(r.from_ring.at[way, index], r.stage_ring.at[0], 3)
        copy.start()
        copy.wait()

        def step(rows):
            at = pl.ds(start + rows.start, rows.size)
            value = r.wide[at, :] + r.stage_ring[0, rows, :].astype(f32)
            r.wide[at, :] = value
            r.total[at, :] = value.astype(bf16)

        tiles(half // 2, 32, step)

    for chunk in y_ring.arrived():
        last(*chunk)
    y_chip[0].start()
    load_out = local(r.resid, r.wide, 8)
    load_out.start()

    for k in others:
        small_got[k].wait()
    small_sum = r.small_out[me]
    for k in others:
        small_sum = small_sum + r.small_in[step_of[k]]
    r.small_total[...] = small_sum
    for i, copy in enumerate(small_swaps):
        r.small_swap[2 * i] = r.small_total[...]
        copy.start()
        copy.wait()
        r.small_total[...] = r.small_swap[2 * i] + r.small_swap[2 * i + 1]

    arrived = w_ring.arrived()
    size = features // 2
    for start in (0, size):
        found = [(way, index) for way, index, at in arrived if at == start]

        def w_last(rows, start=start, found=found):
            at = pl.ds(start + rows.start, rows.size)
            value = r.w_parts[0, at, :].astype(f32)
            for way, index in found:
                value = value + r.w_received[way, index, rows, :].astype(f32)
            r.w_total[at, :] = value

        tiles(size, 32, w_last)
    load_out.wait()
    for i, copy in enumerate(y_chip):
        copy.wait()
        copy.sent()

        def join(rows, i=i):
            value = r.total[rows, :].astype(f32) + r.from_chip[i, rows, :].astype(f32)
            if i + 1 < len(bits):
                r.total[rows, :] = value.astype(bf16)
            else:
                r.layer_half[rows, :] = (r.wide[rows, :] + value).astype(bf16)

        tiles(half, 32, join)
        if i + 1 < len(bits):
            y_chip[i + 1].start()
    layer_core.start()
    own_layer.start()
    layer_core.wait()
    in_core.wait()
    own_in.wait()
    own_layer.wait()
    y_ring.finish(range(2 * far - 2, 2 * far))
    w_ring.finish(range(2 * far - 4, 2 * far))
    copies.finish()


def finish(groups, lanes, sizes, vmem_ins, hbm_ins):
    z = Sizes(groups=groups, lanes=lanes, **sizes)
    seq, width = z.seq, z.width
    half = seq // 2
    bits = (lanes // 2).bit_length() - 1
    far = groups // 2
    head_all = z.heads * z.head
    outs = dict(
        layer_out=((seq, width), bf16, in_place),
        grad_in=((seq, width), bf16, in_place),
        w_total=((z.features, 4 * head_all), f32, whole),
        small_total=(vmem_ins["small_start"].shape[1:], f32, whole),
        from_ring=((2, 2 * far - 1, half // 2, width), bf16, in_place),
    )
    small_shape = vmem_ins["small_start"].shape
    copies = groups + 1 + 8 * far + 2 * bits + 3 + (groups - 1) + 1 + bits
    scratch = dict(
        d_attn=pltpu.VMEM((seq, width), bf16),
        d_qkv=pltpu.VMEM((seq, 3 * head_all), bf16),
        d_norm=pltpu.VMEM((seq, width), bf16),
        scale=pltpu.VMEM((seq, 128), f32),
        mask=pltpu.VMEM((seq, seq), f32),
        stage=pltpu.VMEM((4, half, width), bf16),
        stage_core=pltpu.VMEM((2, half, width), bf16),
        stage_ring=pltpu.VMEM((2, half // 2, width), bf16),
        total=pltpu.VMEM((half, width), bf16),
        from_chip=pltpu.VMEM((max(bits, 1), half, width), bf16),
        layer_half=pltpu.VMEM((half, width), bf16),
        norm_core=pltpu.VMEM((half, width), bf16),
        norm_total=pltpu.VMEM((half, width), bf16),
        norm_chip=pltpu.VMEM((max(bits, 1), half, width), bf16),
        in_half=pltpu.VMEM((half, width), bf16),
        wide=pltpu.VMEM((half, width), f32),
        w_parts=pltpu.VMEM((groups, z.features, 4 * head_all), bf16),
        w_received=pltpu.VMEM((2, 2 * far - 1, z.features // 2, 4 * head_all), bf16),
        small_out=pltpu.VMEM(small_shape, f32),
        small_in=pltpu.VMEM(small_shape, f32),
        small_swap=pltpu.VMEM((2 * (1 + bits),) + small_shape[1:], f32),
        send_sems=pltpu.SemaphoreType.DMA((copies,)),
        recv_sems=pltpu.SemaphoreType.DMA((copies,)),
        local_sems=pltpu.SemaphoreType.DMA((9,)),
    )
    names = list(vmem_ins) + list(hbm_ins) + list(outs) + list(scratch)
    results = pl.pallas_call(
        functools.partial(finish_kernel, z, names),
        out_shape=tuple(jax.ShapeDtypeStruct(s, d) for s, d, _ in outs.values()),
        in_specs=[whole] * len(vmem_ins) + [in_place] * len(hbm_ins),
        out_specs=tuple(spec for _, _, spec in outs.values()),
        scratch_shapes=list(scratch.values()),
        compiler_params=pltpu.CompilerParams(
            collective_id=1, has_side_effects=True, vmem_limit_bytes=63 * 1024 * 1024
        ),
        name="finish",
    )(*vmem_ins.values(), *hbm_ins.values())
    return Sizes(**dict(zip(outs, results)))


def attend_forward(query, key, value, allowed, score_scale):
    scores = jnp.einsum("qhd,khd->hqk", query, key, preferred_element_type=f32) * score_scale
    scores = jnp.where(allowed[None], scores, -1e30)
    highest = jnp.max(scores, axis=-1, keepdims=True)
    log_total = highest + jnp.log(jnp.sum(jnp.exp(scores - highest), axis=-1, keepdims=True))
    probs = jnp.exp(scores - log_total)
    contexts = jnp.einsum("hqk,khd->qhd", probs.astype(bf16), value, preferred_element_type=f32)
    return contexts.astype(bf16), log_total


def norm_backward(values, scale, gain, d_normed):
    inner = d_normed * gain
    mean = jnp.mean(inner * values, axis=-1, keepdims=True)
    return scale * inner - values * (scale * scale * scale) * mean


def on_device(
    hidden_in,
    seq_lengths,
    expert_ids,
    attn_gain,
    w_query,
    w_key,
    w_value,
    b_query,
    b_key,
    b_value,
    w_output,
    ffn_gain,
    w_router,
    w_sigmoid,
    shared_gate,
    shared_up,
    shared_down,
    expert_gate,
    expert_up,
    expert_down,
    out_grad,
):
    seq, width = hidden_in.shape
    heads, head_width = b_query.shape
    head_all = heads * head_width
    top_count = expert_ids.shape[1]
    experts_all = w_router.shape[1]
    held = expert_gate.shape[0]
    groups = lax.axis_size("expert")
    lane_count = lax.axis_size("tensor")
    group = lax.axis_index("expert")
    lane = lax.axis_index("tensor")
    capacity = 3 * seq * top_count // (2 * experts_all)
    score_scale = 1.0 / math.sqrt(head_width)
    length = seq_lengths[0]
    half = seq // 2
    features = width // groups
    half_start = (lane % 2) * half

    def half_of(array):
        return lax.dynamic_slice_in_dim(array, half_start, half, 0)

    hidden = hidden_in.astype(f32)
    position = jnp.arange(seq, dtype=jnp.int32)
    grad_low = jnp.where((position < length)[:, None], out_grad, jnp.zeros_like(out_grad))

    gain_attn = attn_gain.astype(f32)
    attn_scale = rms_scale(hidden)
    normed_attn = (hidden * attn_scale * gain_attn).astype(bf16)
    freq = jnp.exp(
        jnp.arange(head_width // 2, dtype=f32) * (-2.0 * math.log(rope_base) / head_width)
    )
    angle = position.astype(f32)[:, None] * freq[None, :]
    angle = jnp.concatenate([angle, angle], axis=1)
    cosine, sine = jnp.cos(angle)[:, None, :], jnp.sin(angle)[:, None, :]
    by_head = (seq, heads, head_width)
    query_pre = (matmul(normed_attn, w_query) + b_query.reshape(-1).astype(f32)).reshape(by_head)
    key_pre = (matmul(normed_attn, w_key) + b_key.reshape(-1).astype(f32)).reshape(by_head)
    value_pre = matmul(normed_attn, w_value) + b_value.reshape(-1).astype(f32)
    query = (query_pre * cosine + rotate(query_pre) * sine).astype(bf16)
    key = (key_pre * cosine + rotate(key_pre) * sine).astype(bf16)
    value = value_pre.astype(bf16).reshape(by_head)
    allowed = (position[None, :] <= position[:, None]) & (position[None, :] < length)
    context, log_total = attend_forward(query, key, value, allowed, score_scale)
    context_flat = context.reshape(seq, head_all)
    gain_ffn = ffn_gain.astype(f32)
    ids = jnp.pad(expert_ids.T, ((0, -top_count % 8), (0, 0)), constant_values=-1)
    units = shared_gate.shape[1] // groups
    ex = run_experts(
        groups,
        lane_count,
        matmul(context_flat, w_output).astype(bf16),
        hidden_in,
        gain_ffn[None, :],
        grad_low,
        ids,
        (
            jnp.swapaxes(expert_gate, 1, 2),
            jnp.swapaxes(expert_up, 1, 2),
            expert_down,
            lax.dynamic_slice_in_dim(shared_gate, group * units, units, 1),
            lax.dynamic_slice_in_dim(shared_up, group * units, units, 1),
            lax.dynamic_slice_in_dim(shared_down, group * units, units, 0),
        ),
        jnp.concatenate([w_router, w_sigmoid[:, None]], axis=1),
        capacity,
    )
    resid, normed, outs, d_in_sum, small = (
        ex.resid, ex.normed, ex.outs_all, ex.d_total, ex.small_total
    )
    g_gate = jnp.swapaxes(ex.g_gate, 1, 2).astype(f32)
    g_up = jnp.swapaxes(ex.g_up, 1, 2).astype(f32)
    g_down = ex.g_down.astype(f32)

    ffn_scale = rms_scale(resid)
    logits = matmul(normed, w_router)
    route_probs = jax.nn.softmax(logits, axis=-1)
    sig = jax.nn.sigmoid(jnp.dot(normed, w_sigmoid, preferred_element_type=f32))

    small = half_of(small.T)
    d_probs_route, sig_grad = small[:, :experts_all], small[:, experts_all]
    d_logits = (
        route_probs
        * (d_probs_route - jnp.sum(route_probs * d_probs_route, axis=-1, keepdims=True))
    ).astype(bf16)
    d_sig_logit = (sig_grad * sig * (1.0 - sig)).astype(bf16)
    d_from_gates = (
        times_transposed(d_logits, w_router)
        + d_sig_logit.astype(f32)[:, None] * w_sigmoid.astype(f32)[None, :]
    )
    d_normed = d_in_sum + d_from_gates
    d_resid = half_of(grad_low).astype(f32) + norm_backward(resid, ffn_scale, gain_ffn, d_normed)

    rows = half // (lane_count // 2)
    start = (lane // 2) * rows
    mine = [
        lax.dynamic_slice_in_dim(a, start, rows, 0)
        for a in (d_normed * resid * ffn_scale, normed, d_logits, d_sig_logit[:, None])
    ]
    router_part = contract_rows(jnp.concatenate([mine[2], mine[3]], axis=1), mine[1])
    to_groups = jnp.concatenate([router_part, jnp.sum(mine[0], axis=0)[None]], axis=0)
    to_groups = jnp.swapaxes(to_groups.reshape(-1, groups, features), 0, 1)
    bias_rows = 3 * head_all // features
    small_rows = round_up(experts_all + 3 + lane_count * bias_rows, 8)
    small_start = jnp.pad(to_groups, ((0, 0), (0, small_rows - to_groups.shape[1]), (0, 0)))

    signed_sine = jnp.concatenate([-sine[..., : head_width // 2], sine[..., head_width // 2 :]], -1)
    done = finish(
        groups,
        lane_count,
        dict(
            seq=seq, width=width, heads=heads, head=head_width, features=features,
            experts=experts_all, score_scale=score_scale,
        ),
        dict(
            query=jnp.swapaxes(query, 0, 1),
            key=jnp.swapaxes(key, 0, 1),
            value=jnp.swapaxes(value, 0, 1),
            context=context_flat,
            normed=normed_attn,
            hidden=hidden_in,
            gain=gain_attn[None, :],
            w_output=w_output,
            w_query=w_query,
            w_key=w_key,
            w_value=w_value,
            cosine=cosine[:, 0],
            sine=signed_sine[:, 0],
            length=jnp.broadcast_to(length, (8, 128)),
            small_start=small_start,
        ),
        dict(
            outs_all=outs, y_given=ex.y_given, y_early=ex.y_early,
            d_attn_half=d_resid.astype(bf16), d_resid=d_resid, resid=resid,
        ),
    )
    grads, small, layer_out, grad_in = (
        done.w_total, done.small_total, done.layer_out, done.grad_in
    )
    biases = lax.dynamic_slice_in_dim(
        small, experts_all + 3 + lane * bias_rows, bias_rows, 0
    ).reshape(3, heads, head_width)
    biases = lax.dynamic_slice_in_dim(
        biases, group * (head_width // groups), head_width // groups, 2
    )

    shared = lax.all_to_all(ex.s_grads, "expert", split_axis=0, concat_axis=0, tiled=True)
    shared = shared.reshape(groups, 3, ex.units, features)[:, :, :units].astype(f32)
    shared = jnp.swapaxes(shared, 0, 1).reshape(3, groups * units, features)
    grad_shared_gate, grad_shared_up, grad_shared_down = shared[0].T, shared[1].T, shared[2]
    return (
        layer_out,
        grad_in,
        small[experts_all + 2],
        grads[:, :head_all],
        grads[:, head_all : 2 * head_all],
        grads[:, 2 * head_all : 3 * head_all],
        biases[0],
        biases[1],
        biases[2],
        grads[:, 3 * head_all :].T,
        small[experts_all + 1],
        small[:experts_all].T,
        small[experts_all],
        grad_shared_gate,
        grad_shared_up,
        grad_shared_down,
        g_gate,
        g_up,
        g_down,
    )


def solution(mesh):
    placed = (
        P("expert", None),
        P("expert"),
        P("expert", None),
        P(),
        P(None, "tensor"),
        P(None, "tensor"),
        P(None, "tensor"),
        P("tensor", None),
        P("tensor", None),
        P("tensor", None),
        P("tensor", None),
        P(),
        P(),
        P(),
        P(None, "tensor"),
        P(None, "tensor"),
        P("tensor", None),
        P("expert", None, "tensor"),
        P("expert", None, "tensor"),
        P("expert", "tensor", None),
        P("expert", None),
    )
    return jax.shard_map(
        on_device,
        mesh=mesh,
        in_specs=placed,
        out_specs=(
            P("expert", None),
            P("expert", None),
            P("expert"),
            P("expert", "tensor"),
            P("expert", "tensor"),
            P("expert", "tensor"),
            P("tensor", "expert"),
            P("tensor", "expert"),
            P("tensor", "expert"),
            P("tensor", "expert"),
            P("expert"),
            P("expert", None),
            P("expert"),
            P("expert", "tensor"),
            P("expert", "tensor"),
            P("tensor", "expert"),
            P("expert", None, "tensor"),
            P("expert", None, "tensor"),
            P("expert", "tensor", None),
        ),
        check_vma=False,
    )
```

```python
import functools
import math

import jax
import jax.numpy as jnp
from jax import lax
from jax.experimental import pallas as pl
from jax.experimental.pallas import tpu as pltpu
from jax.sharding import PartitionSpec as P

rope_base = 1000000.0
norm_eps = 1e-06
f32 = jnp.float32
bf16 = jnp.bfloat16
whole = pl.BlockSpec(memory_space=pltpu.VMEM)
in_place = pl.BlockSpec(memory_space=pl.ANY)


def rms_scale(values):
    return lax.rsqrt(jnp.mean(values * values, axis=-1, keepdims=True) + norm_eps)


def matmul(left, right):
    return jnp.dot(left, right, preferred_element_type=f32)


def contract_rows(left, right):
    return lax.dot_general(left, right, (((0,), (0,)), ((), ())), preferred_element_type=f32)


def times_transposed(left, right):
    return lax.dot_general(left, right, (((1,), (1,)), ((), ())), preferred_element_type=f32)


def rotate(values):
    half_width = values.shape[-1] // 2
    return jnp.concatenate([-values[..., half_width:], values[..., :half_width]], axis=-1)


def flip_bit(value, bit):
    return value + bit * (1 - 2 * lax.rem(lax.div(value, bit), 2))


class Peers:
    def __init__(self, groups, lanes):
        self.groups, self.lanes = groups, lanes
        self.far = groups // 2
        self.chips = lanes // 2
        self.group = lax.axis_index("expert")
        self.lane = lax.axis_index("tensor")
        self.core = lax.rem(self.lane, 2)
        self.chip = lax.div(self.lane, 2)
        if groups == 8:
            z, y = lax.div(self.group, 2), lax.rem(self.group, 2)
            self.place = z + y * (7 - 2 * z)
        else:
            self.place = self.group

    def group_at(self, offset):
        place = lax.rem(self.place + (offset + self.groups), self.groups)
        if self.groups == 8:
            y = lax.div(place, 4)
            return 2 * (place + y * (7 - 2 * place)) + y
        return place

    def at(self, offset):
        return (self.group_at(offset), self.lane)

    def other_core(self):
        return (self.group, self.lane + 1 - 2 * self.core)

    def chip_bits(self):
        return [1 << i for i in range(self.chips.bit_length() - 1)]

    def other_chip(self, bit):
        return (self.group, 2 * flip_bit(self.chip, bit) + self.core)

    def chip_on(self, step):
        return lax.rem(self.chip + step, self.chips)

    def chip_peers(self):
        return [
            (self.group, 2 * self.chip_on(step) + self.core) for step in range(1, self.chips)
        ]

    def offsets(self):
        return [0] + [s * k for k in range(1, self.far) for s in (1, -1)] + [self.far]

    def meet(self, peers):
        barrier = pltpu.get_barrier_semaphore()
        for peer in peers:
            pl.semaphore_signal(
                barrier, inc=1, device_id=peer, device_id_type=pl.DeviceIdType.MESH
            )
        pl.semaphore_wait(barrier, len(peers))


class Copies:
    def __init__(self, send_sems, recv_sems):
        self.send_sems, self.recv_sems = send_sems, recv_sems
        self.planned = []

    def plan(self, source, target, peer, arriving=None, ends=True):
        index = self.planned_count()
        arriving = target if arriving is None else arriving

        def copy(source, target):
            return pltpu.make_async_remote_copy(
                src_ref=source,
                dst_ref=target,
                send_sem=self.send_sems.at[index],
                recv_sem=self.recv_sems.at[index],
                device_id=peer,
                device_id_type=pl.DeviceIdType.MESH,
            )

        made = Planned(copy(source, target), copy(arriving, arriving))
        self.planned.append((made, ends))
        return made

    def planned_count(self):
        return len(self.planned)

    def start(self, source, target, peer, arriving=None):
        made = self.plan(source, target, peer, arriving)
        made.start()
        return made.wait

    def finish(self):
        for made, ends in self.planned:
            if ends:
                made.sent()


class Planned:
    def __init__(self, mine, theirs):
        self.start, self.sent, self.wait = mine.start, mine.wait_send, theirs.wait_recv


class RingSum:
    def __init__(self, copies, peers, stage, received, rows, places, first=1, last=None, eager=False):
        far = peers.far
        self.far, self.size, self.first, self.eager = far, rows // 2, first, eager
        self.places = places
        self.copies = {}
        for j in range(first, 2 * far if last is None else last + 1):
            for way, peer in ((0, peers.at(1)), (1, peers.at(-1))):
                at = pl.ds(self.start(j, way), self.size)
                self.copies[j, way] = copies.plan(
                    stage.at[self.place(j, way), at],
                    received.at[way, j - 1],
                    peer,
                    ends=False,
                )

    def offset(self, j, way):
        k = self.far - j // 2
        return k if way == 0 or k == self.far else -k

    def start(self, j, way):
        return self.size * ((j + 1 + way) % 2)

    def place(self, j, way):
        return self.places(self.offset(j, way), way)

    def step(self, j, prepare, merge):
        if j % 2 == 0 or j == self.first:
            for way in (0, 1):
                for old in (j - 4, j - 3):
                    if (old, way) in self.copies and j % 2 == 0:
                        self.copies[old, way].sent()
            for way in (0, 1) if j > 1 else (0,):
                prepare(self.offset(j, way), way)
        for way in (0, 1):
            before = (way, j - 3) if j > 2 else None
            if self.eager and j - 2 >= self.first:
                self.copies[j - 2, way].wait()
            merge(self.place(j, way), way if j > 1 else 0, self.start(j, way), self.size, before)
            if self.eager:
                self.copies[j, way].start()
        if self.eager:
            return
        for way in (0, 1):
            if j > self.first:
                self.copies[j - 1, way].wait()
            self.copies[j, way].start()

    def arrived(self):
        for j in (2 * self.far - 2, 2 * self.far - 1)[0 if self.eager else 1 :]:
            for way in (0, 1):
                self.copies[j, way].wait()
        return [
            (way, j - 1, self.start(j, way))
            for j in (2 * self.far - 2, 2 * self.far - 1)
            for way in (0, 1)
        ]

    def finish(self, unsent):
        for j in unsent:
            for way in (0, 1):
                self.copies[j, way].sent()


def tiles(rows, size, step):
    def body(i, carry):
        step(pl.ds(pl.multiple_of(i * size, size), size))
        return carry

    lax.fori_loop(0, rows // size, body, 0)


def nt(left, right):
    return lax.dot_general(left, right, (((1,), (1,)), ((), ())), preferred_element_type=f32)


def spans(total, size):
    return [(at, min(size, total - at)) for at in range(0, total, size)]


class Sizes:
    def __init__(self, **sizes):
        self.__dict__.update(sizes)


class Work:
    def __init__(self, sizes, expert, bufs):
        self.sizes, self.expert = sizes, expert
        self.__dict__.update(bufs)

    def place(self, s, ids):
        z = self.sizes
        named = jnp.max(jnp.where(ids == self.expert, 1.0, 0.0), axis=0, keepdims=True)
        named = jnp.concatenate([named, jnp.zeros((7, z.seq), f32)], axis=0).astype(bf16)
        along = nt(named, self.ranker[...]) - 1024.0
        down = nt(self.ranker[...], named) - 1024.0
        slots = lax.broadcasted_iota(jnp.int32, (z.capacity, z.seq), 0).astype(f32)
        self.pick[s] = jnp.where(along[0:1, :] == slots, 1.0, 0.0).astype(bf16)
        slots = lax.broadcasted_iota(jnp.int32, (z.seq, z.capacity), 1).astype(f32)
        self.put[s] = jnp.where(down[:, 0:1] == slots, 1.0, 0.0).astype(bf16)

    def rows_of(self, s):
        return pl.ds(s * self.sizes.capacity, self.sizes.capacity)

    def tokens_of(self, s):
        return pl.ds(s * self.sizes.seq, self.sizes.seq)

    def take(self):
        z = self.sizes

        def step(cols):
            for s in range(2):
                picked = matmul(self.pick[s], self.tokens[self.tokens_of(s), cols])
                self.rows[self.rows_of(s), cols] = picked.astype(bf16)
                picked = matmul(self.pick[s], self.grads[self.tokens_of(s), cols])
                self.row_grads[self.rows_of(s), cols] = picked.astype(bf16)

        tiles(z.width, 256, step)

    def routed(self, small):
        z = self.sizes
        rows = self.rows[...]
        logits = matmul(rows, self.router[...])
        lanes = lax.broadcasted_iota(jnp.int32, logits.shape, 1)
        logits = jnp.where(lanes < z.experts, logits, -1e30)
        weights = jnp.exp(logits - jnp.max(logits, axis=1, keepdims=True))
        mine = jnp.sum(jnp.where(lanes == self.expert, weights, 0.0), axis=1, keepdims=True)
        gate = mine / jnp.sum(weights, axis=1, keepdims=True)
        d_gate = jnp.zeros_like(gate)
        for at, size in spans(z.ff, 256):
            a = nt(self.rows[...], self.w_in[pl.ds(at, size), :])
            b = nt(self.rows[...], self.w_in[pl.ds(z.ff + at, size), :])
            u = nt(self.row_grads[...], self.w_out[pl.ds(at, size), :])
            cols = pl.ds(at, size)
            sigma = 1.0 / (1.0 + jnp.exp(-a))
            silu = a * sigma
            hidden = (silu * b).astype(bf16).astype(f32)
            d_gate = d_gate + jnp.sum(hidden * u, axis=1, keepdims=True)
            self.gated[:, cols] = (hidden * gate).astype(bf16)
            d_hidden = u * gate
            self.d_a[:, cols] = (d_hidden * b * sigma * (1.0 + a * (1.0 - sigma))).astype(bf16)
            self.d_b[:, cols] = (d_hidden * silu).astype(bf16)
        for s in range(2):
            mine = d_gate[s * z.capacity : (s + 1) * z.capacity]
            small[s][pl.ds(0, 1), :] = jnp.sum(
                jnp.where(self.pick[s].astype(f32) > 0.5, mine, 0.0), axis=0, keepdims=True
            )

        def step(cols):
            back = matmul(self.d_a[...], self.w_in[pl.ds(0, z.ff), cols])
            back = back + matmul(self.d_b[...], self.w_in[pl.ds(z.ff, z.ff), cols])
            self.d_rows[:, cols] = back.astype(bf16)

        tiles(z.width, 256, step)

    def shared(self, small):
        z = self.sizes
        for s in range(2):
            at = self.tokens_of(s)
            tokens = self.tokens[at, :]
            logits = matmul(tokens, self.router[...])
            lanes = lax.broadcasted_iota(jnp.int32, logits.shape, 1)
            logit = jnp.sum(jnp.where(lanes == z.experts, logits, 0.0), axis=1, keepdims=True)
            sig = 1.0 / (1.0 + jnp.exp(-logit))
            both = matmul(tokens, self.s_in[...])
            a, b = both[:, : z.units], both[:, z.units :]
            u = nt(self.grads[at, :], self.s_out[...])
            sigma = 1.0 / (1.0 + jnp.exp(-a))
            silu = a * sigma
            hidden = (silu * b).astype(bf16).astype(f32)
            d_sig = lax.dot_general(
                jnp.ones((8, z.units), f32),
                hidden * u,
                (((1,), (1,)), ((), ())),
                precision=lax.Precision.HIGHEST,
                preferred_element_type=f32,
            )
            small[s][pl.ds(1, 1), :] = d_sig[0:1]
            self.s_gated[at, :] = (hidden * sig).astype(bf16)
            d_hidden = u * sig
            d_a = d_hidden * b * sigma * (1.0 + a * (1.0 - sigma))
            self.s_d_both[at, : z.units] = d_a.astype(bf16)
            self.s_d_both[at, z.units :] = (d_hidden * silu).astype(bf16)

    def give(self):
        z = self.sizes

        def step(cols):
            self.out_rows[...] = matmul(self.gated[...], self.w_out[:, cols]).astype(bf16)
            out = matmul(self.s_gated[...], self.s_out[:, cols])
            back = nt(self.s_d_both[...], self.s_in[cols, :])
            for s in range(2):
                at = slice(s * z.seq, (s + 1) * z.seq)
                mine = out[at] + matmul(self.put[s], self.out_rows[self.rows_of(s), :])
                self.out[self.tokens_of(s), cols] = mine.astype(bf16)
                mine = back[at] + matmul(self.put[s], self.d_rows[self.rows_of(s), cols])
                self.d_in[self.tokens_of(s), cols] = mine.astype(bf16)

        tiles(z.width, 256, step)


def experts_kernel(z, names, *refs):
    r = Sizes(**dict(zip(names, refs)))
    groups, lanes = z.groups, z.lanes
    peers = Peers(groups, lanes)
    far, bits = peers.far, peers.chip_bits()
    seq = z.seq
    half, piece = seq // 2, seq // lanes
    core = peers.core
    own = core * half
    half_rows = pl.ds(pl.multiple_of(own, half), half)
    other_rows = pl.ds(pl.multiple_of(half - own, half), half)
    first = pl.multiple_of((core * peers.chips + peers.chip) * piece, piece)
    me = peers.group
    others = [k for k in peers.offsets() if k != 0]
    step_of = {k: 2 * k - 1 if k > 0 else -2 * k for k in peers.offsets()}
    slot = {k: peers.group_at(k) for k in range(-far, far + 1)}
    ahead, behind = peers.at(1), peers.at(-1)
    core_peer = peers.other_core()
    chip_peer = {b: peers.other_chip(b) for b in bits}
    peers.meet([peers.at(k) for k in others] + [core_peer] + peers.chip_peers())
    copies = Copies(r.send_sems, r.recv_sems)

    def local(source, target, number):
        return pltpu.make_async_copy(source, target, r.local_sems.at[number])

    def remote(source, target, send_sem, recv_sem, peer):
        return pltpu.make_async_remote_copy(
            src_ref=source,
            dst_ref=target,
            send_sem=send_sem,
            recv_sem=recv_sem,
            device_id=peer,
            device_id_type=pl.DeviceIdType.MESH,
        )

    ff_own = z.ff // 2
    mine_at = pl.multiple_of(core * ff_own, 16)
    theirs_at = pl.multiple_of((1 - core) * ff_own, 16)
    weights, traded = [], []
    for number, (source, target, base) in enumerate(
        [(r.gate, r.w_in, 0), (r.up, r.w_in, z.ff), (r.down, r.w_out, 0)]
    ):
        rows = pl.ds(base + mine_at, ff_own)
        weights.append(local(source.at[core], target.at[rows], number))
        traded.append(
            copies.plan(
                source.at[1 - core],
                target.at[rows],
                core_peer,
                target.at[pl.ds(base + theirs_at, ff_own)],
            )
        )
    weights += [
        local(r.s_in_hbm, r.s_in, 3),
        local(
            r.s_out_hbm.at[pl.ds(pl.multiple_of(peers.group * z.down_step, 16), z.down_rows)],
            r.s_out.at[pl.ds(0, z.down_rows)],
            4,
        ),
        local(r.router_hbm, r.router, 5),
    ]
    own_part = local(r.part.at[half_rows], r.total, 6)
    own_grad = local(r.grad, r.grads_all.at[me], 7)
    own_tokens = local(r.normed, r.tokens_all.at[me, half_rows], 8)
    own_hidden = local(r.hidden.at[half_rows], r.stage.at[0], 9)
    keep_resid = local(r.wide, r.resid, 10)

    def hop(array, k, start, size, source=None):
        held = slot[k + 1] if k < 0 else slot[k - 1]
        rows = pl.ds(pl.multiple_of(start, size), size)
        return copies.plan(
            array.at[held, rows] if source is None else source,
            array.at[held, rows],
            ahead if k < 0 else behind,
            array.at[slot[k], rows],
        )

    def chip_swap(array, k, bit):
        size = bit * piece
        start = (core * peers.chips + lax.div(peers.chip, bit) * bit) * piece
        theirs = (core * peers.chips + lax.div(flip_bit(peers.chip, bit), bit) * bit) * piece
        rows = pl.ds(pl.multiple_of(start, size), size)
        arriving = pl.ds(pl.multiple_of(theirs, size), size)
        return copies.plan(
            array.at[slot[k], rows],
            array.at[slot[k], rows],
            chip_peer[bit],
            array.at[slot[k], arriving],
        )

    def core_swap(array, k, source=None):
        return copies.plan(
            array.at[slot[k], half_rows] if source is None else source,
            array.at[slot[k], half_rows],
            core_peer,
            array.at[slot[k], other_rows],
        )

    signed = [s * k for k in range(1, far) for s in (-1, 1)]
    ids_got = [
        copies.plan(r.ids, r.ids_all.at[me], peers.at(k), r.ids_all.at[slot[-k]]) for k in others
    ]
    own_piece = r.grad.at[pl.ds(first, piece)]
    g_ring = {
        k: hop(r.grads_all, k, first, piece, own_piece if abs(k) == 1 else None) for k in signed
    }
    g_ring[-far] = hop(r.grads_all, -far, first, piece // 2)
    g_ring[far] = hop(r.grads_all, far, first + piece // 2, piece // 2)
    steps = range(1, peers.chips)
    own_piece_rows = pl.ds(pl.multiple_of(peers.chip * piece, 32), piece)
    pieces = [own_piece_rows] + [
        pl.ds(pl.multiple_of(peers.chip_on(peers.chips - n) * piece, 32), piece) for n in steps
    ]
    x_first = [
        {s: hop(r.tokens_all, s, own + at.start, piece, r.normed.at[at]) for s in (-1, 1)}
        for at in pieces
    ]
    x_ring = {k: hop(r.tokens_all, k, own, half) for k in signed if abs(k) > 1}
    x_ring[-far] = hop(r.tokens_all, -far, own, half // 2)
    x_ring[far] = hop(r.tokens_all, far, own + half // 2, half // 2)
    g_chip = {k: [chip_swap(r.grads_all, k, b) for b in bits] for k in others}
    g_core = {k: core_swap(r.grads_all, k) for k in others}
    x_core = {
        k: core_swap(r.tokens_all, k, r.normed if k == 0 else None) for k in peers.offsets()
    }
    part_core = copies.plan(r.part.at[other_rows], r.from_core, core_peer)
    part_out = [
        copies.plan(
            r.total.at[pl.ds(pl.multiple_of(peers.chip_on(n) * piece, 32), piece)],
            r.part_in.at[n - 1],
            peers.chip_peers()[n - 1],
            ends=False,
        )
        for n in steps
    ]
    part_back = [
        copies.plan(
            r.total.at[own_piece_rows],
            r.part_all.at[own_piece_rows],
            peers.chip_peers()[n - 1],
            r.part_all.at[pieces[n]],
            ends=False,
        )
        for n in steps
    ]

    d_ring = RingSum(
        copies, peers, r.stage, r.from_ring, half,
        lambda k, way: k % 2 + (2 * way if abs(k) < far else 0), eager=True,
    )
    y_ring = RingSum(
        copies, peers, r.stage, r.y_early, half,
        lambda k, way: k % 2 + (2 * way if abs(k) < far else 0), last=2,
    )
    home_chip = [
        copies.plan(r.total, r.from_chip.at[i], chip_peer[b], ends=False)
        for i, b in enumerate(bits)
    ]
    small_peers = [core_peer] + [chip_peer[b] for b in bits]
    small_swaps = [
        copies.plan(r.small_swap.at[2 * i], r.small_swap.at[2 * i + 1], peer)
        for i, peer in enumerate(small_peers)
    ]

    part_core.start()
    own_part.start()
    own_hidden.start()
    g_ring[-1].start()
    g_ring[1].start()
    for copy in ids_got:
        copy.start()
    r.ids_all[me] = r.ids[...]
    for copy in weights + traded:
        copy.start()
    own_grad.start()
    token = lax.broadcasted_iota(jnp.int32, (seq, seq), 0)
    other = lax.broadcasted_iota(jnp.int32, (seq, seq), 1)
    ranks = jnp.where(other < token, 1.0, jnp.where(other == token, 1024.0, 0.0))
    r.ranker[...] = ranks.astype(bf16)
    if z.down_rows < z.units:
        at = pl.ds(z.down_rows, z.units - z.down_rows)
        r.s_out[at, :] = jnp.zeros((z.units - z.down_rows, z.width), bf16)

    own_part.wait()
    part_core.wait()

    def add_core(rows):
        both = r.total[rows, :].astype(f32) + r.from_core[rows, :].astype(f32)
        r.total[rows, :] = both.astype(bf16)

    tiles(half, 32, add_core)
    for copy in part_out:
        copy.start()
    own_hidden.wait()

    def norm_piece(source, start):
        def step(rows):
            at = pl.ds(pl.multiple_of(start + rows.start, rows.size), rows.size)
            both = r.stage[0, at, :].astype(f32) + source[at, :].astype(f32)
            r.wide[at, :] = both
            r.normed[at, :] = (both * rms_scale(both) * r.gain[...]).astype(bf16)

        tiles(piece, 32, step)

    def add_chips(rows):
        at = pl.ds(pl.multiple_of(own_piece_rows.start + rows.start, rows.size), rows.size)
        total = r.total[at, :].astype(f32)
        for n in steps:
            total = total + r.part_in[n - 1, rows, :].astype(f32)
        r.total[at, :] = total.astype(bf16)

    for k in range(2, far):
        for s in (-1, 1):
            g_ring[s * (k - 1)].wait()
            g_ring[s * k].start()
        if k != 2:
            continue
        for copy in part_out:
            copy.wait()
        tiles(piece, 32, add_chips)
        for copy in part_back:
            copy.start()
        norm_piece(r.total, own_piece_rows.start)
        for s in (-1, 1):
            x_first[0][s].start()
    for n in steps:
        part_back[n - 1].wait()
        norm_piece(r.part_all, pieces[n].start)
        for s in (-1, 1):
            x_first[n][s].start()
    x_core[0].start()
    own_tokens.start()
    keep_resid.start()
    for k in signed[:-2]:
        g_chip[k][0].start()
    for copy in ids_got + weights + traded:
        copy.wait()
    own_grad.wait()
    own_tokens.wait()
    keep_resid.wait()
    for copy in part_out + part_back:
        copy.sent()

    def finish_grads(ks):
        for k in ks:
            for i in range(len(bits)):
                g_chip[k][i].wait()
                if i + 1 < len(bits):
                    g_chip[k][i + 1].start()
            g_core[k].start()

    def forward(p):
        for q in range(far):

            @pl.when(p == q)
            def _(k=q + 1):
                if k < far:
                    for s in (-1, 1):
                        for copy in [one[s] for one in x_first] if k == 1 else [x_ring[s * k]]:
                            copy.wait()
                        if k + 1 < far:
                            x_ring[s * (k + 1)].start()
                    if k + 1 == far:
                        x_ring[-far].start()
                        x_ring[far].start()
                    for s in (1, -1):
                        x_core[s * k].start()
                else:
                    x_ring[-far].wait()
                    x_ring[far].wait()
                    x_core[far].start()
                if k == 1:
                    for s in (-1, 1):
                        g_ring[s * (far - 1)].wait()
                        g_ring[s * far].start()
                        g_chip[s * (far - 1)][0].start()
                if k == 2:
                    g_ring[-far].wait()
                    g_ring[far].wait()
                    g_chip[far][0].start()
                finish_grads([k, -k] if k < far else [far])
                x_core[1 - k].wait()
                if k > 1:
                    g_core[1 - k].wait()

    def complete(p):
        for q in range(far):

            @pl.when(p == q)
            def _(k=q + 1):
                x_core[k].wait()
                g_core[k].wait()

    def small_copy(i, peer):
        return remote(
            r.small_out.at[i], r.small_in.at[i], r.small_send.at[i], r.small_recv.at[i], peer
        )

    def given_copy(i, source):
        return remote(source, r.given.at[i], r.give_send.at[i], r.give_recv.at[i], core_peer)

    def y_given_copy(i, source):
        return remote(source, r.y_given.at[i], r.y_send.at[i], r.y_recv.at[i], core_peer)

    def main(tokens, grads, rows, row_grads, d_rows, out_rows, gated, d_a, d_b, s_gated,
             s_d_both, out, d_in, pick, put):
        work = Work(
            z,
            me * 2 + core,
            dict(
                tokens=tokens, grads=grads, rows=rows, row_grads=row_grads, d_rows=d_rows,
                out_rows=out_rows, gated=gated, d_a=d_a, d_b=d_b, s_gated=s_gated,
                s_d_both=s_d_both, out=out, d_in=d_in, pick=pick, put=put, w_in=r.w_in,
                w_out=r.w_out, s_in=r.s_in, s_out=r.s_out, router=r.router, ranker=r.ranker,
            ),
        )

        def leave(p, slots):
            found = []
            for s in range(2):
                i = 2 * p + s
                keep = pl.ds(pl.multiple_of(s * seq + own, half), half)
                give = pl.ds(pl.multiple_of(s * seq + half - own, half), half)
                sent = given_copy(i, d_in.at[give])
                kept = local(d_in.at[keep], r.kept.at[i], 12 + s)
                found += [(kept.start, kept.wait), (sent.start, sent.wait_send)]
                sent = y_given_copy(i, out.at[give])
                found.append((sent.start, sent.wait_send))
                stored = local(out.at[pl.ds(s * seq, seq)], r.outs_all.at[slots[s]], 14 + s)
                found.append((stored.start, stored.wait))
            return found

        def arrivals(p, s):
            slot_now = peers.group_at(p + 1 if s else -p)
            at = pl.ds(s * seq, seq)
            return [
                local(r.tokens_all.at[slot_now], tokens.at[at], s),
                local(r.grads_all.at[slot_now], grads.at[at], 2 + s),
            ]

        def load(p, s):
            @pl.when(p < far)
            def _():
                for copy in arrivals(p, s):
                    copy.start()

        forward(0)
        load(0, 0)
        complete(0)
        load(0, 1)

        def loop(p, carry):
            slots = [peers.group_at(-p), peers.group_at(p + 1)]
            for s in range(2):
                work.place(s, r.ids_all[slots[s]])
            for copy in arrivals(p, 0) + arrivals(p, 1):
                copy.wait()
            at = pl.ds(pl.multiple_of(p * 2 * z.capacity, 2 * z.capacity), 2 * z.capacity)
            saves = [
                local(source, target.at[at], 16 + n)
                for n, (source, target) in enumerate(
                    [
                        (rows, r.rows_all),
                        (row_grads, r.row_grads_all),
                        (gated, r.gated_all),
                        (d_a, r.d_a_all),
                        (d_b, r.d_b_all),
                    ]
                )
            ]
            for s in range(2):
                mine = pl.ds(s * seq, seq)
                saves.append(local(s_gated.at[mine], r.s_gated_all.at[slots[s]], 21 + 2 * s))
                saves.append(local(s_d_both.at[mine], r.s_d_both_all.at[slots[s]], 22 + 2 * s))
            small = [r.small_out.at[2 * p], r.small_out.at[2 * p + 1]]
            work.take()
            for copy in saves[:2]:
                copy.start()
            work.routed(small)
            for copy in saves[2:5]:
                copy.start()
            work.shared(small)
            for copy in saves[5:]:
                copy.start()
            forward(p + 1)
            load(p + 1, 0)
            small_copy(2 * p + 1, (slots[1], peers.lane)).start()

            @pl.when(p > 0)
            def _():
                small_copy(2 * p, (slots[0], peers.lane)).start()
                for _, wait in leave(p - 1, slots):
                    wait()

            work.give()
            for start, _ in leave(p, slots):
                start()
            complete(p + 1)
            load(p + 1, 1)
            for copy in saves:
                copy.wait()
            return carry

        lax.fori_loop(0, far, loop, 0)
        for _, wait in leave(far - 1, [me, me]):
            wait()

    pl.run_scoped(
        main,
        tokens=pltpu.VMEM((2 * seq, z.width), bf16),
        grads=pltpu.VMEM((2 * seq, z.width), bf16),
        rows=pltpu.VMEM((2 * z.capacity, z.width), bf16),
        row_grads=pltpu.VMEM((2 * z.capacity, z.width), bf16),
        d_rows=pltpu.VMEM((2 * z.capacity, z.width), bf16),
        out_rows=pltpu.VMEM((2 * z.capacity, 256), bf16),
        gated=pltpu.VMEM((2 * z.capacity, z.ff), bf16),
        d_a=pltpu.VMEM((2 * z.capacity, z.ff), bf16),
        d_b=pltpu.VMEM((2 * z.capacity, z.ff), bf16),
        s_gated=pltpu.VMEM((2 * seq, z.units), bf16),
        s_d_both=pltpu.VMEM((2 * seq, 2 * z.units), bf16),
        out=pltpu.VMEM((2 * seq, z.width), bf16),
        d_in=pltpu.VMEM((2 * seq, z.width), bf16),
        pick=pltpu.VMEM((2, z.capacity, seq), bf16),
        put=pltpu.VMEM((2, seq, z.capacity), bf16),
    )

    def fetch(k, place, core_place):
        i = step_of[k]
        given_copy(i, r.given.at[i]).wait_recv()
        loads = [
            local(r.kept.at[i], r.stage.at[place], 0),
            local(r.given.at[i], r.stage_core.at[core_place], 1),
        ]
        for copy in loads:
            copy.start()
        for copy in loads:
            copy.wait()

    def prepare(k, way):
        fetch(k, d_ring.places(k, way), way)

    def merge(place, core_place, start, size, before):
        def step(rows):
            at = pl.ds(start + rows.start, rows.size)
            value = r.stage[place, at, :].astype(f32) + r.stage_core[core_place, at, :].astype(f32)
            if before is not None:
                value = value + r.from_ring[before[0], before[1], rows, :].astype(f32)
            r.stage[place, at, :] = value.astype(bf16)

        tiles(size, 32, step)

    def ring_step(j):
        d_ring.step(j, prepare, merge)

    ring_step(1)
    ring_step(2)

    features = z.width // groups

    def columns_of(t):
        return pl.ds(pl.multiple_of(t * features, features), features)

    def routed_grads(gated, d_a, d_b, rows, row_grads, wide_in, wide_out):
        whole_loads = [
            local(r.gated_all, gated, 4),
            local(r.d_a_all, d_a, 5),
            local(r.d_b_all, d_b, 6),
        ]

        def loads(t):
            odd = lax.rem(t, 2)
            cols = columns_of(t)
            return [
                local(r.rows_all.at[:, cols], rows.at[odd], 7 + odd),
                local(r.row_grads_all.at[:, cols], row_grads.at[odd], 9 + odd),
            ]

        def stores(t):
            odd = lax.rem(t, 2)
            cols = columns_of(t)
            found = []
            for n, (source, base, target) in enumerate(
                [
                    (wide_in, 0, r.g_gate),
                    (wide_in, z.ff, r.g_up),
                    (wide_out, 0, r.g_down),
                ]
            ):
                here = source.at[odd, pl.ds(base + mine_at, ff_own)]
                there = source.at[odd, pl.ds(base + theirs_at, ff_own)]
                kept = local(here, target.at[core, :, cols], 11 + 2 * n + odd)
                sent = remote(
                    there,
                    target.at[core, :, cols],
                    r.grad_send.at[2 * n + odd],
                    r.grad_recv.at[n * groups + t],
                    core_peer,
                )
                found.append((kept, sent))
            return found

        def settle(t):
            for kept, sent in stores(t):
                kept.wait()
                sent.wait_send()

        def unit(t, carry):
            odd = lax.rem(t, 2)

            @pl.when(t + 1 < groups)
            def _():
                for copy in loads(t + 1):
                    copy.start()

            for copy in loads(t):
                copy.wait()

            @pl.when(t >= 2)
            def _():
                settle(t - 2)

            wide_in[odd, pl.ds(0, z.ff), :] = contract_rows(d_a[...], rows[odd]).astype(bf16)
            wide_in[odd, pl.ds(z.ff, z.ff), :] = contract_rows(d_b[...], rows[odd]).astype(bf16)
            wide_out[odd] = contract_rows(gated[...], row_grads[odd]).astype(bf16)
            for kept, sent in stores(t):
                kept.start()
                sent.start()
            return carry

        for copy in whole_loads + loads(0):
            copy.start()
        for copy in whole_loads:
            copy.wait()
        for n in range(3):
            lax.fori_loop(groups * n // 3, groups * (n + 1) // 3, unit, 0)
            if n < 2:
                ring_step(3 + n)
        settle(groups - 2)
        settle(groups - 1)

    tile_rows = groups * z.capacity
    pl.run_scoped(
        routed_grads,
        gated=pltpu.VMEM((tile_rows, z.ff), bf16),
        d_a=pltpu.VMEM((tile_rows, z.ff), bf16),
        d_b=pltpu.VMEM((tile_rows, z.ff), bf16),
        rows=pltpu.VMEM((2, tile_rows, features), bf16),
        row_grads=pltpu.VMEM((2, tile_rows, features), bf16),
        wide_in=pltpu.VMEM((2, 2 * z.ff, features), bf16),
        wide_out=pltpu.VMEM((2, z.ff, features), bf16),
    )

    def shared_grads(s_gated, s_d_both, tokens, grads, wide):
        whole_loads = [local(r.s_gated_all, s_gated, 4), local(r.s_d_both_all, s_d_both, 5)]

        def loads(t):
            odd = lax.rem(t, 2)
            cols = columns_of(t)
            return [
                local(r.tokens_all.at[:, :, cols], tokens.at[odd], 7 + odd),
                local(r.grads_all.at[:, :, cols], grads.at[odd], 9 + odd),
            ]

        def store(t):
            odd = lax.rem(t, 2)
            return local(wide.at[odd], r.s_grads.at[t], 11 + odd)

        def flat(array):
            return array.reshape(groups * seq, array.shape[-1])

        def unit(t, carry):
            odd = lax.rem(t, 2)

            @pl.when(t + 1 < groups)
            def _():
                for copy in loads(t + 1):
                    copy.start()

            for copy in loads(t):
                copy.wait()

            @pl.when(t >= 2)
            def _():
                store(t - 2).wait()

            both = contract_rows(flat(s_d_both[...]), flat(tokens[odd]))
            out = contract_rows(flat(s_gated[...]), flat(grads[odd]))
            used = z.units_used
            for n, part in enumerate((both[:used], both[z.units : z.units + used], out[:used])):
                wide[odd, pl.ds(n * used, used), :] = part.astype(bf16)
            store(t).start()
            return carry

        for copy in whole_loads + loads(0):
            copy.start()
        for copy in whole_loads:
            copy.wait()
        todo = list(range(5, 2 * far))
        for n, j in enumerate(todo):
            ring_step(j)
            lax.fori_loop(groups * n // len(todo), groups * (n + 1) // len(todo), unit, 0)
        store(groups - 2).wait()
        store(groups - 1).wait()

    pl.run_scoped(
        shared_grads,
        s_gated=pltpu.VMEM((groups, seq, z.units), bf16),
        s_d_both=pltpu.VMEM((groups, seq, 2 * z.units), bf16),
        tokens=pltpu.VMEM((2, groups, seq, features), bf16),
        grads=pltpu.VMEM((2, groups, seq, features), bf16),
        wide=pltpu.VMEM((2, 3 * z.units_used, features), bf16),
    )
    d_ring.finish(range(2 * far - 4, 2 * far - 2))
    fetch(0, 0, 0)

    r.small_total[...] = jnp.zeros_like(r.small_total)
    d_sig = r.small_out[0, pl.ds(1, 1), :]
    r.small_total[pl.ds(me * 2 + core, 1), :] = r.small_out[0, pl.ds(0, 1), :]
    for k in others:
        i = step_of[k]
        copy = small_copy(i, peers.at(k))
        copy.wait_recv()
        copy.wait_send()
        d_sig = d_sig + r.small_in[i, pl.ds(1, 1), :]
        r.small_total[pl.ds(slot[-k] * 2 + core, 1), :] = r.small_in[i, pl.ds(0, 1), :]
    r.small_total[pl.ds(z.experts, 1), :] = d_sig
    for i, copy in enumerate(small_swaps):
        r.small_swap[2 * i] = r.small_total[...]
        copy.start()
        copy.wait()
        r.small_total[...] = r.small_swap[2 * i] + r.small_swap[2 * i + 1]

    for n, target in enumerate((r.g_gate, r.g_up, r.g_down)):
        for t in range(groups):
            arriving = target.at[1 - core, :, columns_of(t)]
            remote(
                arriving, arriving, r.grad_send.at[0], r.grad_recv.at[n * groups + t], core_peer
            ).wait_recv()

    def last(way, index, start):
        def step(rows):
            at = pl.ds(start + rows.start, rows.size)
            value = r.wide[at, :] + r.from_ring[way, index, rows, :].astype(f32)
            r.wide[at, :] = value
            r.total[at, :] = value.astype(bf16)

        tiles(half // 2, 32, step)

    def first_of_home(rows):
        both = r.stage[0, rows, :].astype(f32) + r.stage_core[0, rows, :].astype(f32)
        r.wide[rows, :] = both

    tiles(half, 32, first_of_home)
    for chunk in d_ring.arrived():
        last(*chunk)
    d_ring.finish(range(2 * far - 2, 2 * far))

    def y_prepare(k, way):
        loads = [
            local(r.outs_all.at[slot[k], half_rows], r.stage.at[y_ring.places(k, way)], 0),
            local(r.y_given.at[step_of[k]], r.stage_core.at[way], 1),
        ]
        for copy in loads:
            copy.start()
        for copy in loads:
            copy.wait()

    home_chip[0].start()
    for k in peers.offsets():
        i = step_of[k]
        y_given_copy(i, r.y_given.at[i]).wait_recv()
    y_ring.step(1, y_prepare, merge)
    y_ring.step(2, y_prepare, merge)
    for i, copy in enumerate(home_chip):
        if i > 0:
            copy.start()
        copy.wait()
        copy.sent()

        def join(rows, i=i):
            value = r.total[rows, :].astype(f32) + r.from_chip[i, rows, :].astype(f32)
            if i + 1 < len(bits):
                r.total[rows, :] = value.astype(bf16)
            else:
                r.wide[rows, :] = value

        tiles(half, 32, join)
    keep_total = local(r.wide, r.d_total, 0)
    keep_total.start()
    for way in (0, 1):
        y_ring.copies[2, way].wait()
    y_ring.finish((1, 2))
    copies.finish()
    keep_total.wait()


def pad_last(array, size):
    return jnp.pad(array, [(0, 0)] * (array.ndim - 1) + [(0, size - array.shape[-1])])


def round_up(value, unit):
    return -(-value // unit) * unit


def run_experts(groups, lanes, part, hidden, gain, grad, ids, weights, router, capacity):
    gate, up, down, s_gate, s_up, s_down = weights
    seq, width = grad.shape
    ff_own = gate.shape[1]
    units_true = s_gate.shape[1]
    experts = router.shape[1] - 1
    ff, units = 2 * ff_own, round_up(units_true, 128)
    half = seq // 2
    bits = (lanes // 2).bit_length() - 1
    far = groups // 2
    small_rows = round_up(experts + 1, 8)
    whole_down = units_true % 16 == 0
    if whole_down:
        s_out = s_down
    else:
        mine = lax.axis_index("expert") * units_true
        s_out = lax.dynamic_slice_in_dim(s_down, mine, units_true, 0)
        s_out = jnp.pad(s_out, ((0, units - units_true), (0, 0)))
    z = Sizes(
        groups=groups, lanes=lanes, seq=seq, width=width, ff=ff, units=units,
        capacity=capacity, experts=experts, units_used=round_up(units_true, 16), down_step=units_true if whole_down else 0,
        down_rows=units_true if whole_down else units,
    )
    s_in = jnp.concatenate([pad_last(s_gate, units), pad_last(s_up, units)], axis=1)
    router = pad_last(router, 128)
    ins = dict(
        part=(part, in_place), hidden=(hidden, in_place), gain=(gain, whole),
        grad=(grad, in_place), ids=(ids, whole), gate=(gate, in_place),
        up=(up, in_place), down=(down, in_place), s_in_hbm=(s_in, in_place),
        s_out_hbm=(s_out, in_place), router_hbm=(router, in_place),
    )
    rows_all = groups * capacity
    outs = dict(
        normed=((half, width), bf16, whole),
        small_total=((small_rows, seq), f32, whole),
        resid=((half, width), f32, in_place),
        d_total=((half, width), f32, in_place),
        outs_all=((groups, seq, width), bf16, in_place),
        g_gate=(gate.shape, bf16, in_place),
        g_up=(up.shape, bf16, in_place),
        g_down=(down.shape, bf16, in_place),
        s_grads=((groups, 3 * z.units_used, width // groups), bf16, in_place),
        tokens_all=((groups, seq, width), bf16, in_place),
        grads_all=((groups, seq, width), bf16, in_place),
        rows_all=((rows_all, width), bf16, in_place),
        row_grads_all=((rows_all, width), bf16, in_place),
        gated_all=((rows_all, ff), bf16, in_place),
        d_a_all=((rows_all, ff), bf16, in_place),
        d_b_all=((rows_all, ff), bf16, in_place),
        s_gated_all=((groups, seq, units), bf16, in_place),
        s_d_both_all=((groups, seq, 2 * units), bf16, in_place),
        kept=((groups, half, width), bf16, in_place),
        given=((groups, half, width), bf16, in_place),
        y_given=((groups, half, width), bf16, in_place),
        y_early=((2, 2, half // 2, width), bf16, in_place),
    )
    copies = 2 * lanes + 4 + 3 + 2 * groups + (groups - 1) * (2 + bits) + groups + 1 + bits + 4 * far
    copies += 2 * bits + 1
    scratch = dict(
        ids_all=pltpu.VMEM((groups,) + ids.shape, jnp.int32),
        total=pltpu.VMEM((half, width), bf16),
        from_core=pltpu.VMEM((half, width), bf16),
        part_in=pltpu.VMEM((lanes // 2 - 1, seq // lanes, width), bf16),
        part_all=pltpu.VMEM((half, width), bf16),
        from_chip=pltpu.VMEM((max(bits, 1), half, width), bf16),
        wide=pltpu.VMEM((half, width), f32),
        stage=pltpu.VMEM((4, half, width), bf16),
        stage_core=pltpu.VMEM((2, half, width), bf16),
        from_ring=pltpu.VMEM((2, 2 * far - 1, half // 2, width), bf16),
        small_out=pltpu.VMEM((groups, 8, seq), f32),
        small_in=pltpu.VMEM((groups, 8, seq), f32),
        small_swap=pltpu.VMEM((2 * (1 + bits), small_rows, seq), f32),
        ranker=pltpu.VMEM((seq, seq), bf16),
        w_in=pltpu.VMEM((2 * ff, width), bf16),
        w_out=pltpu.VMEM((ff, width), bf16),
        s_in=pltpu.VMEM(s_in.shape, bf16),
        s_out=pltpu.VMEM((units, width), bf16),
        router=pltpu.VMEM(router.shape, bf16),
        send_sems=pltpu.SemaphoreType.DMA((copies,)),
        recv_sems=pltpu.SemaphoreType.DMA((copies,)),
        local_sems=pltpu.SemaphoreType.DMA((25,)),
        give_send=pltpu.SemaphoreType.DMA((groups,)),
        give_recv=pltpu.SemaphoreType.DMA((groups,)),
        y_send=pltpu.SemaphoreType.DMA((groups,)),
        y_recv=pltpu.SemaphoreType.DMA((groups,)),
        small_send=pltpu.SemaphoreType.DMA((groups,)),
        small_recv=pltpu.SemaphoreType.DMA((groups,)),
        grad_send=pltpu.SemaphoreType.DMA((6,)),
        grad_recv=pltpu.SemaphoreType.DMA((3 * groups,)),
    )
    names = list(ins) + list(outs) + list(scratch)
    results = pl.pallas_call(
        functools.partial(experts_kernel, z, names),
        out_shape=tuple(jax.ShapeDtypeStruct(s, d) for s, d, _ in outs.values()),
        in_specs=[spec for _, spec in ins.values()],
        out_specs=tuple(spec for _, _, spec in outs.values()),
        scratch_shapes=list(scratch.values()),
        compiler_params=pltpu.CompilerParams(
            collective_id=0, has_side_effects=True, vmem_limit_bytes=63 * 1024 * 1024
        ),
        name="run_experts",
    )(*[array for array, _ in ins.values()])
    return Sizes(**dict(zip(outs, results)), units=z.units_used)


def finish_kernel(z, names, *refs):
    r = Sizes(**dict(zip(names, refs)))
    groups, lanes = z.groups, z.lanes
    peers = Peers(groups, lanes)
    far, bits = peers.far, peers.chip_bits()
    seq, heads, head, features = z.seq, z.heads, z.head, z.features
    head_all = heads * head
    half = seq // 2
    own = peers.core * half
    half_rows = pl.ds(pl.multiple_of(own, half), half)
    other_rows = pl.ds(pl.multiple_of(half - own, half), half)
    me = peers.group
    others = [k for k in peers.offsets() if k != 0]
    step_of = {k: 2 * k - 1 if k > 0 else -2 * k for k in peers.offsets()}
    slot = {k: peers.group_at(k) for k in range(-far, far + 1)}
    ahead, behind = peers.at(1), peers.at(-1)
    core_peer = peers.other_core()
    chip_peer = {b: peers.other_chip(b) for b in bits}
    peers.meet([peers.at(k) for k in others] + [core_peer] + [chip_peer[b] for b in bits])
    copies = Copies(r.send_sems, r.recv_sems)

    def local(source, target, number):
        return pltpu.make_async_copy(source, target, r.local_sems.at[number])

    attn_core = copies.plan(
        r.d_attn_half, r.d_attn.at[half_rows], core_peer, r.d_attn.at[other_rows]
    )
    own_attn = local(r.d_attn_half, r.d_attn.at[half_rows], 0)

    y_ring = RingSum(
        copies, peers, r.stage, r.from_ring, half,
        lambda k, way: k % 2 + (2 * way if abs(k) < far else 0), first=3, eager=True,
    )
    w_ring = RingSum(
        copies, peers, r.w_parts, r.w_received, features, lambda k, way: step_of[k], eager=True
    )
    y_chip = [
        copies.plan(r.total, r.from_chip.at[i], chip_peer[b], ends=False)
        for i, b in enumerate(bits)
    ]
    layer_core = copies.plan(
        r.norm_total, r.layer_out.at[half_rows], core_peer, r.layer_out.at[other_rows]
    )
    norm_core = copies.plan(r.d_norm.at[other_rows], r.norm_core, core_peer)
    norm_chip = [
        copies.plan(r.norm_total, r.norm_chip.at[i], chip_peer[b], ends=False)
        for i, b in enumerate(bits)
    ]
    in_core = copies.plan(
        r.norm_core, r.grad_in.at[half_rows], core_peer, r.grad_in.at[other_rows]
    )
    small_got = {
        k: copies.plan(r.small_out.at[slot[k]], r.small_in.at[step_of[k]], peers.at(k))
        for k in others
    }
    small_peers = [core_peer] + [chip_peer[b] for b in bits]
    small_swaps = [
        copies.plan(r.small_swap.at[2 * i], r.small_swap.at[2 * i + 1], peer)
        for i, peer in enumerate(small_peers)
    ]

    own_attn.start()
    attn_core.start()
    early = [local(r.y_early.at[way], r.from_ring.at[way, pl.ds(0, 2)], 3 + way) for way in (0, 1)]
    for copy in early:
        copy.start()
    for copy in early:
        copy.wait()

    def fetch(k, place, core_place):
        loads = [
            local(r.outs_all.at[slot[k], half_rows], r.stage.at[place], 1),
            local(r.y_given.at[step_of[k]], r.stage_core.at[core_place], 2),
        ]
        for copy in loads:
            copy.start()
        for copy in loads:
            copy.wait()

    def y_merge(place, core_place, start, size, before):

        def step(rows):
            at = pl.ds(start + rows.start, rows.size)
            value = r.stage[place, at, :].astype(f32) + r.stage_core[core_place, at, :].astype(f32)
            if before is not None:
                value = value + r.from_ring[before[0], before[1], rows, :].astype(f32)
            r.stage[place, at, :] = value.astype(bf16)

        tiles(size, 32, step)

    def y_step(j):
        y_ring.step(j, lambda k, way: fetch(k, y_ring.places(k, way), way), y_merge)

    def w_merge(place, core_place, start, size, before):
        if before is None:
            return

        def step(rows):
            at = pl.ds(start + rows.start, rows.size)
            value = r.w_parts[place, at, :].astype(f32)
            value = value + r.w_received[before[0], before[1], rows, :].astype(f32)
            r.w_parts[place, at, :] = value.astype(bf16)

        tiles(size, 32, step)

    def w_step(j):
        w_ring.step(j, lambda k, way: None, w_merge)

    y_step(3)
    y_step(4)

    def scales(rows):
        scale = rms_scale(r.hidden[rows, :].astype(f32))
        r.scale[rows, :] = jnp.broadcast_to(scale, (scale.shape[0], 128))

    tiles(seq, 64, scales)
    own_attn.wait()
    attn_core.wait()
    lanes_at = lax.broadcasted_iota(jnp.int32, (seq, head), 1)
    r.signed_sine[...] = jnp.where(lanes_at < head // 2, -r.sine[...], r.sine[...])

    def one_head(h, carry):
        signed_sine = r.signed_sine[...]
        query, key, value = r.query[h], r.key[h], r.value[h]
        at = pl.ds(pl.multiple_of(h * head, head), head)
        d_context = nt(r.d_attn[...], r.w_output[at, :]).astype(bf16)
        query_at = lax.broadcasted_iota(jnp.int32, (seq, seq), 0)
        key_at = lax.broadcasted_iota(jnp.int32, (seq, seq), 1)
        allowed = (key_at <= query_at) & (key_at < r.length[0:1, 0:1])
        scores = jnp.where(allowed, nt(query, key) * z.score_scale, -1e30)
        scores = jnp.exp(scores - jnp.max(scores, axis=1, keepdims=True))
        probs = scores / jnp.sum(scores, axis=1, keepdims=True)
        d_probs = matmul(d_context, value)
        row_dot = jnp.sum(probs * d_probs, axis=1, keepdims=True)
        d_scores = (probs * (d_probs - row_dot)).astype(bf16)
        d_query = matmul(d_scores, key) * z.score_scale
        d_key = contract_rows(d_scores, query) * z.score_scale
        d_value = contract_rows(probs.astype(bf16), d_context)

        def unrope(values):
            return values * r.cosine[...] - pltpu.roll(values, head // 2, 1) * signed_sine

        for n, values in enumerate((unrope(d_query), unrope(d_key), d_value)):
            cols = pl.ds(pl.multiple_of(n * head_all + h * head, head), head)
            r.d_qkv[:, cols] = values.astype(bf16)
        return carry

    lax.fori_loop(0, heads, one_head, 0)

    def parts(i, carry):
        k = lax.div(i + 1, 2) * (1 - 2 * lax.rem(i + 1, 2))
        cols = pl.ds(pl.multiple_of(peers.group_at(k) * features, features), features)
        part = contract_rows(r.normed[:, cols], r.d_qkv[...])
        r.w_parts[i, :, pl.ds(0, 3 * head_all)] = part.astype(bf16)
        part = contract_rows(r.d_attn[:, cols], r.context[...])
        r.w_parts[i, :, pl.ds(3 * head_all, head_all)] = part.astype(bf16)
        return carry

    lax.fori_loop(0, groups, parts, 0)
    w_step(1)
    w_step(2)

    r.small_out[...] = r.small_start[...]
    bias = jnp.sum(r.d_qkv[...].astype(f32), axis=0, keepdims=True)
    bias_rows = 3 * head_all // features
    gain_row = z.experts + 2

    def back(g, carry):
        cols = pl.ds(pl.multiple_of(g * features, features), features)
        total = nt(r.d_qkv[:, pl.ds(0, head_all)], r.w_query[cols, :])
        total = total + nt(r.d_qkv[:, pl.ds(head_all, head_all)], r.w_key[cols, :])
        total = total + nt(r.d_qkv[:, pl.ds(2 * head_all, head_all)], r.w_value[cols, :])
        r.d_norm[:, cols] = total.astype(bf16)
        scaled = total * (r.hidden[:, cols].astype(f32) * r.scale[:, 0:1])
        r.small_out[g, pl.ds(gain_row, 1), :] = jnp.sum(scaled, axis=0, keepdims=True)
        for i in range(bias_rows):
            row = gain_row + 1 + peers.lane * bias_rows + i
            r.small_out[g, pl.ds(row, 1), :] = bias[:, i * features : (i + 1) * features]
        return carry

    lax.fori_loop(0, groups, back, 0)
    norm_core.start()
    for k in others:
        small_got[k].start()

    norm_core.wait()

    def add_core(rows):
        mine = pl.ds(pl.multiple_of(own + rows.start, rows.size), rows.size)
        both = r.d_norm[mine, :].astype(f32) + r.norm_core[rows, :].astype(f32)
        r.norm_total[rows, :] = both.astype(bf16)

    tiles(half, 32, add_core)
    norm_chip[0].start()
    load_resid = local(r.d_resid, r.wide, 5)
    load_resid.start()

    def norm_finish():
        for i, copy in enumerate(norm_chip):
            copy.wait()
            copy.sent()
            if i + 1 == len(bits):
                load_resid.wait()

            def join(rows, i=i):
                total = r.norm_total[rows, :].astype(f32) + r.norm_chip[i, rows, :].astype(f32)
                if i + 1 < len(bits):
                    r.norm_total[rows, :] = total.astype(bf16)
                    return
                mine = pl.ds(pl.multiple_of(own + rows.start, rows.size), rows.size)
                hidden = r.hidden[mine, :].astype(f32)
                scale = r.scale[mine, 0:1]
                inner = total * r.gain[...]
                mean = jnp.mean(inner * hidden, axis=-1, keepdims=True)
                total = r.wide[rows, :] + scale * inner - hidden * (scale * scale * scale) * mean
                r.norm_core[rows, :] = total.astype(bf16)

            tiles(half, 32, join)
            if i + 1 < len(bits):
                norm_chip[i + 1].start()
        in_core.start()
        own_in.start()

    own_in = local(r.norm_core, r.grad_in.at[half_rows], 6)
    own_layer = local(r.norm_total, r.layer_out.at[half_rows], 7)
    for j in range(3, 2 * far):
        w_step(j)
        if j + 2 < 2 * far:
            y_step(j + 2)
        if j == 3:
            norm_finish()

    y_ring.finish(range(2 * far - 4, 2 * far - 2))
    fetch(0, 0, 0)

    def first_of_home(rows):
        both = r.stage[0, rows, :].astype(f32) + r.stage_core[0, rows, :].astype(f32)
        r.wide[rows, :] = both

    tiles(half, 32, first_of_home)

    def last(way, index, start):
        def step(rows):
            at = pl.ds(start + rows.start, rows.size)
            value = r.wide[at, :] + r.from_ring[way, index, rows, :].astype(f32)
            r.wide[at, :] = value
            r.total[at, :] = value.astype(bf16)

        tiles(half // 2, 32, step)

    for chunk in y_ring.arrived():
        last(*chunk)
    y_chip[0].start()
    load_out = local(r.resid, r.wide, 8)
    load_out.start()

    for k in others:
        small_got[k].wait()
    small_sum = r.small_out[me]
    for k in others:
        small_sum = small_sum + r.small_in[step_of[k]]
    r.small_total[...] = small_sum
    for i, copy in enumerate(small_swaps):
        r.small_swap[2 * i] = r.small_total[...]
        copy.start()
        copy.wait()
        r.small_total[...] = r.small_swap[2 * i] + r.small_swap[2 * i + 1]

    arrived = w_ring.arrived()
    size = features // 2
    for start in (0, size):
        found = [(way, index) for way, index, at in arrived if at == start]

        def w_last(rows, start=start, found=found):
            at = pl.ds(start + rows.start, rows.size)
            value = r.w_parts[0, at, :].astype(f32)
            for way, index in found:
                value = value + r.w_received[way, index, rows, :].astype(f32)
            r.w_total[at, :] = value

        tiles(size, 32, w_last)
    load_out.wait()
    for i, copy in enumerate(y_chip):
        copy.wait()
        copy.sent()

        def join(rows, i=i):
            value = r.total[rows, :].astype(f32) + r.from_chip[i, rows, :].astype(f32)
            if i + 1 < len(bits):
                r.total[rows, :] = value.astype(bf16)
            else:
                r.norm_total[rows, :] = (r.wide[rows, :] + value).astype(bf16)

        tiles(half, 32, join)
        if i + 1 < len(bits):
            y_chip[i + 1].start()
    layer_core.start()
    own_layer.start()
    layer_core.wait()
    in_core.wait()
    own_in.wait()
    own_layer.wait()
    y_ring.finish(range(2 * far - 2, 2 * far))
    w_ring.finish(range(2 * far - 4, 2 * far))
    copies.finish()


def finish(groups, lanes, sizes, vmem_ins, hbm_ins):
    z = Sizes(groups=groups, lanes=lanes, **sizes)
    seq, width = z.seq, z.width
    half = seq // 2
    bits = (lanes // 2).bit_length() - 1
    far = groups // 2
    head_all = z.heads * z.head
    outs = dict(
        layer_out=((seq, width), bf16, in_place),
        grad_in=((seq, width), bf16, in_place),
        w_total=((z.features, 4 * head_all), f32, whole),
        small_total=(vmem_ins["small_start"].shape[1:], f32, whole),
    )
    small_shape = vmem_ins["small_start"].shape
    copies = groups + 1 + 8 * far + 2 * bits + 3 + (groups - 1) + 1 + bits
    scratch = dict(
        d_attn=pltpu.VMEM((seq, width), bf16),
        d_qkv=pltpu.VMEM((seq, 3 * head_all), bf16),
        d_norm=pltpu.VMEM((seq, width), bf16),
        scale=pltpu.VMEM((seq, 128), f32),
        signed_sine=pltpu.VMEM((seq, z.head), f32),
        stage=pltpu.VMEM((4, half, width), bf16),
        stage_core=pltpu.VMEM((2, half, width), bf16),
        from_ring=pltpu.VMEM((2, 2 * far - 1, half // 2, width), bf16),
        total=pltpu.VMEM((half, width), bf16),
        from_chip=pltpu.VMEM((max(bits, 1), half, width), bf16),
        norm_core=pltpu.VMEM((half, width), bf16),
        norm_total=pltpu.VMEM((half, width), bf16),
        norm_chip=pltpu.VMEM((max(bits, 1), half, width), bf16),
        wide=pltpu.VMEM((half, width), f32),
        w_parts=pltpu.VMEM((groups, z.features, 4 * head_all), bf16),
        w_received=pltpu.VMEM((2, 2 * far - 1, z.features // 2, 4 * head_all), bf16),
        small_out=pltpu.VMEM(small_shape, f32),
        small_in=pltpu.VMEM(small_shape, f32),
        small_swap=pltpu.VMEM((2 * (1 + bits),) + small_shape[1:], f32),
        send_sems=pltpu.SemaphoreType.DMA((copies,)),
        recv_sems=pltpu.SemaphoreType.DMA((copies,)),
        local_sems=pltpu.SemaphoreType.DMA((9,)),
    )
    names = list(vmem_ins) + list(hbm_ins) + list(outs) + list(scratch)
    results = pl.pallas_call(
        functools.partial(finish_kernel, z, names),
        out_shape=tuple(jax.ShapeDtypeStruct(s, d) for s, d, _ in outs.values()),
        in_specs=[whole] * len(vmem_ins) + [in_place] * len(hbm_ins),
        out_specs=tuple(spec for _, _, spec in outs.values()),
        scratch_shapes=list(scratch.values()),
        compiler_params=pltpu.CompilerParams(
            collective_id=1, has_side_effects=True, vmem_limit_bytes=63 * 1024 * 1024
        ),
        name="finish",
    )(*vmem_ins.values(), *hbm_ins.values())
    return Sizes(**dict(zip(outs, results)))


def attend_forward(query, key, value, allowed, score_scale):
    scores = jnp.einsum("qhd,khd->hqk", query, key, preferred_element_type=f32) * score_scale
    scores = jnp.where(allowed[None], scores, -1e30)
    highest = jnp.max(scores, axis=-1, keepdims=True)
    log_total = highest + jnp.log(jnp.sum(jnp.exp(scores - highest), axis=-1, keepdims=True))
    probs = jnp.exp(scores - log_total)
    contexts = jnp.einsum("hqk,khd->qhd", probs.astype(bf16), value, preferred_element_type=f32)
    return contexts.astype(bf16), log_total


def norm_backward(values, scale, gain, d_normed):
    inner = d_normed * gain
    mean = jnp.mean(inner * values, axis=-1, keepdims=True)
    return scale * inner - values * (scale * scale * scale) * mean


def on_device(
    hidden_in,
    seq_lengths,
    expert_ids,
    attn_gain,
    w_query,
    w_key,
    w_value,
    b_query,
    b_key,
    b_value,
    w_output,
    ffn_gain,
    w_router,
    w_sigmoid,
    shared_gate,
    shared_up,
    shared_down,
    expert_gate,
    expert_up,
    expert_down,
    out_grad,
):
    seq, width = hidden_in.shape
    heads, head_width = b_query.shape
    head_all = heads * head_width
    top_count = expert_ids.shape[1]
    experts_all = w_router.shape[1]
    held = expert_gate.shape[0]
    groups = lax.axis_size("expert")
    lane_count = lax.axis_size("tensor")
    group = lax.axis_index("expert")
    lane = lax.axis_index("tensor")
    capacity = 3 * seq * top_count // (2 * experts_all)
    score_scale = 1.0 / math.sqrt(head_width)
    length = seq_lengths[0]
    half = seq // 2
    features = width // groups
    half_start = (lane % 2) * half

    def half_of(array):
        return lax.dynamic_slice_in_dim(array, half_start, half, 0)

    hidden = hidden_in.astype(f32)
    position = jnp.arange(seq, dtype=jnp.int32)
    grad_low = jnp.where((position < length)[:, None], out_grad, jnp.zeros_like(out_grad))

    gain_attn = attn_gain.astype(f32)
    attn_scale = rms_scale(hidden)
    normed_attn = (hidden * attn_scale * gain_attn).astype(bf16)
    freq = jnp.exp(
        jnp.arange(head_width // 2, dtype=f32) * (-2.0 * math.log(rope_base) / head_width)
    )
    angle = position.astype(f32)[:, None] * freq[None, :]
    angle = jnp.concatenate([angle, angle], axis=1)
    cosine, sine = jnp.cos(angle)[:, None, :], jnp.sin(angle)[:, None, :]
    by_head = (seq, heads, head_width)
    query_pre = (matmul(normed_attn, w_query) + b_query.reshape(-1).astype(f32)).reshape(by_head)
    key_pre = (matmul(normed_attn, w_key) + b_key.reshape(-1).astype(f32)).reshape(by_head)
    value_pre = matmul(normed_attn, w_value) + b_value.reshape(-1).astype(f32)
    query = (query_pre * cosine + rotate(query_pre) * sine).astype(bf16)
    key = (key_pre * cosine + rotate(key_pre) * sine).astype(bf16)
    value = value_pre.astype(bf16).reshape(by_head)
    allowed = (position[None, :] <= position[:, None]) & (position[None, :] < length)
    context, log_total = attend_forward(query, key, value, allowed, score_scale)
    context_flat = context.reshape(seq, head_all)
    gain_ffn = ffn_gain.astype(f32)
    ids = jnp.pad(expert_ids.T, ((0, -top_count % 8), (0, 0)), constant_values=-1)
    units = shared_gate.shape[1] // groups
    ex = run_experts(
        groups,
        lane_count,
        matmul(context_flat, w_output).astype(bf16),
        hidden_in,
        gain_ffn[None, :],
        grad_low,
        ids,
        (
            jnp.swapaxes(expert_gate, 1, 2),
            jnp.swapaxes(expert_up, 1, 2),
            expert_down,
            lax.dynamic_slice_in_dim(shared_gate, group * units, units, 1),
            lax.dynamic_slice_in_dim(shared_up, group * units, units, 1),
            shared_down,
        ),
        jnp.concatenate([w_router, w_sigmoid[:, None]], axis=1),
        capacity,
    )
    resid, normed, outs, d_in_sum, small = (
        ex.resid, ex.normed, ex.outs_all, ex.d_total, ex.small_total
    )
    g_gate = jnp.swapaxes(ex.g_gate, 1, 2).astype(f32)
    g_up = jnp.swapaxes(ex.g_up, 1, 2).astype(f32)
    g_down = ex.g_down.astype(f32)

    ffn_scale = rms_scale(resid)
    logits = matmul(normed, w_router)
    route_probs = jax.nn.softmax(logits, axis=-1)
    sig = jax.nn.sigmoid(jnp.dot(normed, w_sigmoid, preferred_element_type=f32))

    small = half_of(small.T)
    d_probs_route, sig_grad = small[:, :experts_all], small[:, experts_all]
    d_logits = (
        route_probs
        * (d_probs_route - jnp.sum(route_probs * d_probs_route, axis=-1, keepdims=True))
    ).astype(bf16)
    d_sig_logit = (sig_grad * sig * (1.0 - sig)).astype(bf16)
    d_from_gates = (
        times_transposed(d_logits, w_router)
        + d_sig_logit.astype(f32)[:, None] * w_sigmoid.astype(f32)[None, :]
    )
    d_normed = d_in_sum + d_from_gates
    d_resid = half_of(grad_low).astype(f32) + norm_backward(resid, ffn_scale, gain_ffn, d_normed)

    rows = half // (lane_count // 2)
    start = (lane // 2) * rows
    mine = [
        lax.dynamic_slice_in_dim(a, start, rows, 0)
        for a in (d_normed * resid * ffn_scale, normed, d_logits, d_sig_logit[:, None])
    ]
    router_part = contract_rows(jnp.concatenate([mine[2], mine[3]], axis=1), mine[1])
    to_groups = jnp.concatenate([router_part, jnp.sum(mine[0], axis=0)[None]], axis=0)
    to_groups = jnp.swapaxes(to_groups.reshape(-1, groups, features), 0, 1)
    bias_rows = 3 * head_all // features
    small_rows = round_up(experts_all + 3 + lane_count * bias_rows, 8)
    small_start = jnp.pad(to_groups, ((0, 0), (0, small_rows - to_groups.shape[1]), (0, 0)))

    done = finish(
        groups,
        lane_count,
        dict(
            seq=seq, width=width, heads=heads, head=head_width, features=features,
            experts=experts_all, score_scale=score_scale,
        ),
        dict(
            query=jnp.swapaxes(query, 0, 1),
            key=jnp.swapaxes(key, 0, 1),
            value=jnp.transpose(value, (1, 2, 0)),
            context=context_flat,
            normed=normed_attn,
            hidden=hidden_in,
            gain=gain_attn[None, :],
            w_output=w_output,
            w_query=w_query,
            w_key=w_key,
            w_value=w_value,
            cosine=cosine[:, 0],
            sine=sine[:, 0],
            length=jnp.broadcast_to(length, (8, 128)),
            small_start=small_start,
        ),
        dict(
            outs_all=outs, y_given=ex.y_given, y_early=ex.y_early,
            d_attn_half=d_resid.astype(bf16), d_resid=d_resid, resid=resid,
        ),
    )
    grads, small, layer_out, grad_in = (
        done.w_total, done.small_total, done.layer_out, done.grad_in
    )
    biases = lax.dynamic_slice_in_dim(
        small, experts_all + 3 + lane * bias_rows, bias_rows, 0
    ).reshape(3, heads, head_width)
    biases = lax.dynamic_slice_in_dim(
        biases, group * (head_width // groups), head_width // groups, 2
    )

    shared = lax.all_to_all(ex.s_grads, "expert", split_axis=0, concat_axis=0, tiled=True)
    shared = shared.reshape(groups, 3, ex.units, features)[:, :, :units].astype(f32)
    shared = jnp.swapaxes(shared, 0, 1).reshape(3, groups * units, features)
    grad_shared_gate, grad_shared_up, grad_shared_down = shared[0].T, shared[1].T, shared[2]
    return (
        layer_out,
        grad_in,
        small[experts_all + 2],
        grads[:, :head_all],
        grads[:, head_all : 2 * head_all],
        grads[:, 2 * head_all : 3 * head_all],
        biases[0],
        biases[1],
        biases[2],
        grads[:, 3 * head_all :].T,
        small[experts_all + 1],
        small[:experts_all].T,
        small[experts_all],
        grad_shared_gate,
        grad_shared_up,
        grad_shared_down,
        g_gate,
        g_up,
        g_down,
    )


def solution(mesh):
    placed = (
        P("expert", None),
        P("expert"),
        P("expert", None),
        P(),
        P(None, "tensor"),
        P(None, "tensor"),
        P(None, "tensor"),
        P("tensor", None),
        P("tensor", None),
        P("tensor", None),
        P("tensor", None),
        P(),
        P(),
        P(),
        P(None, "tensor"),
        P(None, "tensor"),
        P("tensor", None),
        P("expert", None, "tensor"),
        P("expert", None, "tensor"),
        P("expert", "tensor", None),
        P("expert", None),
    )
    return jax.shard_map(
        on_device,
        mesh=mesh,
        in_specs=placed,
        out_specs=(
            P("expert", None),
            P("expert", None),
            P("expert"),
            P("expert", "tensor"),
            P("expert", "tensor"),
            P("expert", "tensor"),
            P("tensor", "expert"),
            P("tensor", "expert"),
            P("tensor", "expert"),
            P("tensor", "expert"),
            P("expert"),
            P("expert", None),
            P("expert"),
            P("expert", "tensor"),
            P("expert", "tensor"),
            P("tensor", "expert"),
            P("expert", None, "tensor"),
            P("expert", None, "tensor"),
            P("expert", "tensor", None),
        ),
        check_vma=False,
    )
```
